128 devices in a mesh: grp: 8 (over y, core), shard: 16 (over x, z).
Axes of the slice: x: 4, y: 4, z: 4, core: 2. Of those that a mesh axis runs over, the one named last changes fastest.
Arguments:
- embed: float32 [131072, 512], P(('grp', 'shard')), may hold values from -6 to 6
- knn_slot: int32 [131072, 80], P(('grp', 'shard')), may hold values from 0 to 4095
- knn_weight: float32 [131072, 80], P(('grp', 'shard')), may hold values from 0.1 to 1
- tile_list: int32 [128, 16, 2], P(('grp', 'shard')), may hold values from 0 to 7, as said below
- send_rows: int32 [128, 128, 8], P(('grp', 'shard')), may hold values from 0 to 1023
- members: int32 [512, 256], P(('grp', 'shard')), may hold values from 0 to 1023
- sub_len: int32 [512], P(('grp', 'shard')), may hold values from 1 to 256, 81920 in all
- w_self: bfloat16 [512, 512], replicated, may hold values from -0.25 to 0.25
- w_nbr: bfloat16 [512, 512], replicated, may hold values from -2 to 2
- bias_v: float32 [512], replicated, may hold values from -6 to 6
- w_conf: bfloat16 [512], replicated, may hold values from -0.25 to 0.25
- w_diff: bfloat16 [512, 512], replicated, may hold values from -0.25 to 0.25
- w_ctx: bfloat16 [512, 512], replicated, may hold values from -0.25 to 0.25
- bias_e: float32 [512], replicated, may hold values from -6 to 6
- w_edge: bfloat16 [512], replicated, may hold values from -0.25 to 0.25
Outputs:
- node_hidden: bfloat16 [131072, 512], P(('grp', 'shard'))
- confidence: float32 [131072], P(('grp', 'shard'))
- edge_scores: float32 [512, 256], P(('grp', 'shard'))
- node_votes: float32 [131072], P(('grp', 'shard'))
The draws below stay inside these ranges and needn't reach their ends.
Inputs may be any that keep to these rules, and one draw needn't show every extreme that they name: `tile_list`: for each providing device and each device of its group, the 2 tile numbers are distinct local tiles of the provider.
All inputs are finite; a program needn't handle non-finite values. No bound on the sum of `sub_len` on one device may be relied on, other than what follows from the above.
Results may differ from the reference program's by a relative error of at most 0.024.
Values may be sent and summed in bfloat16 or wider, within the bound.
A program may use at most 128 MiB of HBM per device.

```python
import math
import jax
import jax.numpy as jnp
import numpy as np
from jax import lax

D = 512
H = 512
KNN = 80
SUBN = 256
TILE = 128
TL = 2
NODE_DEV = 1024
SUBS_DEV = 4
NODES = 131072
SUBS = 512
CAP = 8
N_SHARD = 16
DEVICES = 128


def draw_tile_list(key, part):
    tile_count = NODE_DEV // TILE
    random_keys = jax.random.randint(key, (DEVICES, N_SHARD, tile_count), 0, 65536)
    scores = random_keys * tile_count + jnp.arange(tile_count, dtype=jnp.int32)
    return lax.top_k(scores, TL)[1].astype(jnp.int32)


def with_ends(drawn, rng, low, top_value):
    place = [jax.random.randint(jax.random.fold_in(rng, axis), (), 0, length) for axis, length in enumerate(drawn.shape)]
    longest = drawn.shape.index(max(drawn.shape))
    beside = place[:longest] + [(place[longest] + 1) % drawn.shape[longest]] + place[longest + 1:]
    return drawn.at[tuple(place)].set(low).at[tuple(beside)].set(top_value)


def level_of(stream_key, shape, pieces, least, top_value):
    loudness = 1.0
    for axis_at, shards_of in pieces:
        heights = jax.random.uniform(jax.random.fold_in(jax.random.fold_in(stream_key, 6), axis_at), (shards_of,), jnp.float32, least / len(pieces), top_value / len(pieces))
        loudness = loudness * jnp.repeat(jnp.exp(heights), shape[axis_at] // shards_of).reshape((-1,) + (1,) * (len(shape) - 1 - axis_at))
    return loudness


def length_profile(count, total, reach, slope):
    loads = [(1 << 20) // math.isqrt(rank ** slope) + 1 for rank in range(2, count + 1)]
    surplus, given = total - reach - (count - 1), [1] * (count - 1)
    while surplus > 0:
        free = [i for i in range(count - 1) if given[i] < reach]
        whole, left = sum([loads[i] for i in free]), surplus
        for i in free:
            extra = min(reach - given[i], max(1, left * loads[i] // whole), surplus)
            given[i] = given[i] + extra
            surplus = surplus - extra
    return np.array([reach] + given)


def ragged_sizes(stream_key, amount, total, reach, slope):
    if amount == 2:
        one = jax.random.randint(stream_key, (), max(1, total - reach), min(reach, total - 1) + 1)
        return jnp.stack([one, total - one])
    tallies = jnp.asarray(length_profile(amount, total, reach, slope), jnp.int32)
    pairs = (amount - 1) // 2
    giver, receiver = tallies[1:1 + 2 * pairs:2], tallies[2:2 + 2 * pairs:2]
    room = jnp.minimum(giver - 1, reach - receiver)
    passed = jax.random.randint(jax.random.fold_in(stream_key, 1), (pairs,), 0, 1 << 20) % (room + 1)
    tallies = tallies.at[1:1 + 2 * pairs:2].set(giver - passed).at[2:2 + 2 * pairs:2].set(receiver + passed)
    return tallies[jax.random.permutation(jax.random.fold_in(stream_key, 2), amount)]


def bell_draw(own_key, dims, spread, reach, split=(), held_as=jnp.bfloat16):
    level = level_of(own_key, dims, split, -0.22, 0.18) if split else 1.0
    result = jax.random.normal(own_key, dims, jnp.float32) * spread * level
    return jnp.minimum(jnp.maximum(result, -reach), reach).astype(held_as)


def setup_inputs(seed: int = 0) -> dict:
    key_list = jax.random.split(jax.random.key(seed), 16)
    embed = bell_draw(key_list[0], (NODES, D), 1.0, 6.0, ((0, 128),), jnp.float32)
    knn_slot = with_ends(jax.random.randint(key_list[1], (NODES, KNN), 0, N_SHARD * TL * TILE), jax.random.fold_in(key_list[1], 1), 0, (N_SHARD * TL * TILE) - 1).astype(jnp.int32)
    knn_weight = jnp.clip(jnp.exp(math.log(1.0) - 2.3025851 * jax.random.uniform(key_list[2], (NODES, KNN), jnp.float32) ** level_of(key_list[2], (NODES, KNN), ((0, 128),), -0.2, 0.2)), 0.1, 1.0)
    tile_list = draw_tile_list(jax.random.fold_in(key_list[15], 71), 0)
    send_rows = with_ends(jax.random.randint(key_list[4], (DEVICES, DEVICES, CAP), 0, NODE_DEV), jax.random.fold_in(key_list[4], 1), 0, NODE_DEV - 1).astype(jnp.int32)
    members = with_ends(jax.random.randint(key_list[5], (SUBS, SUBN), 0, DEVICES * CAP), jax.random.fold_in(key_list[5], 1), 0, (DEVICES * CAP) - 1).astype(jnp.int32)
    sub_len = ragged_sizes(key_list[6], SUBS, SUBS * SUBN * 5 // 8, SUBN, 2).astype(jnp.int32)
    w_self = bell_draw(key_list[7], (D, H), D ** -0.5, 0.25)
    w_nbr = bell_draw(key_list[8], (D, H), (max(D // 64, 1)) ** -0.5, 2.0)
    bias_v = bell_draw(key_list[9], (H,), 1.0, 6.0, (), jnp.float32)
    w_conf = bell_draw(key_list[10], (H,), H ** -0.5, 0.25)
    w_diff = bell_draw(key_list[11], (H, H), H ** -0.5, 0.25)
    w_ctx = bell_draw(key_list[12], (H, H), H ** -0.5, 0.25)
    bias_e = bell_draw(key_list[13], (H,), 1.0, 6.0, (), jnp.float32)
    w_edge = bell_draw(key_list[14], (H,), H ** -0.5, 0.25)
    return dict(embed=embed, knn_slot=knn_slot, knn_weight=knn_weight, tile_list=tile_list, send_rows=send_rows, members=members, sub_len=sub_len, w_self=w_self, w_nbr=w_nbr, bias_v=bias_v, w_conf=w_conf, w_diff=w_diff, w_ctx=w_ctx, bias_e=bias_e, w_edge=w_edge)


def reference(embed, knn_slot, knn_weight, tile_list, send_rows, members, sub_len, w_self, w_nbr, bias_v, w_conf, w_diff, w_ctx, bias_e, w_edge):
    embed_bf = embed.astype(jnp.bfloat16)
    weight_sum = jnp.sum(knn_weight, axis=1, keepdims=True)
    coeffs = (knn_weight / weight_sum).astype(jnp.bfloat16)
    node_ids = jnp.arange(NODES, dtype=jnp.int32)
    device_ids = node_ids // NODE_DEV
    group_ids = device_ids // N_SHARD
    shard_ids = device_ids % N_SHARD
    peer_span = TL * TILE
    peer_index = knn_slot // peer_span
    tile_slot = (knn_slot // TILE) % TL
    row_in_tile = knn_slot % TILE
    source = (group_ids[:, None] * N_SHARD + peer_index).astype(jnp.int32)
    tiles = tile_list[source, shard_ids[:, None], tile_slot]
    neighbours = (source * NODE_DEV + tiles * TILE + row_in_tile).astype(jnp.int32)

    def aggregate(blocks):
        index_block, coeff_block = blocks
        picked = embed_bf[index_block].astype(jnp.float32)
        return jnp.einsum("nk,nkd->nd", coeff_block.astype(jnp.float32), picked, precision=lax.Precision.HIGHEST)

    summed = lax.map(aggregate, (neighbours.reshape(DEVICES, NODE_DEV, KNN), coeffs.reshape(DEVICES, NODE_DEV, KNN)))
    gathered_sum = summed.reshape(NODES, D).astype(jnp.bfloat16)
    pre_act = jnp.dot(embed_bf, w_self, preferred_element_type=jnp.float32) + jnp.dot(gathered_sum, w_nbr, preferred_element_type=jnp.float32) + bias_v
    node_hidden = jax.nn.relu(pre_act).astype(jnp.bfloat16)
    confidence = jnp.dot(node_hidden, w_conf, preferred_element_type=jnp.float32)

    owners = (jnp.arange(SUBS, dtype=jnp.int32) // SUBS_DEV).astype(jnp.int32)
    senders = members // CAP
    slot_ids = members % CAP
    member_nodes = (senders * NODE_DEV + send_rows[senders, owners[:, None], slot_ids]).astype(jnp.int32)
    member_rows = node_hidden[member_nodes].astype(jnp.float32)
    relative = member_rows - member_rows[:, :1, :]
    alive = jnp.arange(SUBN, dtype=jnp.int32)[None, :] < sub_len[:, None]
    masked = jnp.where(alive[:, :, None], relative, jnp.float32(0.0))
    context = (jnp.sum(masked, axis=1) / sub_len[:, None].astype(jnp.float32)).astype(jnp.bfloat16)
    relative_bf = relative.astype(jnp.bfloat16)
    inner = jnp.einsum("smh,hk->smk", relative_bf.astype(jnp.float32), w_diff.astype(jnp.float32), precision=lax.Precision.HIGHEST)
    inner = inner + jnp.dot(context, w_ctx, preferred_element_type=jnp.float32)[:, None, :] + bias_e
    edge_hidden = jax.nn.relu(inner).astype(jnp.bfloat16)
    logits = jnp.einsum("smk,k->sm", edge_hidden.astype(jnp.float32), w_edge.astype(jnp.float32), precision=lax.Precision.HIGHEST)
    edge_scores = jnp.where(alive, jax.nn.sigmoid(logits), jnp.float32(0.0))
    node_votes = jnp.zeros((NODES,), jnp.float32).at[member_nodes.reshape(-1)].add(edge_scores.reshape(-1))
    return (node_hidden, confidence, edge_scores, node_votes)
```

```python
import math

import jax
import jax.numpy as jnp
from jax import lax
from jax.sharding import PartitionSpec as P

TILE = 128


def select_matrix(indices, count, dtype):
    return (indices[:, None] == jnp.arange(count, dtype=jnp.int32)[None, :]).astype(dtype)


def body(
    embed,
    knn_slot,
    knn_weight,
    tile_list,
    send_rows,
    members,
    sub_len,
    w_self,
    w_nbr,
    bias_v,
    w_conf,
    w_diff,
    w_ctx,
    bias_e,
    w_edge,
):
    nodes = embed.shape[0]
    width = embed.shape[1]
    neighbour_count = knn_slot.shape[1]
    shard_count = lax.axis_size("shard")
    list_len = tile_list.shape[2]
    peer_span = list_len * TILE
    column_total = shard_count * peer_span
    embed_bf = embed.astype(jnp.bfloat16)
    weight_sum = jnp.sum(knn_weight, axis=1, keepdims=True)
    coeff_bf = (knn_weight / weight_sum).astype(jnp.bfloat16)
    block_rows = math.gcd(nodes, 256)
    block_count = nodes // block_rows
    peer_part = (knn_slot // peer_span).reshape(block_count, block_rows, neighbour_count)
    row_part = (knn_slot % peer_span).reshape(block_count, block_rows, neighbour_count)
    coeff_blocks = coeff_bf.reshape(block_count, block_rows, neighbour_count)

    def build_block(pieces):
        peer_block, row_block, coeff_block = pieces
        peer_hot = jnp.where(
            peer_block[:, :, None] == jnp.arange(shard_count, dtype=jnp.int32),
            coeff_block[:, :, None],
            jnp.zeros((), jnp.bfloat16),
        )
        row_hot = (row_block[:, :, None] == jnp.arange(peer_span, dtype=jnp.int32)).astype(
            jnp.bfloat16
        )
        joined = jnp.einsum("nkp,nkr->npr", peer_hot, row_hot, preferred_element_type=jnp.float32)
        return joined.reshape(block_rows, column_total)

    adjacency = (
        lax.map(build_block, (peer_part, row_part, coeff_blocks))
        .reshape(nodes, column_total)
        .astype(jnp.bfloat16)
    )
    tile_count = nodes // TILE
    embed_tiles = embed_bf.reshape(tile_count, TILE, width)
    outgoing = jnp.take(embed_tiles, tile_list[0].reshape(shard_count * list_len), axis=0)
    outgoing = outgoing.reshape(shard_count, peer_span, width)
    provided = lax.all_to_all(outgoing, "shard", split_axis=0, concat_axis=0, tiled=True)
    provided = provided.reshape(column_total, width)
    gathered_sum = jnp.dot(adjacency, provided, preferred_element_type=jnp.float32)
    pre_act = (
        jnp.dot(embed_bf, w_self, preferred_element_type=jnp.float32)
        + jnp.dot(gathered_sum.astype(jnp.bfloat16), w_nbr, preferred_element_type=jnp.float32)
        + bias_v
    )
    node_hidden = jax.nn.relu(pre_act).astype(jnp.bfloat16)
    confidence = jnp.dot(node_hidden, w_conf, preferred_element_type=jnp.float32)
    device_total = send_rows.shape[1]
    capacity = send_rows.shape[2]
    hidden_width = node_hidden.shape[1]
    slot_total = device_total * capacity
    send_flat = send_rows[0].reshape(slot_total)
    send_chooser = select_matrix(send_flat, nodes, jnp.bfloat16)
    outbound = jnp.dot(send_chooser, node_hidden, preferred_element_type=jnp.float32).astype(
        jnp.bfloat16
    )
    outbound = outbound.reshape(device_total, capacity, hidden_width)
    received = lax.all_to_all(outbound, ("grp", "shard"), split_axis=0, concat_axis=0, tiled=True)
    received_rows = received.reshape(slot_total, hidden_width)
    sub_count = members.shape[0]
    member_width = members.shape[1]
    member_flat = members.reshape(sub_count * member_width)
    member_chooser = select_matrix(member_flat, slot_total, jnp.bfloat16)
    member_rows = jnp.dot(member_chooser, received_rows, preferred_element_type=jnp.float32)
    member_rows = member_rows.reshape(sub_count, member_width, hidden_width)
    relative = member_rows - member_rows[:, :1, :]
    alive = jnp.arange(member_width, dtype=jnp.int32)[None, :] < sub_len[:, None]
    masked = jnp.where(alive[:, :, None], relative, 0.0)
    context = (jnp.sum(masked, axis=1) / sub_len[:, None].astype(jnp.float32)).astype(jnp.bfloat16)
    relative_bf = relative.astype(jnp.bfloat16)
    inner = jnp.einsum("smh,hk->smk", relative_bf, w_diff, preferred_element_type=jnp.float32)
    inner = inner + jnp.dot(context, w_ctx, preferred_element_type=jnp.float32)[:, None, :] + bias_e
    edge_hidden = jax.nn.relu(inner).astype(jnp.bfloat16)
    logits = jnp.einsum("smk,k->sm", edge_hidden, w_edge, preferred_element_type=jnp.float32)
    edge_scores = jnp.where(alive, jax.nn.sigmoid(logits), 0.0)
    slot_scores = jnp.dot(
        member_chooser.astype(jnp.float32).T,
        edge_scores.reshape(sub_count * member_width),
        precision=lax.Precision.HIGHEST,
    )
    slot_scores = slot_scores.reshape(device_total, capacity)
    returned = lax.all_to_all(
        slot_scores, ("grp", "shard"), split_axis=0, concat_axis=0, tiled=True
    )
    node_votes = jnp.dot(
        send_chooser.astype(jnp.float32).T,
        returned.reshape(slot_total),
        precision=lax.Precision.HIGHEST,
    )
    return (node_hidden, confidence, edge_scores, node_votes)


def solution(mesh):
    return jax.shard_map(
        body,
        mesh=mesh,
        in_specs=(
            P(("grp", "shard"), None),
            P(("grp", "shard"), None),
            P(("grp", "shard"), None),
            P(("grp", "shard"), None, None),
            P(("grp", "shard"), None, None),
            P(("grp", "shard"), None),
            P(("grp", "shard")),
            P(),
            P(),
            P(),
            P(),
            P(),
            P(),
            P(),
            P(),
        ),
        out_specs=(
            P(("grp", "shard"), None),
            P(("grp", "shard")),
            P(("grp", "shard"), None),
            P(("grp", "shard")),
        ),
        check_vma=False,
    )
```

```python
import math

import jax
import jax.numpy as jnp
from jax import lax
from jax.sharding import PartitionSpec as P

TILE = 128


def select_matrix(indices, count, dtype):
    return (indices[:, None] == jnp.arange(count, dtype=jnp.int32)[None, :]).astype(dtype)


def scatter_sum(indices, values, count):
    hit = indices[:, None] == jnp.arange(count, dtype=jnp.int32)[None, :]
    return jnp.sum(jnp.where(hit, values[:, None], jnp.float32(0.0)), axis=0)


def body(
    embed,
    knn_slot,
    knn_weight,
    tile_list,
    send_rows,
    members,
    sub_len,
    w_self,
    w_nbr,
    bias_v,
    w_conf,
    w_diff,
    w_ctx,
    bias_e,
    w_edge,
):
    nodes = embed.shape[0]
    width = embed.shape[1]
    neighbour_count = knn_slot.shape[1]
    shard_count = lax.axis_size("shard")
    list_len = tile_list.shape[2]
    peer_span = list_len * TILE
    column_total = shard_count * peer_span
    embed_bf = embed.astype(jnp.bfloat16)
    weight_sum = jnp.sum(knn_weight, axis=1, keepdims=True)
    coeff_bf = (knn_weight / weight_sum).astype(jnp.bfloat16)
    block_rows = math.gcd(nodes, 256)
    block_count = nodes // block_rows
    peer_part = (knn_slot // peer_span).reshape(block_count, block_rows, neighbour_count)
    row_part = (knn_slot % peer_span).reshape(block_count, block_rows, neighbour_count)
    coeff_blocks = coeff_bf.reshape(block_count, block_rows, neighbour_count)

    def build_block(pieces):
        peer_block, row_block, coeff_block = pieces
        peer_hot = jnp.where(
            peer_block[:, :, None] == jnp.arange(shard_count, dtype=jnp.int32),
            coeff_block[:, :, None],
            jnp.zeros((), jnp.bfloat16),
        )
        row_hot = (row_block[:, :, None] == jnp.arange(peer_span, dtype=jnp.int32)).astype(
            jnp.bfloat16
        )
        joined = jnp.einsum("nkp,nkr->npr", peer_hot, row_hot, preferred_element_type=jnp.float32)
        return joined.reshape(block_rows, column_total)

    adjacency = (
        lax.map(build_block, (peer_part, row_part, coeff_blocks))
        .reshape(nodes, column_total)
        .astype(jnp.bfloat16)
    )
    tile_count = nodes // TILE
    embed_tiles = embed_bf.reshape(tile_count, TILE, width)
    outgoing = jnp.take(embed_tiles, tile_list[0].reshape(shard_count * list_len), axis=0)
    outgoing = outgoing.reshape(shard_count, peer_span, width)
    provided = lax.all_to_all(outgoing, "shard", split_axis=0, concat_axis=0, tiled=True)
    provided = provided.reshape(column_total, width)
    gathered_sum = jnp.dot(adjacency, provided, preferred_element_type=jnp.float32)
    pre_act = (
        jnp.dot(embed_bf, w_self, preferred_element_type=jnp.float32)
        + jnp.dot(gathered_sum.astype(jnp.bfloat16), w_nbr, preferred_element_type=jnp.float32)
        + bias_v
    )
    node_hidden = jax.nn.relu(pre_act).astype(jnp.bfloat16)
    confidence = jnp.dot(node_hidden, w_conf, preferred_element_type=jnp.float32)
    device_total = send_rows.shape[1]
    capacity = send_rows.shape[2]
    hidden_width = node_hidden.shape[1]
    slot_total = device_total * capacity
    send_flat = send_rows[0].reshape(slot_total)
    send_chooser = select_matrix(send_flat, nodes, jnp.bfloat16)
    outbound = jnp.dot(send_chooser, node_hidden, preferred_element_type=jnp.float32).astype(
        jnp.bfloat16
    )
    outbound = outbound.reshape(device_total, capacity, hidden_width)
    received = lax.all_to_all(outbound, ("grp", "shard"), split_axis=0, concat_axis=0, tiled=True)
    received_rows = received.reshape(slot_total, hidden_width)
    sub_count = members.shape[0]
    member_width = members.shape[1]
    member_flat = members.reshape(sub_count * member_width)
    member_chooser = select_matrix(member_flat, slot_total, jnp.bfloat16)
    member_rows = jnp.dot(member_chooser, received_rows, preferred_element_type=jnp.float32)
    member_rows = member_rows.reshape(sub_count, member_width, hidden_width)
    relative = member_rows - member_rows[:, :1, :]
    alive = jnp.arange(member_width, dtype=jnp.int32)[None, :] < sub_len[:, None]
    masked = jnp.where(alive[:, :, None], relative, 0.0)
    context = (jnp.sum(masked, axis=1) / sub_len[:, None].astype(jnp.float32)).astype(jnp.bfloat16)
    relative_bf = relative.astype(jnp.bfloat16)
    inner = jnp.einsum("smh,hk->smk", relative_bf, w_diff, preferred_element_type=jnp.float32)
    inner = inner + jnp.dot(context, w_ctx, preferred_element_type=jnp.float32)[:, None, :] + bias_e
    edge_hidden = jax.nn.relu(inner).astype(jnp.bfloat16)
    logits = jnp.einsum("smk,k->sm", edge_hidden, w_edge, preferred_element_type=jnp.float32)
    edge_scores = jnp.where(alive, jax.nn.sigmoid(logits), 0.0)
    slot_scores = scatter_sum(member_flat, edge_scores.reshape(sub_count * member_width), slot_total)
    slot_scores = slot_scores.reshape(device_total, capacity)
    returned = lax.all_to_all(
        slot_scores, ("grp", "shard"), split_axis=0, concat_axis=0, tiled=True
    )
    node_votes = scatter_sum(send_flat, returned.reshape(slot_total), nodes)
    return (node_hidden, confidence, edge_scores, node_votes)


def solution(mesh):
    return jax.shard_map(
        body,
        mesh=mesh,
        in_specs=(
            P(("grp", "shard"), None),
            P(("grp", "shard"), None),
            P(("grp", "shard"), None),
            P(("grp", "shard"), None, None),
            P(("grp", "shard"), None, None),
            P(("grp", "shard"), None),
            P(("grp", "shard")),
            P(),
            P(),
            P(),
            P(),
            P(),
            P(),
            P(),
            P(),
        ),
        out_specs=(
            P(("grp", "shard"), None),
            P(("grp", "shard")),
            P(("grp", "shard"), None),
            P(("grp", "shard")),
        ),
        check_vma=False,
    )
```

```python
import math

import jax
import jax.numpy as jnp
from jax import lax
from jax.experimental import pallas as pl
from jax.experimental.pallas import tpu as pltpu
from jax.sharding import PartitionSpec as P

TILE = 128


SUB = 8


def node_kernel(slot_ref, coef_ref, table_ref, embed_ref, w_self_ref, w_nbr_ref, bias_ref, out_ref, adj_ref):
    rows_in_block = out_ref.shape[0]
    peers = adj_ref.shape[0]
    span = adj_ref.shape[2]
    sub_count = rows_in_block // SUB
    width = slot_ref.shape[1]
    row_hit = lax.broadcasted_iota(jnp.int32, (span, width), 0)
    lane_node = lax.broadcasted_iota(jnp.int32, (peers * SUB, width), 1) // (width // SUB)
    pair_row = lax.broadcasted_iota(jnp.int32, (peers * SUB, width), 0)
    pair_peer = pair_row // SUB
    pair_node = pair_row % SUB

    def one_sub(s, carry):
        slots = slot_ref[pl.ds(s, 1), :]
        coefs = coef_ref[pl.ds(s, 1), :]
        peer = slots // span
        row = slots % span
        onehot = jnp.where(row_hit == row, 1.0, 0.0).astype(jnp.bfloat16)
        picked = (pair_peer == peer) & (pair_node == lane_node)
        weights = jnp.where(picked, coefs, 0.0).astype(jnp.bfloat16)
        block = lax.dot_general(
            weights, onehot, (((1,), (1,)), ((), ())), preferred_element_type=jnp.float32
        )
        start = pl.multiple_of(s * SUB, SUB)
        adj_ref[:, pl.ds(start, SUB), :] = block.astype(jnp.bfloat16).astype(jnp.float32).reshape(peers, SUB, span)
        return carry

    lax.fori_loop(0, sub_count, one_sub, 0)
    total = jnp.zeros((rows_in_block, table_ref.shape[1]), jnp.float32)
    for p in range(peers):
        total = total + jnp.dot(
            adj_ref[p].astype(jnp.bfloat16),
            table_ref[pl.ds(p * span, span), :],
            preferred_element_type=jnp.float32,
        )
    pre = (
        jnp.dot(embed_ref[...], w_self_ref[...], preferred_element_type=jnp.float32)
        + jnp.dot(total.astype(jnp.bfloat16), w_nbr_ref[...], preferred_element_type=jnp.float32)
        + bias_ref[...]
    )
    out_ref[...] = jnp.maximum(pre, 0.0).astype(out_ref.dtype)


def node_layer(slot_rows, coef_rows, table, embed_bf, w_self, w_nbr, bias, peers, span):
    nodes, width = embed_bf.shape
    hidden = w_self.shape[1]
    block_rows = 128
    subs_per_block = block_rows // SUB
    row_width = slot_rows.shape[1]
    return pl.pallas_call(
        node_kernel,
        grid=(nodes // block_rows,),
        in_specs=[
            pl.BlockSpec((subs_per_block, row_width), lambda b: (b, 0)),
            pl.BlockSpec((subs_per_block, row_width), lambda b: (b, 0)),
            pl.BlockSpec(table.shape, lambda b: (0, 0)),
            pl.BlockSpec((block_rows, width), lambda b: (b, 0)),
            pl.BlockSpec(w_self.shape, lambda b: (0, 0)),
            pl.BlockSpec(w_nbr.shape, lambda b: (0, 0)),
            pl.BlockSpec((1, hidden), lambda b: (0, 0)),
        ],
        out_specs=pl.BlockSpec((block_rows, hidden), lambda b: (b, 0)),
        out_shape=jax.ShapeDtypeStruct((nodes, hidden), jnp.bfloat16),
        scratch_shapes=[pltpu.VMEM((peers, block_rows, span), jnp.float32)],
    )(slot_rows, coef_rows, table, embed_bf, w_self, w_nbr, bias.reshape(1, hidden))


def select_matrix(indices, count, dtype):
    return (indices[:, None] == jnp.arange(count, dtype=jnp.int32)[None, :]).astype(dtype)


def scatter_sum(indices, values, count):
    hit = indices[:, None] == jnp.arange(count, dtype=jnp.int32)[None, :]
    return jnp.sum(jnp.where(hit, values[:, None], jnp.float32(0.0)), axis=0)


def body(
    embed,
    knn_slot,
    knn_weight,
    tile_list,
    send_rows,
    members,
    sub_len,
    w_self,
    w_nbr,
    bias_v,
    w_conf,
    w_diff,
    w_ctx,
    bias_e,
    w_edge,
):
    nodes = embed.shape[0]
    width = embed.shape[1]
    neighbour_count = knn_slot.shape[1]
    shard_count = lax.axis_size("shard")
    list_len = tile_list.shape[2]
    peer_span = list_len * TILE
    column_total = shard_count * peer_span
    embed_bf = embed.astype(jnp.bfloat16)
    weight_sum = jnp.sum(knn_weight, axis=1, keepdims=True)
    coeff_bf = (knn_weight / weight_sum).astype(jnp.bfloat16)
    tile_count = nodes // TILE
    embed_tiles = embed_bf.reshape(tile_count, TILE, width)
    outgoing = jnp.take(embed_tiles, tile_list[0].reshape(shard_count * list_len), axis=0)
    outgoing = outgoing.reshape(shard_count, peer_span, width)
    provided = lax.all_to_all(outgoing, "shard", split_axis=0, concat_axis=0, tiled=True)
    provided = provided.reshape(column_total, width)
    sub_rows = nodes // SUB
    slot_rows = knn_slot.reshape(sub_rows, SUB * neighbour_count)
    coef_rows = coeff_bf.astype(jnp.float32).reshape(sub_rows, SUB * neighbour_count)
    node_hidden = node_layer(slot_rows, coef_rows, provided, embed_bf, w_self, w_nbr, bias_v, shard_count, peer_span)
    confidence = jnp.dot(node_hidden, w_conf, preferred_element_type=jnp.float32)
    device_total = send_rows.shape[1]
    capacity = send_rows.shape[2]
    hidden_width = node_hidden.shape[1]
    slot_total = device_total * capacity
    send_flat = send_rows[0].reshape(slot_total)
    send_chooser = select_matrix(send_flat, nodes, jnp.bfloat16)
    outbound = jnp.dot(send_chooser, node_hidden, preferred_element_type=jnp.float32).astype(
        jnp.bfloat16
    )
    outbound = outbound.reshape(device_total, capacity, hidden_width)
    received = lax.all_to_all(outbound, ("grp", "shard"), split_axis=0, concat_axis=0, tiled=True)
    received_rows = received.reshape(slot_total, hidden_width)
    sub_count = members.shape[0]
    member_width = members.shape[1]
    member_flat = members.reshape(sub_count * member_width)
    member_chooser = select_matrix(member_flat, slot_total, jnp.bfloat16)
    member_rows = jnp.dot(member_chooser, received_rows, preferred_element_type=jnp.float32)
    member_rows = member_rows.reshape(sub_count, member_width, hidden_width)
    relative = member_rows - member_rows[:, :1, :]
    alive = jnp.arange(member_width, dtype=jnp.int32)[None, :] < sub_len[:, None]
    masked = jnp.where(alive[:, :, None], relative, 0.0)
    context = (jnp.sum(masked, axis=1) / sub_len[:, None].astype(jnp.float32)).astype(jnp.bfloat16)
    relative_bf = relative.astype(jnp.bfloat16)
    inner = jnp.einsum("smh,hk->smk", relative_bf, w_diff, preferred_element_type=jnp.float32)
    inner = inner + jnp.dot(context, w_ctx, preferred_element_type=jnp.float32)[:, None, :] + bias_e
    edge_hidden = jax.nn.relu(inner).astype(jnp.bfloat16)
    logits = jnp.einsum("smk,k->sm", edge_hidden, w_edge, preferred_element_type=jnp.float32)
    edge_scores = jnp.where(alive, jax.nn.sigmoid(logits), 0.0)
    slot_scores = scatter_sum(member_flat, edge_scores.reshape(sub_count * member_width), slot_total)
    slot_scores = slot_scores.reshape(device_total, capacity)
    returned = lax.all_to_all(
        slot_scores, ("grp", "shard"), split_axis=0, concat_axis=0, tiled=True
    )
    node_votes = scatter_sum(send_flat, returned.reshape(slot_total), nodes)
    return (node_hidden, confidence, edge_scores, node_votes)


def solution(mesh):
    return jax.shard_map(
        body,
        mesh=mesh,
        in_specs=(
            P(("grp", "shard"), None),
            P(("grp", "shard"), None),
            P(("grp", "shard"), None),
            P(("grp", "shard"), None, None),
            P(("grp", "shard"), None, None),
            P(("grp", "shard"), None),
            P(("grp", "shard")),
            P(),
            P(),
            P(),
            P(),
            P(),
            P(),
            P(),
            P(),
        ),
        out_specs=(
            P(("grp", "shard"), None),
            P(("grp", "shard")),
            P(("grp", "shard"), None),
            P(("grp", "shard")),
        ),
        check_vma=False,
    )
```

```python
import math

import jax
import jax.numpy as jnp
from jax import lax
from jax.experimental import pallas as pl
from jax.experimental.pallas import tpu as pltpu
from jax.sharding import PartitionSpec as P

TILE = 128


SUB = 8


def build_adjacency(slot_ref, coef_ref, adj_ref):
    peers = adj_ref.shape[0]
    span = adj_ref.shape[2]
    sub_count = adj_ref.shape[1] // SUB
    width = slot_ref.shape[1]
    row_hit = lax.broadcasted_iota(jnp.int32, (span, width), 0)
    lane_node = lax.broadcasted_iota(jnp.int32, (peers * SUB, width), 1) // (width // SUB)
    pair_row = lax.broadcasted_iota(jnp.int32, (peers * SUB, width), 0)
    pair_peer = pair_row // SUB
    pair_node = pair_row % SUB

    def one_sub(s, carry):
        slots = slot_ref[pl.ds(s, 1), :]
        coefs = coef_ref[pl.ds(s, 1), :]
        peer = slots // span
        row = slots % span
        onehot = jnp.where(row_hit == row, 1.0, 0.0).astype(jnp.bfloat16)
        picked = (pair_peer == peer) & (pair_node == lane_node)
        weights = jnp.where(picked, coefs, 0.0).astype(jnp.bfloat16)
        block = lax.dot_general(
            weights, onehot, (((1,), (1,)), ((), ())), preferred_element_type=jnp.float32
        )
        start = pl.multiple_of(s * SUB, SUB)
        adj_ref[:, pl.ds(start, SUB), :] = block.astype(jnp.bfloat16).astype(jnp.float32).reshape(peers, SUB, span)
        return carry

    lax.fori_loop(0, sub_count, one_sub, 0)


def node_kernel(
    outgoing_ref, slot_ref, coef_ref, embed_ref, w_self_ref, w_nbr_ref, bias_ref,
    out_ref, table_ref, adj_ref, send_sems, recv_sems, self_sem,
):
    peers = adj_ref.shape[0]
    span = adj_ref.shape[2]
    block_rows = 128
    group = lax.axis_index("grp")
    me = lax.axis_index("shard")
    barrier = pltpu.get_barrier_semaphore()
    for d in range(1, peers):
        pl.semaphore_signal(barrier, 1, device_id=(group, lax.rem(me + d, peers)), device_id_type=pl.DeviceIdType.MESH)
    pl.semaphore_wait(barrier, peers - 1)

    def link(target, slot):
        return pltpu.make_async_remote_copy(
            src_ref=outgoing_ref.at[target],
            dst_ref=table_ref.at[slot],
            send_sem=send_sems.at[target],
            recv_sem=recv_sems.at[slot],
            device_id=(group, target),
            device_id_type=pl.DeviceIdType.MESH,
        )

    own = pltpu.make_async_copy(outgoing_ref.at[me], table_ref.at[me], self_sem)
    own.start()
    sends = []
    for d in range(1, peers):
        copy = link(lax.rem(me + d, peers), me)
        copy.start()
        sends.append(copy)
    build_adjacency(slot_ref, coef_ref, adj_ref)
    own.wait()
    for d in range(1, peers):
        source = lax.rem(me + peers - d, peers)
        link(source, source).wait_recv()
    for copy in sends:
        copy.wait_send()

    def one_block(b, carry):
        rows = pl.ds(pl.multiple_of(b * block_rows, block_rows), block_rows)
        total = jnp.zeros((block_rows, table_ref.shape[2]), jnp.float32)
        for p in range(peers):
            total = total + jnp.dot(
                adj_ref[p, rows, :].astype(jnp.bfloat16),
                table_ref[p],
                preferred_element_type=jnp.float32,
            )
        pre = (
            jnp.dot(embed_ref[rows, :], w_self_ref[...], preferred_element_type=jnp.float32)
            + jnp.dot(total.astype(jnp.bfloat16), w_nbr_ref[...], preferred_element_type=jnp.float32)
            + bias_ref[...]
        )
        out_ref[rows, :] = jnp.maximum(pre, 0.0).astype(out_ref.dtype)
        return carry

    lax.fori_loop(0, out_ref.shape[0] // block_rows, one_block, 0)


def node_layer(outgoing, slot_rows, coef_rows, embed_bf, w_self, w_nbr, bias):
    nodes, width = embed_bf.shape
    hidden = w_self.shape[1]
    peers, span, _ = outgoing.shape
    vmem = pl.BlockSpec(memory_space=pltpu.VMEM)
    return pl.pallas_call(
        node_kernel,
        in_specs=[pl.BlockSpec(memory_space=pl.ANY)] + [vmem] * 6,
        out_specs=vmem,
        out_shape=jax.ShapeDtypeStruct((nodes, hidden), jnp.bfloat16),
        scratch_shapes=[
            pltpu.VMEM((peers, span, width), jnp.bfloat16),
            pltpu.VMEM((peers, nodes, span), jnp.float32),
            pltpu.SemaphoreType.DMA((peers,)),
            pltpu.SemaphoreType.DMA((peers,)),
            pltpu.SemaphoreType.DMA,
        ],
        compiler_params=pltpu.CompilerParams(
            collective_id=0, has_side_effects=True, vmem_limit_bytes=60 * 1024 * 1024
        ),
    )(outgoing, slot_rows, coef_rows, embed_bf, w_self, w_nbr, bias.reshape(1, hidden))


def select_matrix(indices, count, dtype):
    return (indices[:, None] == jnp.arange(count, dtype=jnp.int32)[None, :]).astype(dtype)


def scatter_sum(indices, values, count):
    hit = indices[:, None] == jnp.arange(count, dtype=jnp.int32)[None, :]
    return jnp.sum(jnp.where(hit, values[:, None], jnp.float32(0.0)), axis=0)


def body(
    embed,
    knn_slot,
    knn_weight,
    tile_list,
    send_rows,
    members,
    sub_len,
    w_self,
    w_nbr,
    bias_v,
    w_conf,
    w_diff,
    w_ctx,
    bias_e,
    w_edge,
):
    nodes = embed.shape[0]
    width = embed.shape[1]
    neighbour_count = knn_slot.shape[1]
    shard_count = lax.axis_size("shard")
    list_len = tile_list.shape[2]
    peer_span = list_len * TILE
    column_total = shard_count * peer_span
    embed_bf = embed.astype(jnp.bfloat16)
    weight_sum = jnp.sum(knn_weight, axis=1, keepdims=True)
    coeff_bf = (knn_weight / weight_sum).astype(jnp.bfloat16)
    tile_count = nodes // TILE
    embed_tiles = embed_bf.reshape(tile_count, TILE, width)
    outgoing = jnp.take(embed_tiles, tile_list[0].reshape(shard_count * list_len), axis=0)
    outgoing = outgoing.reshape(shard_count, peer_span, width)
    sub_rows = nodes // SUB
    slot_rows = knn_slot.reshape(sub_rows, SUB * neighbour_count)
    coef_rows = coeff_bf.astype(jnp.float32).reshape(sub_rows, SUB * neighbour_count)
    node_hidden = node_layer(outgoing, slot_rows, coef_rows, embed_bf, w_self, w_nbr, bias_v)
    confidence = jnp.dot(node_hidden, w_conf, preferred_element_type=jnp.float32)
    device_total = send_rows.shape[1]
    capacity = send_rows.shape[2]
    hidden_width = node_hidden.shape[1]
    slot_total = device_total * capacity
    send_flat = send_rows[0].reshape(slot_total)
    send_chooser = select_matrix(send_flat, nodes, jnp.bfloat16)
    outbound = jnp.dot(send_chooser, node_hidden, preferred_element_type=jnp.float32).astype(
        jnp.bfloat16
    )
    outbound = outbound.reshape(device_total, capacity, hidden_width)
    received = lax.all_to_all(outbound, ("grp", "shard"), split_axis=0, concat_axis=0, tiled=True)
    received_rows = received.reshape(slot_total, hidden_width)
    sub_count = members.shape[0]
    member_width = members.shape[1]
    member_flat = members.reshape(sub_count * member_width)
    member_chooser = select_matrix(member_flat, slot_total, jnp.bfloat16)
    member_rows = jnp.dot(member_chooser, received_rows, preferred_element_type=jnp.float32)
    member_rows = member_rows.reshape(sub_count, member_width, hidden_width)
    relative = member_rows - member_rows[:, :1, :]
    alive = jnp.arange(member_width, dtype=jnp.int32)[None, :] < sub_len[:, None]
    masked = jnp.where(alive[:, :, None], relative, 0.0)
    context = (jnp.sum(masked, axis=1) / sub_len[:, None].astype(jnp.float32)).astype(jnp.bfloat16)
    relative_bf = relative.astype(jnp.bfloat16)
    inner = jnp.einsum("smh,hk->smk", relative_bf, w_diff, preferred_element_type=jnp.float32)
    inner = inner + jnp.dot(context, w_ctx, preferred_element_type=jnp.float32)[:, None, :] + bias_e
    edge_hidden = jax.nn.relu(inner).astype(jnp.bfloat16)
    logits = jnp.einsum("smk,k->sm", edge_hidden, w_edge, preferred_element_type=jnp.float32)
    edge_scores = jnp.where(alive, jax.nn.sigmoid(logits), 0.0)
    slot_scores = scatter_sum(member_flat, edge_scores.reshape(sub_count * member_width), slot_total)
    slot_scores = slot_scores.reshape(device_total, capacity)
    returned = lax.all_to_all(
        slot_scores, ("grp", "shard"), split_axis=0, concat_axis=0, tiled=True
    )
    node_votes = scatter_sum(send_flat, returned.reshape(slot_total), nodes)
    return (node_hidden, confidence, edge_scores, node_votes)


def solution(mesh):
    return jax.shard_map(
        body,
        mesh=mesh,
        in_specs=(
            P(("grp", "shard"), None),
            P(("grp", "shard"), None),
            P(("grp", "shard"), None),
            P(("grp", "shard"), None, None),
            P(("grp", "shard"), None, None),
            P(("grp", "shard"), None),
            P(("grp", "shard")),
            P(),
            P(),
            P(),
            P(),
            P(),
            P(),
            P(),
            P(),
        ),
        out_specs=(
            P(("grp", "shard"), None),
            P(("grp", "shard")),
            P(("grp", "shard"), None),
            P(("grp", "shard")),
        ),
        check_vma=False,
    )
```

```python
import math

import jax
import jax.numpy as jnp
from jax import lax
from jax.sharding import PartitionSpec as P

TILE = 128


def select_matrix(indices, count, dtype):
    return (indices[:, None] == jnp.arange(count, dtype=jnp.int32)[None, :]).astype(dtype)


def scatter_sum(indices, values, count):
    hit = indices[:, None] == jnp.arange(count, dtype=jnp.int32)[None, :]
    return jnp.sum(jnp.where(hit, values[:, None], jnp.float32(0.0)), axis=0)


def body(
    embed,
    knn_slot,
    knn_weight,
    tile_list,
    send_rows,
    members,
    sub_len,
    w_self,
    w_nbr,
    bias_v,
    w_conf,
    w_diff,
    w_ctx,
    bias_e,
    w_edge,
):
    nodes = embed.shape[0]
    width = embed.shape[1]
    neighbour_count = knn_slot.shape[1]
    shard_count = lax.axis_size("shard")
    list_len = tile_list.shape[2]
    peer_span = list_len * TILE
    column_total = shard_count * peer_span
    embed_bf = embed.astype(jnp.bfloat16)
    weight_sum = jnp.sum(knn_weight, axis=1, keepdims=True)
    coeff_bf = (knn_weight / weight_sum).astype(jnp.bfloat16)
    block_rows = math.gcd(nodes, 256)
    block_count = nodes // block_rows
    peer_part = (knn_slot // peer_span).reshape(block_count, block_rows, neighbour_count)
    row_part = (knn_slot % peer_span).reshape(block_count, block_rows, neighbour_count)
    coeff_blocks = coeff_bf.reshape(block_count, block_rows, neighbour_count)

    def build_block(pieces):
        peer_block, row_block, coeff_block = pieces
        peer_hot = jnp.where(
            peer_block[:, :, None] == jnp.arange(shard_count, dtype=jnp.int32),
            coeff_block[:, :, None],
            jnp.zeros((), jnp.bfloat16),
        )
        row_hot = (row_block[:, :, None] == jnp.arange(peer_span, dtype=jnp.int32)).astype(
            jnp.bfloat16
        )
        joined = jnp.einsum("nkp,nkr->npr", peer_hot, row_hot, preferred_element_type=jnp.float32)
        return joined.reshape(block_rows, column_total)

    adjacency = (
        lax.map(build_block, (peer_part, row_part, coeff_blocks))
        .reshape(nodes, column_total)
        .astype(jnp.bfloat16)
    )
    tile_count = nodes // TILE
    embed_tiles = embed_bf.reshape(tile_count, TILE, width)
    outgoing = embed_tiles.at[tile_list[0].reshape(shard_count * list_len)].get(mode="promise_in_bounds")
    outgoing = outgoing.reshape(shard_count, peer_span, width)
    provided = lax.all_to_all(outgoing, "shard", split_axis=0, concat_axis=0, tiled=True)
    provided = provided.reshape(column_total, width)
    gathered_sum = jnp.dot(adjacency, provided, preferred_element_type=jnp.float32)
    self_term = jnp.dot(embed_bf, w_self, preferred_element_type=jnp.float32) + bias_v
    pre_act = self_term + jnp.dot(gathered_sum.astype(jnp.bfloat16), w_nbr, preferred_element_type=jnp.float32)
    node_hidden = jax.nn.relu(pre_act).astype(jnp.bfloat16)
    confidence = jnp.dot(node_hidden, w_conf, preferred_element_type=jnp.float32)
    device_total = send_rows.shape[1]
    capacity = send_rows.shape[2]
    hidden_width = node_hidden.shape[1]
    slot_total = device_total * capacity
    send_flat = send_rows[0].reshape(slot_total)
    send_chooser = select_matrix(send_flat, nodes, jnp.bfloat16)
    outbound = jnp.dot(send_chooser, node_hidden, preferred_element_type=jnp.float32).astype(
        jnp.bfloat16
    )
    outbound = outbound.reshape(device_total, capacity, hidden_width)
    received = lax.all_to_all(outbound, ("grp", "shard"), split_axis=0, concat_axis=0, tiled=True)
    received_rows = received.reshape(slot_total, hidden_width)
    sub_count = members.shape[0]
    member_width = members.shape[1]
    member_flat = members.reshape(sub_count * member_width)
    member_chooser = select_matrix(member_flat, slot_total, jnp.bfloat16)
    member_rows = jnp.dot(member_chooser, received_rows, preferred_element_type=jnp.float32)
    member_rows = member_rows.reshape(sub_count, member_width, hidden_width)
    relative = member_rows - member_rows[:, :1, :]
    alive = jnp.arange(member_width, dtype=jnp.int32)[None, :] < sub_len[:, None]
    masked = jnp.where(alive[:, :, None], relative, 0.0)
    context = (jnp.sum(masked, axis=1) / sub_len[:, None].astype(jnp.float32)).astype(jnp.bfloat16)
    relative_bf = relative.astype(jnp.bfloat16)
    inner = jnp.einsum("smh,hk->smk", relative_bf, w_diff, preferred_element_type=jnp.float32)
    inner = inner + jnp.dot(context, w_ctx, preferred_element_type=jnp.float32)[:, None, :] + bias_e
    edge_hidden = jax.nn.relu(inner).astype(jnp.bfloat16)
    logits = jnp.einsum("smk,k->sm", edge_hidden, w_edge, preferred_element_type=jnp.float32)
    edge_scores = jnp.where(alive, jax.nn.sigmoid(logits), 0.0)
    slot_scores = scatter_sum(member_flat, edge_scores.reshape(sub_count * member_width), slot_total)
    slot_scores = slot_scores.reshape(device_total, capacity)
    returned = lax.all_to_all(
        slot_scores, ("grp", "shard"), split_axis=0, concat_axis=0, tiled=True
    )
    node_votes = scatter_sum(send_flat, returned.reshape(slot_total), nodes)
    return (node_hidden, confidence, edge_scores, node_votes)


def solution(mesh):
    return jax.shard_map(
        body,
        mesh=mesh,
        in_specs=(
            P(("grp", "shard"), None),
            P(("grp", "shard"), None),
            P(("grp", "shard"), None),
            P(("grp", "shard"), None, None),
            P(("grp", "shard"), None, None),
            P(("grp", "shard"), None),
            P(("grp", "shard")),
            P(),
            P(),
            P(),
            P(),
            P(),
            P(),
            P(),
            P(),
        ),
        out_specs=(
            P(("grp", "shard"), None),
            P(("grp", "shard")),
            P(("grp", "shard"), None),
            P(("grp", "shard")),
        ),
        check_vma=False,
    )
```

```python
import math

import jax
import jax.numpy as jnp
from jax import lax
from jax.sharding import PartitionSpec as P

TILE = 128


def select_matrix(indices, count, dtype):
    return (indices[:, None] == jnp.arange(count, dtype=jnp.int32)[None, :]).astype(dtype)


def scatter_sum(indices, values, count):
    hit = indices[:, None] == jnp.arange(count, dtype=jnp.int32)[None, :]
    return jnp.sum(jnp.where(hit, values[:, None], jnp.float32(0.0)), axis=0)


def body(
    embed,
    knn_slot,
    knn_weight,
    tile_list,
    send_rows,
    members,
    sub_len,
    w_self,
    w_nbr,
    bias_v,
    w_conf,
    w_diff,
    w_ctx,
    bias_e,
    w_edge,
):
    nodes = embed.shape[0]
    width = embed.shape[1]
    neighbour_count = knn_slot.shape[1]
    shard_count = lax.axis_size("shard")
    list_len = tile_list.shape[2]
    peer_span = list_len * TILE
    column_total = shard_count * peer_span
    embed_bf = embed.astype(jnp.bfloat16)
    weight_sum = jnp.sum(knn_weight, axis=1, keepdims=True)
    coeff_bf = (knn_weight / weight_sum).astype(jnp.bfloat16)
    block_rows = math.gcd(nodes, 256)
    block_count = nodes // block_rows
    peer_part = (knn_slot // peer_span).reshape(block_count, block_rows, neighbour_count)
    row_part = (knn_slot % peer_span).reshape(block_count, block_rows, neighbour_count)
    coeff_blocks = coeff_bf.reshape(block_count, block_rows, neighbour_count)

    def build_block(pieces):
        peer_block, row_block, coeff_block = pieces
        peer_hot = jnp.where(
            peer_block[:, :, None] == jnp.arange(shard_count, dtype=jnp.int32),
            coeff_block[:, :, None],
            jnp.zeros((), jnp.bfloat16),
        )
        row_hot = (row_block[:, :, None] == jnp.arange(peer_span, dtype=jnp.int32)).astype(
            jnp.bfloat16
        )
        joined = jnp.einsum("nkp,nkr->npr", peer_hot, row_hot, preferred_element_type=jnp.float32)
        return joined.reshape(block_rows, column_total)

    adjacency = (
        lax.map(build_block, (peer_part, row_part, coeff_blocks))
        .reshape(nodes, column_total)
        .astype(jnp.bfloat16)
    )
    tile_count = nodes // TILE
    embed_tiles = embed_bf.reshape(tile_count, TILE, width)
    outgoing = embed_tiles.at[tile_list[0].reshape(shard_count * list_len)].get(mode="promise_in_bounds")
    outgoing = outgoing.reshape(shard_count, peer_span, width)
    provided = lax.all_to_all(outgoing, "shard", split_axis=0, concat_axis=0, tiled=True)
    provided = provided.reshape(column_total, width)
    gathered_sum = jnp.dot(adjacency, provided, preferred_element_type=jnp.float32)
    self_term = jnp.dot(embed_bf, w_self, preferred_element_type=jnp.float32) + bias_v
    pre_act = self_term + jnp.dot(gathered_sum.astype(jnp.bfloat16), w_nbr, preferred_element_type=jnp.float32)
    node_hidden = jax.nn.relu(pre_act).astype(jnp.bfloat16)
    confidence = jnp.dot(node_hidden, w_conf, preferred_element_type=jnp.float32)
    device_total = send_rows.shape[1]
    capacity = send_rows.shape[2]
    hidden_width = node_hidden.shape[1]
    slot_total = device_total * capacity
    send_flat = send_rows[0].reshape(slot_total)
    outbound = node_hidden.at[send_flat].get(mode="promise_in_bounds")
    outbound = outbound.reshape(device_total, capacity, hidden_width)
    received = lax.all_to_all(outbound, ("grp", "shard"), split_axis=0, concat_axis=0, tiled=True)
    received_rows = received.reshape(slot_total, hidden_width)
    sub_count = members.shape[0]
    member_width = members.shape[1]
    member_flat = members.reshape(sub_count * member_width)
    member_rows = received_rows.at[member_flat].get(mode="promise_in_bounds").astype(jnp.float32)
    member_rows = member_rows.reshape(sub_count, member_width, hidden_width)
    relative = member_rows - member_rows[:, :1, :]
    alive = jnp.arange(member_width, dtype=jnp.int32)[None, :] < sub_len[:, None]
    masked = jnp.where(alive[:, :, None], relative, 0.0)
    context = (jnp.sum(masked, axis=1) / sub_len[:, None].astype(jnp.float32)).astype(jnp.bfloat16)
    relative_bf = relative.astype(jnp.bfloat16)
    inner = jnp.einsum("smh,hk->smk", relative_bf, w_diff, preferred_element_type=jnp.float32)
    inner = inner + jnp.dot(context, w_ctx, preferred_element_type=jnp.float32)[:, None, :] + bias_e
    edge_hidden = jax.nn.relu(inner).astype(jnp.bfloat16)
    logits = jnp.einsum("smk,k->sm", edge_hidden, w_edge, preferred_element_type=jnp.float32)
    edge_scores = jnp.where(alive, jax.nn.sigmoid(logits), 0.0)
    slot_scores = scatter_sum(member_flat, edge_scores.reshape(sub_count * member_width), slot_total)
    slot_scores = slot_scores.reshape(device_total, capacity)
    returned = lax.all_to_all(
        slot_scores, ("grp", "shard"), split_axis=0, concat_axis=0, tiled=True
    )
    node_votes = scatter_sum(send_flat, returned.reshape(slot_total), nodes)
    return (node_hidden, confidence, edge_scores, node_votes)


def solution(mesh):
    return jax.shard_map(
        body,
        mesh=mesh,
        in_specs=(
            P(("grp", "shard"), None),
            P(("grp", "shard"), None),
            P(("grp", "shard"), None),
            P(("grp", "shard"), None, None),
            P(("grp", "shard"), None, None),
            P(("grp", "shard"), None),
            P(("grp", "shard")),
            P(),
            P(),
            P(),
            P(),
            P(),
            P(),
            P(),
            P(),
        ),
        out_specs=(
            P(("grp", "shard"), None),
            P(("grp", "shard")),
            P(("grp", "shard"), None),
            P(("grp", "shard")),
        ),
        check_vma=False,
    )
```

```python
import math

import jax
import jax.numpy as jnp
from jax import lax
from jax.experimental import pallas as pl
from jax.experimental.pallas import tpu as pltpu
from jax.sharding import PartitionSpec as P

TILE = 128


def node_kernel(adj_ref, table_ref, embed_ref, w_self_ref, w_nbr_ref, bias_ref, send_ref, out_ref, outbound_ref, held_ref):
    b = pl.program_id(0)
    rows = out_ref.shape[0]
    total = jnp.dot(adj_ref[...], table_ref[...], preferred_element_type=jnp.float32)
    pre = (
        jnp.dot(embed_ref[...], w_self_ref[...], preferred_element_type=jnp.float32)
        + bias_ref[...]
        + jnp.dot(total.astype(jnp.bfloat16), w_nbr_ref[...], preferred_element_type=jnp.float32)
    )
    hidden = jnp.maximum(pre, 0.0).astype(out_ref.dtype)
    out_ref[...] = hidden
    held_ref[pl.ds(pl.multiple_of(b * rows, rows), rows), :] = hidden

    @pl.when(b == pl.num_programs(0) - 1)
    def _():
        nodes = held_ref.shape[0]
        chooser = jnp.where(
            send_ref[...] == lax.broadcasted_iota(jnp.int32, (send_ref.shape[0], nodes), 1), 1.0, 0.0
        ).astype(jnp.bfloat16)
        outbound_ref[...] = jnp.dot(chooser, held_ref[...], preferred_element_type=jnp.float32).astype(
            outbound_ref.dtype
        )


def node_layer(adjacency, table, embed_bf, w_self, w_nbr, bias, send_flat):
    nodes, width = embed_bf.shape
    hidden = w_self.shape[1]
    columns = adjacency.shape[1]
    rows = 128
    slots = send_flat.shape[0]
    return pl.pallas_call(
        node_kernel,
        grid=(nodes // rows,),
        in_specs=[
            pl.BlockSpec((rows, columns), lambda b: (b, 0)),
            pl.BlockSpec(table.shape, lambda b: (0, 0)),
            pl.BlockSpec((rows, width), lambda b: (b, 0)),
            pl.BlockSpec(w_self.shape, lambda b: (0, 0)),
            pl.BlockSpec(w_nbr.shape, lambda b: (0, 0)),
            pl.BlockSpec((1, hidden), lambda b: (0, 0)),
            pl.BlockSpec((slots, 1), lambda b: (0, 0)),
        ],
        out_specs=[
            pl.BlockSpec((rows, hidden), lambda b: (b, 0)),
            pl.BlockSpec((slots, hidden), lambda b: (0, 0)),
        ],
        out_shape=[
            jax.ShapeDtypeStruct((nodes, hidden), jnp.bfloat16),
            jax.ShapeDtypeStruct((slots, hidden), jnp.bfloat16),
        ],
        scratch_shapes=[pltpu.VMEM((nodes, hidden), jnp.bfloat16)],
        compiler_params=pltpu.CompilerParams(vmem_limit_bytes=48 * 1024 * 1024),
    )(adjacency, table, embed_bf, w_self, w_nbr, bias.reshape(1, hidden), send_flat.reshape(slots, 1))


def select_matrix(indices, count, dtype):
    return (indices[:, None] == jnp.arange(count, dtype=jnp.int32)[None, :]).astype(dtype)


def scatter_sum(indices, values, count):
    hit = indices[:, None] == jnp.arange(count, dtype=jnp.int32)[None, :]
    return jnp.sum(jnp.where(hit, values[:, None], jnp.float32(0.0)), axis=0)


def body(
    embed,
    knn_slot,
    knn_weight,
    tile_list,
    send_rows,
    members,
    sub_len,
    w_self,
    w_nbr,
    bias_v,
    w_conf,
    w_diff,
    w_ctx,
    bias_e,
    w_edge,
):
    nodes = embed.shape[0]
    width = embed.shape[1]
    neighbour_count = knn_slot.shape[1]
    shard_count = lax.axis_size("shard")
    list_len = tile_list.shape[2]
    peer_span = list_len * TILE
    column_total = shard_count * peer_span
    embed_bf = embed.astype(jnp.bfloat16)
    weight_sum = jnp.sum(knn_weight, axis=1, keepdims=True)
    coeff_bf = (knn_weight / weight_sum).astype(jnp.bfloat16)
    block_rows = math.gcd(nodes, 256)
    block_count = nodes // block_rows
    peer_part = (knn_slot // peer_span).reshape(block_count, block_rows, neighbour_count)
    row_part = (knn_slot % peer_span).reshape(block_count, block_rows, neighbour_count)
    coeff_blocks = coeff_bf.reshape(block_count, block_rows, neighbour_count)

    def build_block(pieces):
        peer_block, row_block, coeff_block = pieces
        peer_hot = jnp.where(
            peer_block[:, :, None] == jnp.arange(shard_count, dtype=jnp.int32),
            coeff_block[:, :, None],
            jnp.zeros((), jnp.bfloat16),
        )
        row_hot = (row_block[:, :, None] == jnp.arange(peer_span, dtype=jnp.int32)).astype(
            jnp.bfloat16
        )
        joined = jnp.einsum("nkp,nkr->npr", peer_hot, row_hot, preferred_element_type=jnp.float32)
        return joined.reshape(block_rows, column_total)

    adjacency = (
        lax.map(build_block, (peer_part, row_part, coeff_blocks))
        .reshape(nodes, column_total)
        .astype(jnp.bfloat16)
    )
    tile_count = nodes // TILE
    embed_tiles = embed_bf.reshape(tile_count, TILE, width)
    outgoing = embed_tiles.at[tile_list[0].reshape(shard_count * list_len)].get(mode="promise_in_bounds")
    outgoing = outgoing.reshape(shard_count, peer_span, width)
    provided = lax.all_to_all(outgoing, "shard", split_axis=0, concat_axis=0, tiled=True)
    provided = provided.reshape(column_total, width)
    send_flat = send_rows[0].reshape(send_rows.shape[1] * send_rows.shape[2])
    node_hidden, outbound = node_layer(adjacency, provided, embed_bf, w_self, w_nbr, bias_v, send_flat)
    confidence = jnp.dot(node_hidden, w_conf, preferred_element_type=jnp.float32)
    device_total = send_rows.shape[1]
    capacity = send_rows.shape[2]
    hidden_width = node_hidden.shape[1]
    slot_total = device_total * capacity
    outbound = outbound.reshape(device_total, capacity, hidden_width)
    received = lax.all_to_all(outbound, ("grp", "shard"), split_axis=0, concat_axis=0, tiled=True)
    received_rows = received.reshape(slot_total, hidden_width)
    sub_count = members.shape[0]
    member_width = members.shape[1]
    member_flat = members.reshape(sub_count * member_width)
    member_chooser = select_matrix(member_flat, slot_total, jnp.bfloat16)
    member_rows = jnp.dot(member_chooser, received_rows, preferred_element_type=jnp.float32)
    member_rows = member_rows.reshape(sub_count, member_width, hidden_width)
    relative = member_rows - member_rows[:, :1, :]
    alive = jnp.arange(member_width, dtype=jnp.int32)[None, :] < sub_len[:, None]
    masked = jnp.where(alive[:, :, None], relative, 0.0)
    context = (jnp.sum(masked, axis=1) / sub_len[:, None].astype(jnp.float32)).astype(jnp.bfloat16)
    relative_bf = relative.astype(jnp.bfloat16)
    inner = jnp.einsum("smh,hk->smk", relative_bf, w_diff, preferred_element_type=jnp.float32)
    inner = inner + jnp.dot(context, w_ctx, preferred_element_type=jnp.float32)[:, None, :] + bias_e
    edge_hidden = jax.nn.relu(inner).astype(jnp.bfloat16)
    logits = jnp.einsum("smk,k->sm", edge_hidden, w_edge, preferred_element_type=jnp.float32)
    edge_scores = jnp.where(alive, jax.nn.sigmoid(logits), 0.0)
    slot_scores = scatter_sum(member_flat, edge_scores.reshape(sub_count * member_width), slot_total)
    slot_scores = slot_scores.reshape(device_total, capacity)
    returned = lax.all_to_all(
        slot_scores, ("grp", "shard"), split_axis=0, concat_axis=0, tiled=True
    )
    node_votes = scatter_sum(send_flat, returned.reshape(slot_total), nodes)
    return (node_hidden, confidence, edge_scores, node_votes)


def solution(mesh):
    return jax.shard_map(
        body,
        mesh=mesh,
        in_specs=(
            P(("grp", "shard"), None),
            P(("grp", "shard"), None),
            P(("grp", "shard"), None),
            P(("grp", "shard"), None, None),
            P(("grp", "shard"), None, None),
            P(("grp", "shard"), None),
            P(("grp", "shard")),
            P(),
            P(),
            P(),
            P(),
            P(),
            P(),
            P(),
            P(),
        ),
        out_specs=(
            P(("grp", "shard"), None),
            P(("grp", "shard")),
            P(("grp", "shard"), None),
            P(("grp", "shard")),
        ),
        check_vma=False,
    )
```

```python
import math

import jax
import jax.numpy as jnp
from jax import lax
from jax.experimental import pallas as pl
from jax.experimental.pallas import tpu as pltpu
from jax.sharding import PartitionSpec as P

TILE = 128


SUB = 8


def adjacency_kernel(slot_ref, coef_ref, out_ref, acc_ref):
    span = 256
    peers = out_ref.shape[1] // span
    sub_count = out_ref.shape[0] // SUB
    width = slot_ref.shape[1]
    row_hit = lax.broadcasted_iota(jnp.int32, (span, width), 0)
    lane_node = lax.broadcasted_iota(jnp.int32, (peers * SUB, width), 1) // (width // SUB)
    pair_row = lax.broadcasted_iota(jnp.int32, (peers * SUB, width), 0)
    pair_peer = pair_row // SUB
    pair_node = pair_row % SUB

    def one_sub(s, carry):
        slots = slot_ref[pl.ds(s, 1), :]
        coefs = coef_ref[pl.ds(s, 1), :]
        onehot = jnp.where(row_hit == slots % span, 1.0, 0.0).astype(jnp.bfloat16)
        picked = (pair_peer == slots // span) & (pair_node == lane_node)
        weights = jnp.where(picked, coefs, 0.0).astype(jnp.bfloat16)
        block = lax.dot_general(
            weights, onehot, (((1,), (1,)), ((), ())), preferred_element_type=jnp.float32
        )
        block = block.astype(jnp.bfloat16).astype(jnp.float32)
        rows = pl.ds(pl.multiple_of(s * SUB, SUB), SUB)
        for p in range(peers):
            acc_ref[rows, p * span:(p + 1) * span] = block[p * SUB:(p + 1) * SUB, :]
        return carry

    lax.fori_loop(0, sub_count, one_sub, 0)
    out_ref[...] = acc_ref[...].astype(out_ref.dtype)


def build_adjacency(slot_rows, coef_rows, nodes, columns):
    rows = 128
    subs = rows // SUB
    return pl.pallas_call(
        adjacency_kernel,
        grid=(nodes // rows,),
        in_specs=[
            pl.BlockSpec((subs, slot_rows.shape[1]), lambda b: (b, 0)),
            pl.BlockSpec((subs, coef_rows.shape[1]), lambda b: (b, 0)),
        ],
        out_specs=pl.BlockSpec((rows, columns), lambda b: (b, 0)),
        out_shape=jax.ShapeDtypeStruct((nodes, columns), jnp.bfloat16),
        scratch_shapes=[pltpu.VMEM((rows, columns), jnp.float32)],
    )(slot_rows, coef_rows)


def node_kernel(adj_ref, table_ref, embed_ref, w_self_ref, w_nbr_ref, bias_ref, send_ref, out_ref, outbound_ref, held_ref):
    b = pl.program_id(0)
    rows = out_ref.shape[0]
    total = jnp.dot(adj_ref[...], table_ref[...], preferred_element_type=jnp.float32)
    pre = (
        jnp.dot(embed_ref[...], w_self_ref[...], preferred_element_type=jnp.float32)
        + bias_ref[...]
        + jnp.dot(total.astype(jnp.bfloat16), w_nbr_ref[...], preferred_element_type=jnp.float32)
    )
    hidden = jnp.maximum(pre, 0.0).astype(out_ref.dtype)
    out_ref[...] = hidden
    held_ref[pl.ds(pl.multiple_of(b * rows, rows), rows), :] = hidden

    @pl.when(b == pl.num_programs(0) - 1)
    def _():
        nodes = held_ref.shape[0]
        chooser = jnp.where(
            send_ref[...] == lax.broadcasted_iota(jnp.int32, (send_ref.shape[0], nodes), 1), 1.0, 0.0
        ).astype(jnp.bfloat16)
        outbound_ref[...] = jnp.dot(chooser, held_ref[...], preferred_element_type=jnp.float32).astype(
            outbound_ref.dtype
        )


def node_layer(adjacency, table, embed_bf, w_self, w_nbr, bias, send_flat):
    nodes, width = embed_bf.shape
    hidden = w_self.shape[1]
    columns = adjacency.shape[1]
    rows = 128
    slots = send_flat.shape[0]
    return pl.pallas_call(
        node_kernel,
        grid=(nodes // rows,),
        in_specs=[
            pl.BlockSpec((rows, columns), lambda b: (b, 0)),
            pl.BlockSpec(table.shape, lambda b: (0, 0)),
            pl.BlockSpec((rows, width), lambda b: (b, 0)),
            pl.BlockSpec(w_self.shape, lambda b: (0, 0)),
            pl.BlockSpec(w_nbr.shape, lambda b: (0, 0)),
            pl.BlockSpec((1, hidden), lambda b: (0, 0)),
            pl.BlockSpec((slots, 1), lambda b: (0, 0)),
        ],
        out_specs=[
            pl.BlockSpec((rows, hidden), lambda b: (b, 0)),
            pl.BlockSpec((slots, hidden), lambda b: (0, 0)),
        ],
        out_shape=[
            jax.ShapeDtypeStruct((nodes, hidden), jnp.bfloat16),
            jax.ShapeDtypeStruct((slots, hidden), jnp.bfloat16),
        ],
        scratch_shapes=[pltpu.VMEM((nodes, hidden), jnp.bfloat16)],
        compiler_params=pltpu.CompilerParams(vmem_limit_bytes=48 * 1024 * 1024),
    )(adjacency, table, embed_bf, w_self, w_nbr, bias.reshape(1, hidden), send_flat.reshape(slots, 1))


def select_matrix(indices, count, dtype):
    return (indices[:, None] == jnp.arange(count, dtype=jnp.int32)[None, :]).astype(dtype)


def scatter_sum(indices, values, count):
    hit = indices[:, None] == jnp.arange(count, dtype=jnp.int32)[None, :]
    return jnp.sum(jnp.where(hit, values[:, None], jnp.float32(0.0)), axis=0)


def body(
    embed,
    knn_slot,
    knn_weight,
    tile_list,
    send_rows,
    members,
    sub_len,
    w_self,
    w_nbr,
    bias_v,
    w_conf,
    w_diff,
    w_ctx,
    bias_e,
    w_edge,
):
    nodes = embed.shape[0]
    width = embed.shape[1]
    neighbour_count = knn_slot.shape[1]
    shard_count = lax.axis_size("shard")
    list_len = tile_list.shape[2]
    peer_span = list_len * TILE
    column_total = shard_count * peer_span
    embed_bf = embed.astype(jnp.bfloat16)
    weight_sum = jnp.sum(knn_weight, axis=1, keepdims=True)
    coeff_bf = (knn_weight / weight_sum).astype(jnp.bfloat16)
    sub_rows = nodes // SUB
    adjacency = build_adjacency(
        knn_slot.reshape(sub_rows, SUB * neighbour_count),
        coeff_bf.astype(jnp.float32).reshape(sub_rows, SUB * neighbour_count),
        nodes,
        column_total,
    )
    tile_count = nodes // TILE
    embed_tiles = embed_bf.reshape(tile_count, TILE, width)
    outgoing = embed_tiles.at[tile_list[0].reshape(shard_count * list_len)].get(mode="promise_in_bounds")
    outgoing = outgoing.reshape(shard_count, peer_span, width)
    provided = lax.all_to_all(outgoing, "shard", split_axis=0, concat_axis=0, tiled=True)
    provided = provided.reshape(column_total, width)
    send_flat = send_rows[0].reshape(send_rows.shape[1] * send_rows.shape[2])
    node_hidden, outbound = node_layer(adjacency, provided, embed_bf, w_self, w_nbr, bias_v, send_flat)
    confidence = jnp.dot(node_hidden, w_conf, preferred_element_type=jnp.float32)
    device_total = send_rows.shape[1]
    capacity = send_rows.shape[2]
    hidden_width = node_hidden.shape[1]
    slot_total = device_total * capacity
    outbound = outbound.reshape(device_total, capacity, hidden_width)
    received = lax.all_to_all(outbound, ("grp", "shard"), split_axis=0, concat_axis=0, tiled=True)
    received_rows = received.reshape(slot_total, hidden_width)
    sub_count = members.shape[0]
    member_width = members.shape[1]
    member_flat = members.reshape(sub_count * member_width)
    member_chooser = select_matrix(member_flat, slot_total, jnp.bfloat16)
    member_rows = jnp.dot(member_chooser, received_rows, preferred_element_type=jnp.float32)
    member_rows = member_rows.reshape(sub_count, member_width, hidden_width)
    relative = member_rows - member_rows[:, :1, :]
    alive = jnp.arange(member_width, dtype=jnp.int32)[None, :] < sub_len[:, None]
    masked = jnp.where(alive[:, :, None], relative, 0.0)
    context = (jnp.sum(masked, axis=1) / sub_len[:, None].astype(jnp.float32)).astype(jnp.bfloat16)
    relative_bf = relative.astype(jnp.bfloat16)
    inner = jnp.einsum("smh,hk->smk", relative_bf, w_diff, preferred_element_type=jnp.float32)
    inner = inner + jnp.dot(context, w_ctx, preferred_element_type=jnp.float32)[:, None, :] + bias_e
    edge_hidden = jax.nn.relu(inner).astype(jnp.bfloat16)
    logits = jnp.einsum("smk,k->sm", edge_hidden, w_edge, preferred_element_type=jnp.float32)
    edge_scores = jnp.where(alive, jax.nn.sigmoid(logits), 0.0)
    slot_scores = scatter_sum(member_flat, edge_scores.reshape(sub_count * member_width), slot_total)
    slot_scores = slot_scores.reshape(device_total, capacity)
    returned = lax.all_to_all(
        slot_scores, ("grp", "shard"), split_axis=0, concat_axis=0, tiled=True
    )
    node_votes = scatter_sum(send_flat, returned.reshape(slot_total), nodes)
    return (node_hidden, confidence, edge_scores, node_votes)


def solution(mesh):
    return jax.shard_map(
        body,
        mesh=mesh,
        in_specs=(
            P(("grp", "shard"), None),
            P(("grp", "shard"), None),
            P(("grp", "shard"), None),
            P(("grp", "shard"), None, None),
            P(("grp", "shard"), None, None),
            P(("grp", "shard"), None),
            P(("grp", "shard")),
            P(),
            P(),
            P(),
            P(),
            P(),
            P(),
            P(),
            P(),
        ),
        out_specs=(
            P(("grp", "shard"), None),
            P(("grp", "shard")),
            P(("grp", "shard"), None),
            P(("grp", "shard")),
        ),
        check_vma=False,
    )
```

```python
import math

import jax
import jax.numpy as jnp
from jax import lax
from jax.experimental import pallas as pl
from jax.experimental.pallas import tpu as pltpu
from jax.sharding import PartitionSpec as P

TILE = 128


SUB = 8


def adjacency_kernel(slot_ref, coef_ref, out_ref, acc_ref):
    span = 256
    peers = out_ref.shape[1] // span
    sub_count = out_ref.shape[0] // SUB
    width = slot_ref.shape[1]
    row_hit = lax.broadcasted_iota(jnp.int32, (span, width), 0)
    lane_node = lax.broadcasted_iota(jnp.int32, (peers * SUB, width), 1) // (width // SUB)
    pair_row = lax.broadcasted_iota(jnp.int32, (peers * SUB, width), 0)
    pair_peer = pair_row // SUB
    pair_node = pair_row % SUB

    def one_sub(s, carry):
        slots = slot_ref[pl.ds(s, 1), :]
        coefs = coef_ref[pl.ds(s, 1), :]
        onehot = jnp.where(row_hit == slots % span, 1.0, 0.0).astype(jnp.bfloat16)
        picked = (pair_peer == slots // span) & (pair_node == lane_node)
        weights = jnp.where(picked, coefs, 0.0).astype(jnp.bfloat16)
        block = lax.dot_general(
            weights, onehot, (((1,), (1,)), ((), ())), preferred_element_type=jnp.float32
        )
        block = block.astype(jnp.bfloat16).astype(jnp.float32)
        rows = pl.ds(pl.multiple_of(s * SUB, SUB), SUB)
        for p in range(peers):
            acc_ref[rows, p * span:(p + 1) * span] = block[p * SUB:(p + 1) * SUB, :]
        return carry

    lax.fori_loop(0, sub_count, one_sub, 0)
    out_ref[...] = acc_ref[...].astype(out_ref.dtype)


def build_adjacency(slot_rows, coef_rows, nodes, columns):
    rows = 128
    subs = rows // SUB
    return pl.pallas_call(
        adjacency_kernel,
        grid=(nodes // rows,),
        in_specs=[
            pl.BlockSpec((subs, slot_rows.shape[1]), lambda b: (b, 0)),
            pl.BlockSpec((subs, coef_rows.shape[1]), lambda b: (b, 0)),
        ],
        out_specs=pl.BlockSpec((rows, columns), lambda b: (b, 0)),
        out_shape=jax.ShapeDtypeStruct((nodes, columns), jnp.bfloat16),
        scratch_shapes=[pltpu.VMEM((rows, columns), jnp.float32)],
    )(slot_rows, coef_rows)


def node_kernel(adj_ref, table_ref, self_ref, w_nbr_ref, out_ref):
    total = jnp.dot(adj_ref[...], table_ref[...], preferred_element_type=jnp.float32)
    pre = self_ref[...] + jnp.dot(total.astype(jnp.bfloat16), w_nbr_ref[...], preferred_element_type=jnp.float32)
    out_ref[...] = jnp.maximum(pre, 0.0).astype(out_ref.dtype)


def node_layer(adjacency, table, self_term, w_nbr):
    count, columns = adjacency.shape
    hidden = w_nbr.shape[1]
    rows = 128
    return pl.pallas_call(
        node_kernel,
        grid=(count // rows,),
        in_specs=[
            pl.BlockSpec((rows, columns), lambda b: (b, 0)),
            pl.BlockSpec(table.shape, lambda b: (0, 0)),
            pl.BlockSpec((rows, hidden), lambda b: (b, 0)),
            pl.BlockSpec(w_nbr.shape, lambda b: (0, 0)),
        ],
        out_specs=pl.BlockSpec((rows, hidden), lambda b: (b, 0)),
        out_shape=jax.ShapeDtypeStruct((count, hidden), jnp.bfloat16),
        compiler_params=pltpu.CompilerParams(vmem_limit_bytes=48 * 1024 * 1024),
    )(adjacency, table, self_term, w_nbr)


def select_matrix(indices, count, dtype):
    return (indices[:, None] == jnp.arange(count, dtype=jnp.int32)[None, :]).astype(dtype)


def scatter_sum(indices, values, count):
    hit = indices[:, None] == jnp.arange(count, dtype=jnp.int32)[None, :]
    return jnp.sum(jnp.where(hit, values[:, None], jnp.float32(0.0)), axis=0)


def body(
    embed,
    knn_slot,
    knn_weight,
    tile_list,
    send_rows,
    members,
    sub_len,
    w_self,
    w_nbr,
    bias_v,
    w_conf,
    w_diff,
    w_ctx,
    bias_e,
    w_edge,
):
    nodes = embed.shape[0]
    width = embed.shape[1]
    neighbour_count = knn_slot.shape[1]
    shard_count = lax.axis_size("shard")
    list_len = tile_list.shape[2]
    peer_span = list_len * TILE
    column_total = shard_count * peer_span
    embed_bf = embed.astype(jnp.bfloat16)
    weight_sum = jnp.sum(knn_weight, axis=1, keepdims=True)
    coeff_bf = (knn_weight / weight_sum).astype(jnp.bfloat16)
    sub_rows = nodes // SUB
    adjacency = build_adjacency(
        knn_slot.reshape(sub_rows, SUB * neighbour_count),
        coeff_bf.astype(jnp.float32).reshape(sub_rows, SUB * neighbour_count),
        nodes,
        column_total,
    )
    tile_count = nodes // TILE
    embed_tiles = embed_bf.reshape(tile_count, TILE, width)
    outgoing = embed_tiles.at[tile_list[0].reshape(shard_count * list_len)].get(mode="promise_in_bounds")
    outgoing = outgoing.reshape(shard_count, peer_span, width)
    provided = lax.all_to_all(outgoing, "shard", split_axis=0, concat_axis=0, tiled=True)
    provided = provided.reshape(column_total, width)
    send_flat = send_rows[0].reshape(send_rows.shape[1] * send_rows.shape[2])
    self_term = jnp.dot(embed_bf, w_self, preferred_element_type=jnp.float32) + bias_v
    send_adjacency = adjacency.at[send_flat].get(mode="promise_in_bounds")
    send_self = self_term.at[send_flat].get(mode="promise_in_bounds")
    outbound = node_layer(send_adjacency, provided, send_self, w_nbr)
    node_hidden = node_layer(adjacency, provided, self_term, w_nbr)
    confidence = jnp.dot(node_hidden, w_conf, preferred_element_type=jnp.float32)
    device_total = send_rows.shape[1]
    capacity = send_rows.shape[2]
    hidden_width = node_hidden.shape[1]
    slot_total = device_total * capacity
    outbound = outbound.reshape(device_total, capacity, hidden_width)
    received = lax.all_to_all(outbound, ("grp", "shard"), split_axis=0, concat_axis=0, tiled=True)
    received_rows = received.reshape(slot_total, hidden_width)
    sub_count = members.shape[0]
    member_width = members.shape[1]
    member_flat = members.reshape(sub_count * member_width)
    member_chooser = select_matrix(member_flat, slot_total, jnp.bfloat16)
    member_rows = jnp.dot(member_chooser, received_rows, preferred_element_type=jnp.float32)
    member_rows = member_rows.reshape(sub_count, member_width, hidden_width)
    relative = member_rows - member_rows[:, :1, :]
    alive = jnp.arange(member_width, dtype=jnp.int32)[None, :] < sub_len[:, None]
    masked = jnp.where(alive[:, :, None], relative, 0.0)
    context = (jnp.sum(masked, axis=1) / sub_len[:, None].astype(jnp.float32)).astype(jnp.bfloat16)
    relative_bf = relative.astype(jnp.bfloat16)
    inner = jnp.einsum("smh,hk->smk", relative_bf, w_diff, preferred_element_type=jnp.float32)
    inner = inner + jnp.dot(context, w_ctx, preferred_element_type=jnp.float32)[:, None, :] + bias_e
    edge_hidden = jax.nn.relu(inner).astype(jnp.bfloat16)
    logits = jnp.einsum("smk,k->sm", edge_hidden, w_edge, preferred_element_type=jnp.float32)
    edge_scores = jnp.where(alive, jax.nn.sigmoid(logits), 0.0)
    slot_scores = scatter_sum(member_flat, edge_scores.reshape(sub_count * member_width), slot_total)
    slot_scores = slot_scores.reshape(device_total, capacity)
    returned = lax.all_to_all(
        slot_scores, ("grp", "shard"), split_axis=0, concat_axis=0, tiled=True
    )
    node_votes = scatter_sum(send_flat, returned.reshape(slot_total), nodes)
    return (node_hidden, confidence, edge_scores, node_votes)


def solution(mesh):
    return jax.shard_map(
        body,
        mesh=mesh,
        in_specs=(
            P(("grp", "shard"), None),
            P(("grp", "shard"), None),
            P(("grp", "shard"), None),
            P(("grp", "shard"), None, None),
            P(("grp", "shard"), None, None),
            P(("grp", "shard"), None),
            P(("grp", "shard")),
            P(),
            P(),
            P(),
            P(),
            P(),
            P(),
            P(),
            P(),
        ),
        out_specs=(
            P(("grp", "shard"), None),
            P(("grp", "shard")),
            P(("grp", "shard"), None),
            P(("grp", "shard")),
        ),
        check_vma=False,
    )
```

```python
import math

import jax
import jax.numpy as jnp
from jax import lax
from jax.experimental import pallas as pl
from jax.experimental.pallas import tpu as pltpu
from jax.sharding import PartitionSpec as P

TILE = 128


SUB = 8


def adjacency_kernel(slot_ref, coef_ref, out_ref, acc_ref):
    span = 256
    peers = out_ref.shape[1] // span
    sub_count = out_ref.shape[0] // SUB
    width = slot_ref.shape[1]
    row_hit = lax.broadcasted_iota(jnp.int32, (span, width), 0)
    lane_node = lax.broadcasted_iota(jnp.int32, (peers * SUB, width), 1) // (width // SUB)
    pair_row = lax.broadcasted_iota(jnp.int32, (peers * SUB, width), 0)
    pair_peer = pair_row // SUB
    pair_node = pair_row % SUB

    def one_sub(s, carry):
        slots = slot_ref[pl.ds(s, 1), :]
        coefs = coef_ref[pl.ds(s, 1), :]
        onehot = jnp.where(row_hit == slots % span, 1.0, 0.0).astype(jnp.bfloat16)
        picked = (pair_peer == slots // span) & (pair_node == lane_node)
        weights = jnp.where(picked, coefs, 0.0).astype(jnp.bfloat16)
        block = lax.dot_general(
            weights, onehot, (((1,), (1,)), ((), ())), preferred_element_type=jnp.float32
        )
        block = block.astype(jnp.bfloat16).astype(jnp.float32)
        rows = pl.ds(pl.multiple_of(s * SUB, SUB), SUB)
        for p in range(peers):
            acc_ref[rows, p * span:(p + 1) * span] = block[p * SUB:(p + 1) * SUB, :]
        return carry

    lax.fori_loop(0, sub_count, one_sub, 0)
    out_ref[...] = acc_ref[...].astype(out_ref.dtype)


def build_adjacency(slot_rows, coef_rows, nodes, columns):
    rows = 128
    subs = rows // SUB
    return pl.pallas_call(
        adjacency_kernel,
        grid=(nodes // rows,),
        in_specs=[
            pl.BlockSpec((subs, slot_rows.shape[1]), lambda b: (b, 0)),
            pl.BlockSpec((subs, coef_rows.shape[1]), lambda b: (b, 0)),
        ],
        out_specs=pl.BlockSpec((rows, columns), lambda b: (b, 0)),
        out_shape=jax.ShapeDtypeStruct((nodes, columns), jnp.bfloat16),
        scratch_shapes=[pltpu.VMEM((rows, columns), jnp.float32)],
    )(slot_rows, coef_rows)


def node_kernel(adj_ref, table_ref, self_ref, w_nbr_ref, out_ref):
    total = jnp.dot(adj_ref[...], table_ref[...], preferred_element_type=jnp.float32)
    pre = self_ref[...] + jnp.dot(total.astype(jnp.bfloat16), w_nbr_ref[...], preferred_element_type=jnp.float32)
    out_ref[...] = jnp.maximum(pre, 0.0).astype(out_ref.dtype)


def node_layer(adjacency, table, self_term, w_nbr):
    count, columns = adjacency.shape
    hidden = w_nbr.shape[1]
    rows = 128
    return pl.pallas_call(
        node_kernel,
        grid=(count // rows,),
        in_specs=[
            pl.BlockSpec((rows, columns), lambda b: (b, 0)),
            pl.BlockSpec(table.shape, lambda b: (0, 0)),
            pl.BlockSpec((rows, hidden), lambda b: (b, 0)),
            pl.BlockSpec(w_nbr.shape, lambda b: (0, 0)),
        ],
        out_specs=pl.BlockSpec((rows, hidden), lambda b: (b, 0)),
        out_shape=jax.ShapeDtypeStruct((count, hidden), jnp.bfloat16),
        compiler_params=pltpu.CompilerParams(vmem_limit_bytes=48 * 1024 * 1024),
    )(adjacency, table, self_term, w_nbr)


def select_matrix(indices, count, dtype):
    return (indices[:, None] == jnp.arange(count, dtype=jnp.int32)[None, :]).astype(dtype)


def scatter_sum(indices, values, count):
    hit = indices[:, None] == jnp.arange(count, dtype=jnp.int32)[None, :]
    return jnp.sum(jnp.where(hit, values[:, None], jnp.float32(0.0)), axis=0)


def body(
    embed,
    knn_slot,
    knn_weight,
    tile_list,
    send_rows,
    members,
    sub_len,
    w_self,
    w_nbr,
    bias_v,
    w_conf,
    w_diff,
    w_ctx,
    bias_e,
    w_edge,
):
    nodes = embed.shape[0]
    width = embed.shape[1]
    neighbour_count = knn_slot.shape[1]
    shard_count = lax.axis_size("shard")
    list_len = tile_list.shape[2]
    peer_span = list_len * TILE
    column_total = shard_count * peer_span
    embed_bf = embed.astype(jnp.bfloat16)
    weight_sum = jnp.sum(knn_weight, axis=1, keepdims=True)
    coeff_bf = (knn_weight / weight_sum).astype(jnp.bfloat16)
    sub_rows = nodes // SUB
    adjacency = build_adjacency(
        knn_slot.reshape(sub_rows, SUB * neighbour_count),
        coeff_bf.astype(jnp.float32).reshape(sub_rows, SUB * neighbour_count),
        nodes,
        column_total,
    )
    tile_count = nodes // TILE
    embed_tiles = embed_bf.reshape(tile_count, TILE, width)
    outgoing = embed_tiles.at[tile_list[0].reshape(shard_count * list_len)].get(mode="promise_in_bounds")
    outgoing = outgoing.reshape(shard_count, peer_span, width)
    provided = lax.all_to_all(outgoing, "shard", split_axis=0, concat_axis=0, tiled=True)
    provided = provided.reshape(column_total, width)
    send_flat = send_rows[0].reshape(send_rows.shape[1] * send_rows.shape[2])
    self_term = jnp.dot(embed_bf, w_self, preferred_element_type=jnp.float32) + bias_v
    send_chooser = select_matrix(send_flat, nodes, jnp.bfloat16)
    send_adjacency = jnp.dot(send_chooser, adjacency, preferred_element_type=jnp.float32).astype(jnp.bfloat16)
    send_embed = jnp.dot(send_chooser, embed_bf, preferred_element_type=jnp.float32).astype(jnp.bfloat16)
    send_self = jnp.dot(send_embed, w_self, preferred_element_type=jnp.float32) + bias_v
    outbound = node_layer(send_adjacency, provided, send_self, w_nbr)
    node_hidden = node_layer(adjacency, provided, self_term, w_nbr)
    confidence = jnp.dot(node_hidden, w_conf, preferred_element_type=jnp.float32)
    device_total = send_rows.shape[1]
    capacity = send_rows.shape[2]
    hidden_width = node_hidden.shape[1]
    slot_total = device_total * capacity
    outbound = outbound.reshape(device_total, capacity, hidden_width)
    received = lax.all_to_all(outbound, ("grp", "shard"), split_axis=0, concat_axis=0, tiled=True)
    received_rows = received.reshape(slot_total, hidden_width)
    sub_count = members.shape[0]
    member_width = members.shape[1]
    member_flat = members.reshape(sub_count * member_width)
    member_chooser = select_matrix(member_flat, slot_total, jnp.bfloat16)
    member_rows = jnp.dot(member_chooser, received_rows, preferred_element_type=jnp.float32)
    member_rows = member_rows.reshape(sub_count, member_width, hidden_width)
    relative = member_rows - member_rows[:, :1, :]
    alive = jnp.arange(member_width, dtype=jnp.int32)[None, :] < sub_len[:, None]
    masked = jnp.where(alive[:, :, None], relative, 0.0)
    context = (jnp.sum(masked, axis=1) / sub_len[:, None].astype(jnp.float32)).astype(jnp.bfloat16)
    relative_bf = relative.astype(jnp.bfloat16)
    inner = jnp.einsum("smh,hk->smk", relative_bf, w_diff, preferred_element_type=jnp.float32)
    inner = inner + jnp.dot(context, w_ctx, preferred_element_type=jnp.float32)[:, None, :] + bias_e
    edge_hidden = jax.nn.relu(inner).astype(jnp.bfloat16)
    logits = jnp.einsum("smk,k->sm", edge_hidden, w_edge, preferred_element_type=jnp.float32)
    edge_scores = jnp.where(alive, jax.nn.sigmoid(logits), 0.0)
    slot_scores = scatter_sum(member_flat, edge_scores.reshape(sub_count * member_width), slot_total)
    slot_scores = slot_scores.reshape(device_total, capacity)
    returned = lax.all_to_all(
        slot_scores, ("grp", "shard"), split_axis=0, concat_axis=0, tiled=True
    )
    node_votes = scatter_sum(send_flat, returned.reshape(slot_total), nodes)
    return (node_hidden, confidence, edge_scores, node_votes)


def solution(mesh):
    return jax.shard_map(
        body,
        mesh=mesh,
        in_specs=(
            P(("grp", "shard"), None),
            P(("grp", "shard"), None),
            P(("grp", "shard"), None),
            P(("grp", "shard"), None, None),
            P(("grp", "shard"), None, None),
            P(("grp", "shard"), None),
            P(("grp", "shard")),
            P(),
            P(),
            P(),
            P(),
            P(),
            P(),
            P(),
            P(),
        ),
        out_specs=(
            P(("grp", "shard"), None),
            P(("grp", "shard")),
            P(("grp", "shard"), None),
            P(("grp", "shard")),
        ),
        check_vma=False,
    )
```

```python
import math

import jax
import jax.numpy as jnp
from jax import lax
from jax.experimental import pallas as pl
from jax.experimental.pallas import tpu as pltpu
from jax.sharding import PartitionSpec as P

TILE = 128


SUB = 8


def adjacency_kernel(slot_ref, coef_ref, out_ref, acc_ref):
    span = 256
    peers = out_ref.shape[1] // span
    sub_count = out_ref.shape[0] // SUB
    width = slot_ref.shape[1]
    row_hit = lax.broadcasted_iota(jnp.int32, (span, width), 0)
    lane_node = lax.broadcasted_iota(jnp.int32, (peers * SUB, width), 1) // (width // SUB)
    pair_row = lax.broadcasted_iota(jnp.int32, (peers * SUB, width), 0)
    pair_peer = pair_row // SUB
    pair_node = pair_row % SUB

    def one_sub(s, carry):
        slots = slot_ref[pl.ds(s, 1), :]
        coefs = coef_ref[pl.ds(s, 1), :]
        onehot = jnp.where(row_hit == slots % span, 1.0, 0.0).astype(jnp.bfloat16)
        picked = (pair_peer == slots // span) & (pair_node == lane_node)
        weights = jnp.where(picked, coefs, 0.0).astype(jnp.bfloat16)
        block = lax.dot_general(
            weights, onehot, (((1,), (1,)), ((), ())), preferred_element_type=jnp.float32
        )
        block = block.astype(jnp.bfloat16).astype(jnp.float32)
        rows = pl.ds(pl.multiple_of(s * SUB, SUB), SUB)
        for p in range(peers):
            acc_ref[rows, p * span:(p + 1) * span] = block[p * SUB:(p + 1) * SUB, :]
        return carry

    lax.fori_loop(0, sub_count, one_sub, 0)
    out_ref[...] = acc_ref[...].astype(out_ref.dtype)


def build_adjacency(slot_rows, coef_rows, nodes, columns):
    rows = 128
    subs = rows // SUB
    return pl.pallas_call(
        adjacency_kernel,
        grid=(nodes // rows,),
        in_specs=[
            pl.BlockSpec((subs, slot_rows.shape[1]), lambda b: (b, 0)),
            pl.BlockSpec((subs, coef_rows.shape[1]), lambda b: (b, 0)),
        ],
        out_specs=pl.BlockSpec((rows, columns), lambda b: (b, 0)),
        out_shape=jax.ShapeDtypeStruct((nodes, columns), jnp.bfloat16),
        scratch_shapes=[pltpu.VMEM((rows, columns), jnp.float32)],
    )(slot_rows, coef_rows)


def node_kernel(adj_ref, table_ref, self_ref, w_nbr_ref, out_ref):
    total = jnp.dot(adj_ref[...], table_ref[...], preferred_element_type=jnp.float32)
    pre = self_ref[...] + jnp.dot(total.astype(jnp.bfloat16), w_nbr_ref[...], preferred_element_type=jnp.float32)
    out_ref[...] = jnp.maximum(pre, 0.0).astype(out_ref.dtype)


def node_layer(adjacency, table, self_term, w_nbr):
    count, columns = adjacency.shape
    hidden = w_nbr.shape[1]
    rows = 128
    return pl.pallas_call(
        node_kernel,
        grid=(count // rows,),
        in_specs=[
            pl.BlockSpec((rows, columns), lambda b: (b, 0)),
            pl.BlockSpec(table.shape, lambda b: (0, 0)),
            pl.BlockSpec((rows, hidden), lambda b: (b, 0)),
            pl.BlockSpec(w_nbr.shape, lambda b: (0, 0)),
        ],
        out_specs=pl.BlockSpec((rows, hidden), lambda b: (b, 0)),
        out_shape=jax.ShapeDtypeStruct((count, hidden), jnp.bfloat16),
        compiler_params=pltpu.CompilerParams(vmem_limit_bytes=48 * 1024 * 1024),
    )(adjacency, table, self_term, w_nbr)


def edge_kernel(len_ref, rows_ref, member_ref, w_diff_ref, w_ctx_ref, bias_ref, w_edge_ref, scores_ref):
    slots = rows_ref.shape[0]
    subs, width = scores_ref.shape
    hidden = w_diff_ref.shape[1]
    chooser = jnp.where(
        member_ref[...] == lax.broadcasted_iota(jnp.int32, (subs * width, slots), 1), 1.0, 0.0
    ).astype(jnp.bfloat16)
    member_rows = jnp.dot(chooser, rows_ref[...], preferred_element_type=jnp.float32)
    for s in range(subs):
        block = member_rows[s * width:(s + 1) * width, :]
        relative = block - block[0:1, :]
        length = len_ref[s]
        alive = lax.broadcasted_iota(jnp.int32, (width, 1), 0) < length
        total = jnp.sum(jnp.where(alive, relative, 0.0), axis=0, keepdims=True)
        count = jnp.full((1, hidden), length, jnp.int32).astype(jnp.float32)
        context = jnp.broadcast_to((total / count).astype(jnp.bfloat16), (8, hidden))
        inner = (
            jnp.dot(relative.astype(jnp.bfloat16), w_diff_ref[...], preferred_element_type=jnp.float32)
            + jnp.dot(context, w_ctx_ref[...], preferred_element_type=jnp.float32)[0:1, :]
            + bias_ref[...]
        )
        edge_hidden = jnp.maximum(inner, 0.0).astype(jnp.bfloat16)
        logits = lax.dot_general(
            w_edge_ref[...], edge_hidden, (((1,), (1,)), ((), ())), preferred_element_type=jnp.float32
        )[0:1, :]
        live = lax.broadcasted_iota(jnp.int32, (1, width), 1) < length
        scores_ref[s:s + 1, :] = jnp.where(live, 1.0 / (1.0 + jnp.exp(-logits)), 0.0)


def edge_layer(sub_len, rows, member_flat, w_diff, w_ctx, bias, w_edge, subs, width):
    vmem = pl.BlockSpec(memory_space=pltpu.VMEM)
    hidden = w_diff.shape[1]
    return pl.pallas_call(
        edge_kernel,
        in_specs=[pl.BlockSpec(memory_space=pltpu.SMEM)] + [vmem] * 6,
        out_specs=vmem,
        out_shape=jax.ShapeDtypeStruct((subs, width), jnp.float32),
    )(
        sub_len,
        rows,
        member_flat.reshape(subs * width, 1),
        w_diff,
        w_ctx,
        bias.reshape(1, hidden),
        jnp.broadcast_to(w_edge.reshape(1, hidden), (8, hidden)),
    )


def select_matrix(indices, count, dtype):
    return (indices[:, None] == jnp.arange(count, dtype=jnp.int32)[None, :]).astype(dtype)


def scatter_sum(indices, values, count):
    hit = indices[:, None] == jnp.arange(count, dtype=jnp.int32)[None, :]
    return jnp.sum(jnp.where(hit, values[:, None], jnp.float32(0.0)), axis=0)


def body(
    embed,
    knn_slot,
    knn_weight,
    tile_list,
    send_rows,
    members,
    sub_len,
    w_self,
    w_nbr,
    bias_v,
    w_conf,
    w_diff,
    w_ctx,
    bias_e,
    w_edge,
):
    nodes = embed.shape[0]
    width = embed.shape[1]
    neighbour_count = knn_slot.shape[1]
    shard_count = lax.axis_size("shard")
    list_len = tile_list.shape[2]
    peer_span = list_len * TILE
    column_total = shard_count * peer_span
    embed_bf = embed.astype(jnp.bfloat16)
    weight_sum = jnp.sum(knn_weight, axis=1, keepdims=True)
    coeff_bf = (knn_weight / weight_sum).astype(jnp.bfloat16)
    sub_rows = nodes // SUB
    adjacency = build_adjacency(
        knn_slot.reshape(sub_rows, SUB * neighbour_count),
        coeff_bf.astype(jnp.float32).reshape(sub_rows, SUB * neighbour_count),
        nodes,
        column_total,
    )
    tile_count = nodes // TILE
    embed_tiles = embed_bf.reshape(tile_count, TILE, width)
    outgoing = embed_tiles.at[tile_list[0].reshape(shard_count * list_len)].get(mode="promise_in_bounds")
    outgoing = outgoing.reshape(shard_count, peer_span, width)
    provided = lax.all_to_all(outgoing, "shard", split_axis=0, concat_axis=0, tiled=True)
    provided = provided.reshape(column_total, width)
    send_flat = send_rows[0].reshape(send_rows.shape[1] * send_rows.shape[2])
    self_term = jnp.dot(embed_bf, w_self, preferred_element_type=jnp.float32) + bias_v
    send_chooser = select_matrix(send_flat, nodes, jnp.bfloat16)
    send_adjacency = jnp.dot(send_chooser, adjacency, preferred_element_type=jnp.float32).astype(jnp.bfloat16)
    send_embed = jnp.dot(send_chooser, embed_bf, preferred_element_type=jnp.float32).astype(jnp.bfloat16)
    send_self = jnp.dot(send_embed, w_self, preferred_element_type=jnp.float32) + bias_v
    outbound = node_layer(send_adjacency, provided, send_self, w_nbr)
    node_hidden = node_layer(adjacency, provided, self_term, w_nbr)
    confidence = jnp.dot(node_hidden, w_conf, preferred_element_type=jnp.float32)
    device_total = send_rows.shape[1]
    capacity = send_rows.shape[2]
    hidden_width = node_hidden.shape[1]
    slot_total = device_total * capacity
    outbound = outbound.reshape(device_total, capacity, hidden_width)
    received = lax.all_to_all(outbound, ("grp", "shard"), split_axis=0, concat_axis=0, tiled=True)
    received_rows = received.reshape(slot_total, hidden_width)
    sub_count = members.shape[0]
    member_width = members.shape[1]
    member_flat = members.reshape(sub_count * member_width)
    edge_scores = edge_layer(sub_len, received_rows, member_flat, w_diff, w_ctx, bias_e, w_edge, sub_count, member_width)
    slot_scores = scatter_sum(member_flat, edge_scores.reshape(sub_count * member_width), slot_total)
    slot_scores = slot_scores.reshape(device_total, capacity)
    returned = lax.all_to_all(
        slot_scores, ("grp", "shard"), split_axis=0, concat_axis=0, tiled=True
    )
    node_votes = scatter_sum(send_flat, returned.reshape(slot_total), nodes)
    return (node_hidden, confidence, edge_scores, node_votes)


def solution(mesh):
    return jax.shard_map(
        body,
        mesh=mesh,
        in_specs=(
            P(("grp", "shard"), None),
            P(("grp", "shard"), None),
            P(("grp", "shard"), None),
            P(("grp", "shard"), None, None),
            P(("grp", "shard"), None, None),
            P(("grp", "shard"), None),
            P(("grp", "shard")),
            P(),
            P(),
            P(),
            P(),
            P(),
            P(),
            P(),
            P(),
        ),
        out_specs=(
            P(("grp", "shard"), None),
            P(("grp", "shard")),
            P(("grp", "shard"), None),
            P(("grp", "shard")),
        ),
        check_vma=False,
    )
```

```python
import math

import jax
import jax.numpy as jnp
from jax import lax
from jax.experimental import pallas as pl
from jax.experimental.pallas import tpu as pltpu
from jax.sharding import PartitionSpec as P

TILE = 128


SUB = 8


def adjacency_kernel(slot_ref, coef_ref, out_ref, acc_ref):
    span = 256
    peers = out_ref.shape[1] // span
    sub_count = out_ref.shape[0] // SUB
    width = slot_ref.shape[1]
    row_hit = lax.broadcasted_iota(jnp.int32, (span, width), 0)
    lane_node = lax.broadcasted_iota(jnp.int32, (peers * SUB, width), 1) // (width // SUB)
    pair_row = lax.broadcasted_iota(jnp.int32, (peers * SUB, width), 0)
    pair_peer = pair_row // SUB
    pair_node = pair_row % SUB

    def one_sub(s, carry):
        slots = slot_ref[pl.ds(s, 1), :]
        coefs = coef_ref[pl.ds(s, 1), :]
        onehot = jnp.where(row_hit == slots % span, 1.0, 0.0).astype(jnp.bfloat16)
        picked = (pair_peer == slots // span) & (pair_node == lane_node)
        weights = jnp.where(picked, coefs, 0.0).astype(jnp.bfloat16)
        block = lax.dot_general(
            weights, onehot, (((1,), (1,)), ((), ())), preferred_element_type=jnp.float32
        )
        block = block.astype(jnp.bfloat16).astype(jnp.float32)
        rows = pl.ds(pl.multiple_of(s * SUB, SUB), SUB)
        for p in range(peers):
            acc_ref[rows, p * span:(p + 1) * span] = block[p * SUB:(p + 1) * SUB, :]
        return carry

    lax.fori_loop(0, sub_count, one_sub, 0)
    out_ref[...] = acc_ref[...].astype(out_ref.dtype)


def build_adjacency(slot_rows, coef_rows, nodes, columns):
    rows = 128
    subs = rows // SUB
    return pl.pallas_call(
        adjacency_kernel,
        grid=(nodes // rows,),
        in_specs=[
            pl.BlockSpec((subs, slot_rows.shape[1]), lambda b: (b, 0)),
            pl.BlockSpec((subs, coef_rows.shape[1]), lambda b: (b, 0)),
        ],
        out_specs=pl.BlockSpec((rows, columns), lambda b: (b, 0)),
        out_shape=jax.ShapeDtypeStruct((nodes, columns), jnp.bfloat16),
        scratch_shapes=[pltpu.VMEM((rows, columns), jnp.float32)],
    )(slot_rows, coef_rows)


def node_kernel(adj_ref, table_ref, embed_ref, w_self_ref, w_nbr_ref, bias_ref, send_ref, out_ref, outbound_ref, held_ref):
    b = pl.program_id(0)
    rows = out_ref.shape[0]
    total = jnp.dot(adj_ref[...], table_ref[...], preferred_element_type=jnp.float32)
    pre = (
        jnp.dot(embed_ref[...], w_self_ref[...], preferred_element_type=jnp.float32)
        + bias_ref[...]
        + jnp.dot(total.astype(jnp.bfloat16), w_nbr_ref[...], preferred_element_type=jnp.float32)
    )
    hidden = jnp.maximum(pre, 0.0).astype(out_ref.dtype)
    out_ref[...] = hidden
    held_ref[pl.ds(pl.multiple_of(b * rows, rows), rows), :] = hidden

    @pl.when(b == pl.num_programs(0) - 1)
    def _():
        nodes = held_ref.shape[0]
        chooser = jnp.where(
            send_ref[...] == lax.broadcasted_iota(jnp.int32, (send_ref.shape[0], nodes), 1), 1.0, 0.0
        ).astype(jnp.bfloat16)
        outbound_ref[...] = jnp.dot(chooser, held_ref[...], preferred_element_type=jnp.float32).astype(
            outbound_ref.dtype
        )


def node_layer(adjacency, table, embed_bf, w_self, w_nbr, bias, send_flat):
    nodes, width = embed_bf.shape
    hidden = w_self.shape[1]
    columns = adjacency.shape[1]
    rows = 128
    slots = send_flat.shape[0]
    return pl.pallas_call(
        node_kernel,
        grid=(nodes // rows,),
        in_specs=[
            pl.BlockSpec((rows, columns), lambda b: (b, 0)),
            pl.BlockSpec(table.shape, lambda b: (0, 0)),
            pl.BlockSpec((rows, width), lambda b: (b, 0)),
            pl.BlockSpec(w_self.shape, lambda b: (0, 0)),
            pl.BlockSpec(w_nbr.shape, lambda b: (0, 0)),
            pl.BlockSpec((1, hidden), lambda b: (0, 0)),
            pl.BlockSpec((slots, 1), lambda b: (0, 0)),
        ],
        out_specs=[
            pl.BlockSpec((rows, hidden), lambda b: (b, 0)),
            pl.BlockSpec((slots, hidden), lambda b: (0, 0)),
        ],
        out_shape=[
            jax.ShapeDtypeStruct((nodes, hidden), jnp.bfloat16),
            jax.ShapeDtypeStruct((slots, hidden), jnp.bfloat16),
        ],
        scratch_shapes=[pltpu.VMEM((nodes, hidden), jnp.bfloat16)],
        compiler_params=pltpu.CompilerParams(vmem_limit_bytes=48 * 1024 * 1024),
    )(adjacency, table, embed_bf, w_self, w_nbr, bias.reshape(1, hidden), send_flat.reshape(slots, 1))


def select_matrix(indices, count, dtype):
    return (indices[:, None] == jnp.arange(count, dtype=jnp.int32)[None, :]).astype(dtype)


def scatter_sum(indices, values, count):
    hit = indices[:, None] == jnp.arange(count, dtype=jnp.int32)[None, :]
    return jnp.sum(jnp.where(hit, values[:, None], jnp.float32(0.0)), axis=0)


def body(
    embed,
    knn_slot,
    knn_weight,
    tile_list,
    send_rows,
    members,
    sub_len,
    w_self,
    w_nbr,
    bias_v,
    w_conf,
    w_diff,
    w_ctx,
    bias_e,
    w_edge,
):
    nodes = embed.shape[0]
    width = embed.shape[1]
    neighbour_count = knn_slot.shape[1]
    shard_count = lax.axis_size("shard")
    list_len = tile_list.shape[2]
    peer_span = list_len * TILE
    column_total = shard_count * peer_span
    embed_bf = embed.astype(jnp.bfloat16)
    weight_sum = jnp.sum(knn_weight, axis=1, keepdims=True)
    coeff_bf = (knn_weight / weight_sum).astype(jnp.bfloat16)
    sub_rows = nodes // SUB
    adjacency = build_adjacency(
        knn_slot.reshape(sub_rows, SUB * neighbour_count),
        coeff_bf.astype(jnp.float32).reshape(sub_rows, SUB * neighbour_count),
        nodes,
        column_total,
    )
    tile_count = nodes // TILE
    embed_tiles = embed.reshape(tile_count, TILE, width)
    outgoing = embed_tiles.at[tile_list[0].reshape(shard_count * list_len)].get(mode="promise_in_bounds")
    outgoing = outgoing.astype(jnp.bfloat16)
    outgoing = outgoing.reshape(shard_count, peer_span, width)
    provided = lax.all_to_all(outgoing, "shard", split_axis=0, concat_axis=0, tiled=True)
    provided = provided.reshape(column_total, width)
    send_flat = send_rows[0].reshape(send_rows.shape[1] * send_rows.shape[2])
    node_hidden, outbound = node_layer(adjacency, provided, embed_bf, w_self, w_nbr, bias_v, send_flat)
    confidence = jnp.dot(node_hidden, w_conf, preferred_element_type=jnp.float32)
    device_total = send_rows.shape[1]
    capacity = send_rows.shape[2]
    hidden_width = node_hidden.shape[1]
    slot_total = device_total * capacity
    outbound = outbound.reshape(device_total, capacity, hidden_width)
    received = lax.all_to_all(outbound, ("grp", "shard"), split_axis=0, concat_axis=0, tiled=True)
    received_rows = received.reshape(slot_total, hidden_width)
    sub_count = members.shape[0]
    member_width = members.shape[1]
    member_flat = members.reshape(sub_count * member_width)
    member_chooser = select_matrix(member_flat, slot_total, jnp.bfloat16)
    member_rows = jnp.dot(member_chooser, received_rows, preferred_element_type=jnp.float32)
    member_rows = member_rows.reshape(sub_count, member_width, hidden_width)
    relative = member_rows - member_rows[:, :1, :]
    alive = jnp.arange(member_width, dtype=jnp.int32)[None, :] < sub_len[:, None]
    masked = jnp.where(alive[:, :, None], relative, 0.0)
    context = (jnp.sum(masked, axis=1) / sub_len[:, None].astype(jnp.float32)).astype(jnp.bfloat16)
    relative_bf = relative.astype(jnp.bfloat16)
    inner = jnp.einsum("smh,hk->smk", relative_bf, w_diff, preferred_element_type=jnp.float32)
    inner = inner + jnp.dot(context, w_ctx, preferred_element_type=jnp.float32)[:, None, :] + bias_e
    edge_hidden = jax.nn.relu(inner).astype(jnp.bfloat16)
    logits = jnp.einsum("smk,k->sm", edge_hidden, w_edge, preferred_element_type=jnp.float32)
    edge_scores = jnp.where(alive, jax.nn.sigmoid(logits), 0.0)
    slot_scores = scatter_sum(member_flat, edge_scores.reshape(sub_count * member_width), slot_total)
    slot_scores = slot_scores.reshape(device_total, capacity)
    returned = lax.all_to_all(
        slot_scores, ("grp", "shard"), split_axis=0, concat_axis=0, tiled=True
    )
    node_votes = scatter_sum(send_flat, returned.reshape(slot_total), nodes)
    return (node_hidden, confidence, edge_scores, node_votes)


def solution(mesh):
    return jax.shard_map(
        body,
        mesh=mesh,
        in_specs=(
            P(("grp", "shard"), None),
            P(("grp", "shard"), None),
            P(("grp", "shard"), None),
            P(("grp", "shard"), None, None),
            P(("grp", "shard"), None, None),
            P(("grp", "shard"), None),
            P(("grp", "shard")),
            P(),
            P(),
            P(),
            P(),
            P(),
            P(),
            P(),
            P(),
        ),
        out_specs=(
            P(("grp", "shard"), None),
            P(("grp", "shard")),
            P(("grp", "shard"), None),
            P(("grp", "shard")),
        ),
        check_vma=False,
    )
```

```python
import math

import jax
import jax.numpy as jnp
from jax import lax
from jax.experimental import pallas as pl
from jax.experimental.pallas import tpu as pltpu
from jax.sharding import PartitionSpec as P

TILE = 128


SUB = 8


def adjacency_kernel(slot_ref, coef_ref, out_ref, acc_ref):
    span = 256
    peers = out_ref.shape[1] // span
    sub_count = out_ref.shape[0] // SUB
    width = slot_ref.shape[1]
    row_hit = lax.broadcasted_iota(jnp.int32, (span, width), 0)
    lane_node = lax.broadcasted_iota(jnp.int32, (peers * SUB, width), 1) // (width // SUB)
    pair_row = lax.broadcasted_iota(jnp.int32, (peers * SUB, width), 0)
    pair_peer = pair_row // SUB
    pair_node = pair_row % SUB

    def one_sub(s, carry):
        slots = slot_ref[pl.ds(s, 1), :]
        coefs = coef_ref[pl.ds(s, 1), :]
        onehot = jnp.where(row_hit == slots % span, 1.0, 0.0).astype(jnp.bfloat16)
        picked = (pair_peer == slots // span) & (pair_node == lane_node)
        weights = jnp.where(picked, coefs, 0.0).astype(jnp.bfloat16)
        block = lax.dot_general(
            weights, onehot, (((1,), (1,)), ((), ())), preferred_element_type=jnp.float32
        )
        block = block.astype(jnp.bfloat16).astype(jnp.float32)
        rows = pl.ds(pl.multiple_of(s * SUB, SUB), SUB)
        for p in range(peers):
            acc_ref[rows, p * span:(p + 1) * span] = block[p * SUB:(p + 1) * SUB, :]
        return carry

    lax.fori_loop(0, sub_count, one_sub, 0)
    out_ref[...] = acc_ref[...].astype(out_ref.dtype)


def build_adjacency(slot_rows, coef_rows, nodes, columns):
    rows = 128
    subs = rows // SUB
    return pl.pallas_call(
        adjacency_kernel,
        grid=(nodes // rows,),
        in_specs=[
            pl.BlockSpec((subs, slot_rows.shape[1]), lambda b: (b, 0)),
            pl.BlockSpec((subs, coef_rows.shape[1]), lambda b: (b, 0)),
        ],
        out_specs=pl.BlockSpec((rows, columns), lambda b: (b, 0)),
        out_shape=jax.ShapeDtypeStruct((nodes, columns), jnp.bfloat16),
        scratch_shapes=[pltpu.VMEM((rows, columns), jnp.float32)],
    )(slot_rows, coef_rows)


def node_kernel(adj_ref, table_ref, self_ref, w_nbr_ref, send_ref, out_ref, outbound_ref, held_ref):
    b = pl.program_id(0)
    rows = out_ref.shape[0]
    total = jnp.dot(adj_ref[...], table_ref[...], preferred_element_type=jnp.float32)
    pre = self_ref[...] + jnp.dot(total.astype(jnp.bfloat16), w_nbr_ref[...], preferred_element_type=jnp.float32)
    hidden = jnp.maximum(pre, 0.0).astype(out_ref.dtype)
    out_ref[...] = hidden
    held_ref[pl.ds(pl.multiple_of(b * rows, rows), rows), :] = hidden

    @pl.when(b == pl.num_programs(0) - 1)
    def _():
        nodes = held_ref.shape[0]
        chooser = jnp.where(
            send_ref[...] == lax.broadcasted_iota(jnp.int32, (send_ref.shape[0], nodes), 1), 1.0, 0.0
        ).astype(jnp.bfloat16)
        outbound_ref[...] = jnp.dot(chooser, held_ref[...], preferred_element_type=jnp.float32).astype(
            outbound_ref.dtype
        )


def node_layer(adjacency, table, self_term, w_nbr, send_flat):
    nodes, hidden = self_term.shape
    columns = adjacency.shape[1]
    rows = 128
    slots = send_flat.shape[0]
    return pl.pallas_call(
        node_kernel,
        grid=(nodes // rows,),
        in_specs=[
            pl.BlockSpec((rows, columns), lambda b: (b, 0)),
            pl.BlockSpec(table.shape, lambda b: (0, 0)),
            pl.BlockSpec((rows, hidden), lambda b: (b, 0)),
            pl.BlockSpec(w_nbr.shape, lambda b: (0, 0)),
            pl.BlockSpec((slots, 1), lambda b: (0, 0)),
        ],
        out_specs=[
            pl.BlockSpec((rows, hidden), lambda b: (b, 0)),
            pl.BlockSpec((slots, hidden), lambda b: (0, 0)),
        ],
        out_shape=[
            jax.ShapeDtypeStruct((nodes, hidden), jnp.bfloat16),
            jax.ShapeDtypeStruct((slots, hidden), jnp.bfloat16),
        ],
        scratch_shapes=[pltpu.VMEM((nodes, hidden), jnp.bfloat16)],
        compiler_params=pltpu.CompilerParams(vmem_limit_bytes=48 * 1024 * 1024),
    )(adjacency, table, self_term, w_nbr, send_flat.reshape(slots, 1))


def select_matrix(indices, count, dtype):
    return (indices[:, None] == jnp.arange(count, dtype=jnp.int32)[None, :]).astype(dtype)


def scatter_sum(indices, values, count):
    hit = indices[:, None] == jnp.arange(count, dtype=jnp.int32)[None, :]
    return jnp.sum(jnp.where(hit, values[:, None], jnp.float32(0.0)), axis=0)


def body(
    embed,
    knn_slot,
    knn_weight,
    tile_list,
    send_rows,
    members,
    sub_len,
    w_self,
    w_nbr,
    bias_v,
    w_conf,
    w_diff,
    w_ctx,
    bias_e,
    w_edge,
):
    nodes = embed.shape[0]
    width = embed.shape[1]
    neighbour_count = knn_slot.shape[1]
    shard_count = lax.axis_size("shard")
    list_len = tile_list.shape[2]
    peer_span = list_len * TILE
    column_total = shard_count * peer_span
    embed_bf = embed.astype(jnp.bfloat16)
    weight_sum = jnp.sum(knn_weight, axis=1, keepdims=True)
    coeff_bf = (knn_weight / weight_sum).astype(jnp.bfloat16)
    sub_rows = nodes // SUB
    adjacency = build_adjacency(
        knn_slot.reshape(sub_rows, SUB * neighbour_count),
        coeff_bf.astype(jnp.float32).reshape(sub_rows, SUB * neighbour_count),
        nodes,
        column_total,
    )
    tile_count = nodes // TILE
    embed_tiles = embed.reshape(tile_count, TILE, width)
    outgoing = embed_tiles.at[tile_list[0].reshape(shard_count * list_len)].get(mode="promise_in_bounds")
    outgoing = outgoing.astype(jnp.bfloat16)
    outgoing = outgoing.reshape(shard_count, peer_span, width)
    provided = lax.all_to_all(outgoing, "shard", split_axis=0, concat_axis=0, tiled=True)
    provided = provided.reshape(column_total, width)
    send_flat = send_rows[0].reshape(send_rows.shape[1] * send_rows.shape[2])
    self_term = jnp.dot(embed_bf, w_self, preferred_element_type=jnp.float32) + bias_v
    node_hidden, outbound = node_layer(adjacency, provided, self_term, w_nbr, send_flat)
    confidence = jnp.dot(node_hidden, w_conf, preferred_element_type=jnp.float32)
    device_total = send_rows.shape[1]
    capacity = send_rows.shape[2]
    hidden_width = node_hidden.shape[1]
    slot_total = device_total * capacity
    outbound = outbound.reshape(device_total, capacity, hidden_width)
    received = lax.all_to_all(outbound, ("grp", "shard"), split_axis=0, concat_axis=0, tiled=True)
    received_rows = received.reshape(slot_total, hidden_width)
    sub_count = members.shape[0]
    member_width = members.shape[1]
    member_flat = members.reshape(sub_count * member_width)
    member_chooser = select_matrix(member_flat, slot_total, jnp.bfloat16)
    member_rows = jnp.dot(member_chooser, received_rows, preferred_element_type=jnp.float32)
    member_rows = member_rows.reshape(sub_count, member_width, hidden_width)
    relative = member_rows - member_rows[:, :1, :]
    alive = jnp.arange(member_width, dtype=jnp.int32)[None, :] < sub_len[:, None]
    masked = jnp.where(alive[:, :, None], relative, 0.0)
    context = (jnp.sum(masked, axis=1) / sub_len[:, None].astype(jnp.float32)).astype(jnp.bfloat16)
    relative_bf = relative.astype(jnp.bfloat16)
    inner = jnp.einsum("smh,hk->smk", relative_bf, w_diff, preferred_element_type=jnp.float32)
    inner = inner + jnp.dot(context, w_ctx, preferred_element_type=jnp.float32)[:, None, :] + bias_e
    edge_hidden = jax.nn.relu(inner).astype(jnp.bfloat16)
    logits = jnp.einsum("smk,k->sm", edge_hidden, w_edge, preferred_element_type=jnp.float32)
    edge_scores = jnp.where(alive, jax.nn.sigmoid(logits), 0.0)
    slot_scores = scatter_sum(member_flat, edge_scores.reshape(sub_count * member_width), slot_total)
    slot_scores = slot_scores.reshape(device_total, capacity)
    returned = lax.all_to_all(
        slot_scores, ("grp", "shard"), split_axis=0, concat_axis=0, tiled=True
    )
    node_votes = scatter_sum(send_flat, returned.reshape(slot_total), nodes)
    return (node_hidden, confidence, edge_scores, node_votes)


def solution(mesh):
    return jax.shard_map(
        body,
        mesh=mesh,
        in_specs=(
            P(("grp", "shard"), None),
            P(("grp", "shard"), None),
            P(("grp", "shard"), None),
            P(("grp", "shard"), None, None),
            P(("grp", "shard"), None, None),
            P(("grp", "shard"), None),
            P(("grp", "shard")),
            P(),
            P(),
            P(),
            P(),
            P(),
            P(),
            P(),
            P(),
        ),
        out_specs=(
            P(("grp", "shard"), None),
            P(("grp", "shard")),
            P(("grp", "shard"), None),
            P(("grp", "shard")),
        ),
        check_vma=False,
    )
```

```python
import math

import jax
import jax.numpy as jnp
from jax import lax
from jax.experimental import pallas as pl
from jax.experimental.pallas import tpu as pltpu
from jax.sharding import PartitionSpec as P

TILE = 128


SUB = 8


def adjacency_kernel(slot_ref, coef_ref, out_ref, acc_ref):
    span = 256
    peers = out_ref.shape[1] // span
    sub_count = out_ref.shape[0] // SUB
    width = slot_ref.shape[1]
    row_hit = lax.broadcasted_iota(jnp.int32, (span, width), 0)
    lane_node = lax.broadcasted_iota(jnp.int32, (peers * SUB, width), 1) // (width // SUB)
    pair_row = lax.broadcasted_iota(jnp.int32, (peers * SUB, width), 0)
    pair_peer = pair_row // SUB
    pair_node = pair_row % SUB

    def one_sub(s, carry):
        slots = slot_ref[pl.ds(s, 1), :]
        coefs = coef_ref[pl.ds(s, 1), :]
        onehot = jnp.where(row_hit == slots % span, 1.0, 0.0).astype(jnp.bfloat16)
        picked = (pair_peer == slots // span) & (pair_node == lane_node)
        weights = jnp.where(picked, coefs, 0.0).astype(jnp.bfloat16)
        block = lax.dot_general(
            weights, onehot, (((1,), (1,)), ((), ())), preferred_element_type=jnp.float32
        )
        block = block.astype(jnp.bfloat16).astype(jnp.float32)
        rows = pl.ds(pl.multiple_of(s * SUB, SUB), SUB)
        for p in range(peers):
            acc_ref[rows, p * span:(p + 1) * span] = block[p * SUB:(p + 1) * SUB, :]
        return carry

    lax.fori_loop(0, sub_count, one_sub, 0)
    out_ref[...] = acc_ref[...].astype(out_ref.dtype)


def build_adjacency(slot_rows, coef_rows, nodes, columns):
    rows = 128
    subs = rows // SUB
    return pl.pallas_call(
        adjacency_kernel,
        grid=(nodes // rows,),
        in_specs=[
            pl.BlockSpec((subs, slot_rows.shape[1]), lambda b: (b, 0)),
            pl.BlockSpec((subs, coef_rows.shape[1]), lambda b: (b, 0)),
        ],
        out_specs=pl.BlockSpec((rows, columns), lambda b: (b, 0)),
        out_shape=jax.ShapeDtypeStruct((nodes, columns), jnp.bfloat16),
        scratch_shapes=[pltpu.VMEM((rows, columns), jnp.float32)],
    )(slot_rows, coef_rows)


def node_kernel(adj_ref, table_ref, embed_ref, w_self_ref, w_nbr_ref, bias_ref, send_ref, out_ref, outbound_ref, held_ref):
    b = pl.program_id(0)
    rows = out_ref.shape[0]
    total = jnp.dot(adj_ref[...], table_ref[...], preferred_element_type=jnp.float32)
    pre = (
        jnp.dot(embed_ref[...], w_self_ref[...], preferred_element_type=jnp.float32)
        + bias_ref[...]
        + jnp.dot(total.astype(jnp.bfloat16), w_nbr_ref[...], preferred_element_type=jnp.float32)
    )
    hidden = jnp.maximum(pre, 0.0).astype(out_ref.dtype)
    out_ref[...] = hidden
    held_ref[pl.ds(pl.multiple_of(b * rows, rows), rows), :] = hidden

    @pl.when(b == pl.num_programs(0) - 1)
    def _():
        nodes = held_ref.shape[0]
        chooser = jnp.where(
            send_ref[...] == lax.broadcasted_iota(jnp.int32, (send_ref.shape[0], nodes), 1), 1.0, 0.0
        ).astype(jnp.bfloat16)
        outbound_ref[...] = jnp.dot(chooser, held_ref[...], preferred_element_type=jnp.float32).astype(
            outbound_ref.dtype
        )


def node_layer(adjacency, table, embed_bf, w_self, w_nbr, bias, send_flat):
    nodes, width = embed_bf.shape
    hidden = w_self.shape[1]
    columns = adjacency.shape[1]
    rows = 256
    slots = send_flat.shape[0]
    return pl.pallas_call(
        node_kernel,
        grid=(nodes // rows,),
        in_specs=[
            pl.BlockSpec((rows, columns), lambda b: (b, 0)),
            pl.BlockSpec(table.shape, lambda b: (0, 0)),
            pl.BlockSpec((rows, width), lambda b: (b, 0)),
            pl.BlockSpec(w_self.shape, lambda b: (0, 0)),
            pl.BlockSpec(w_nbr.shape, lambda b: (0, 0)),
            pl.BlockSpec((1, hidden), lambda b: (0, 0)),
            pl.BlockSpec((slots, 1), lambda b: (0, 0)),
        ],
        out_specs=[
            pl.BlockSpec((rows, hidden), lambda b: (b, 0)),
            pl.BlockSpec((slots, hidden), lambda b: (0, 0)),
        ],
        out_shape=[
            jax.ShapeDtypeStruct((nodes, hidden), jnp.bfloat16),
            jax.ShapeDtypeStruct((slots, hidden), jnp.bfloat16),
        ],
        scratch_shapes=[pltpu.VMEM((nodes, hidden), jnp.bfloat16)],
        compiler_params=pltpu.CompilerParams(vmem_limit_bytes=48 * 1024 * 1024),
    )(adjacency, table, embed_bf, w_self, w_nbr, bias.reshape(1, hidden), send_flat.reshape(slots, 1))


def select_matrix(indices, count, dtype):
    return (indices[:, None] == jnp.arange(count, dtype=jnp.int32)[None, :]).astype(dtype)


def scatter_sum(indices, values, count):
    hit = indices[:, None] == jnp.arange(count, dtype=jnp.int32)[None, :]
    return jnp.sum(jnp.where(hit, values[:, None], jnp.float32(0.0)), axis=0)


def body(
    embed,
    knn_slot,
    knn_weight,
    tile_list,
    send_rows,
    members,
    sub_len,
    w_self,
    w_nbr,
    bias_v,
    w_conf,
    w_diff,
    w_ctx,
    bias_e,
    w_edge,
):
    nodes = embed.shape[0]
    width = embed.shape[1]
    neighbour_count = knn_slot.shape[1]
    shard_count = lax.axis_size("shard")
    list_len = tile_list.shape[2]
    peer_span = list_len * TILE
    column_total = shard_count * peer_span
    embed_bf = embed.astype(jnp.bfloat16)
    weight_sum = jnp.sum(knn_weight, axis=1, keepdims=True)
    coeff_bf = (knn_weight / weight_sum).astype(jnp.bfloat16)
    sub_rows = nodes // SUB
    adjacency = build_adjacency(
        knn_slot.reshape(sub_rows, SUB * neighbour_count),
        coeff_bf.astype(jnp.float32).reshape(sub_rows, SUB * neighbour_count),
        nodes,
        column_total,
    )
    tile_count = nodes // TILE
    embed_tiles = embed.reshape(tile_count, TILE, width)
    outgoing = embed_tiles.at[tile_list[0].reshape(shard_count * list_len)].get(mode="promise_in_bounds")
    outgoing = outgoing.astype(jnp.bfloat16)
    outgoing = outgoing.reshape(shard_count, peer_span, width)
    provided = lax.all_to_all(outgoing, "shard", split_axis=0, concat_axis=0, tiled=True)
    provided = provided.reshape(column_total, width)
    send_flat = send_rows[0].reshape(send_rows.shape[1] * send_rows.shape[2])
    node_hidden, outbound = node_layer(adjacency, provided, embed_bf, w_self, w_nbr, bias_v, send_flat)
    confidence = jnp.dot(node_hidden, w_conf, preferred_element_type=jnp.float32)
    device_total = send_rows.shape[1]
    capacity = send_rows.shape[2]
    hidden_width = node_hidden.shape[1]
    slot_total = device_total * capacity
    outbound = outbound.reshape(device_total, capacity, hidden_width)
    received = lax.all_to_all(outbound, ("grp", "shard"), split_axis=0, concat_axis=0, tiled=True)
    received_rows = received.reshape(slot_total, hidden_width)
    sub_count = members.shape[0]
    member_width = members.shape[1]
    member_flat = members.reshape(sub_count * member_width)
    member_chooser = select_matrix(member_flat, slot_total, jnp.bfloat16)
    member_rows = jnp.dot(member_chooser, received_rows, preferred_element_type=jnp.float32)
    member_rows = member_rows.reshape(sub_count, member_width, hidden_width)
    relative = member_rows - member_rows[:, :1, :]
    alive = jnp.arange(member_width, dtype=jnp.int32)[None, :] < sub_len[:, None]
    masked = jnp.where(alive[:, :, None], relative, 0.0)
    context = (jnp.sum(masked, axis=1) / sub_len[:, None].astype(jnp.float32)).astype(jnp.bfloat16)
    relative_bf = relative.astype(jnp.bfloat16)
    inner = jnp.einsum("smh,hk->smk", relative_bf, w_diff, preferred_element_type=jnp.float32)
    inner = inner + jnp.dot(context, w_ctx, preferred_element_type=jnp.float32)[:, None, :] + bias_e
    edge_hidden = jax.nn.relu(inner).astype(jnp.bfloat16)
    logits = jnp.einsum("smk,k->sm", edge_hidden, w_edge, preferred_element_type=jnp.float32)
    edge_scores = jnp.where(alive, jax.nn.sigmoid(logits), 0.0)
    slot_scores = scatter_sum(member_flat, edge_scores.reshape(sub_count * member_width), slot_total)
    slot_scores = slot_scores.reshape(device_total, capacity)
    returned = lax.all_to_all(
        slot_scores, ("grp", "shard"), split_axis=0, concat_axis=0, tiled=True
    )
    node_votes = scatter_sum(send_flat, returned.reshape(slot_total), nodes)
    return (node_hidden, confidence, edge_scores, node_votes)


def solution(mesh):
    return jax.shard_map(
        body,
        mesh=mesh,
        in_specs=(
            P(("grp", "shard"), None),
            P(("grp", "shard"), None),
            P(("grp", "shard"), None),
            P(("grp", "shard"), None, None),
            P(("grp", "shard"), None, None),
            P(("grp", "shard"), None),
            P(("grp", "shard")),
            P(),
            P(),
            P(),
            P(),
            P(),
            P(),
            P(),
            P(),
        ),
        out_specs=(
            P(("grp", "shard"), None),
            P(("grp", "shard")),
            P(("grp", "shard"), None),
            P(("grp", "shard")),
        ),
        check_vma=False,
    )
```

```python
import math

import jax
import jax.numpy as jnp
from jax import lax
from jax.experimental import pallas as pl
from jax.experimental.pallas import tpu as pltpu
from jax.sharding import PartitionSpec as P

TILE = 128


SUB = 8


def adjacency_kernel(slot_ref, coef_ref, out_ref, acc_ref):
    span = 256
    peers = out_ref.shape[1] // span
    sub_count = out_ref.shape[0] // SUB
    width = slot_ref.shape[1]
    row_hit = lax.broadcasted_iota(jnp.int32, (span, width), 0)
    lane_node = lax.broadcasted_iota(jnp.int32, (peers * SUB, width), 1) // (width // SUB)
    pair_row = lax.broadcasted_iota(jnp.int32, (peers * SUB, width), 0)
    pair_peer = pair_row // SUB
    pair_node = pair_row % SUB

    def one_sub(s, carry):
        slots = slot_ref[pl.ds(s, 1), :]
        coefs = coef_ref[pl.ds(s, 1), :]
        onehot = jnp.where(row_hit == slots % span, 1.0, 0.0).astype(jnp.bfloat16)
        picked = (pair_peer == slots // span) & (pair_node == lane_node)
        weights = jnp.where(picked, coefs, 0.0).astype(jnp.bfloat16)
        block = lax.dot_general(
            weights, onehot, (((1,), (1,)), ((), ())), preferred_element_type=jnp.float32
        )
        block = block.astype(jnp.bfloat16).astype(jnp.float32)
        rows = pl.ds(pl.multiple_of(s * SUB, SUB), SUB)
        for p in range(peers):
            acc_ref[rows, p * span:(p + 1) * span] = block[p * SUB:(p + 1) * SUB, :]
        return carry

    lax.fori_loop(0, sub_count, one_sub, 0)
    out_ref[...] = acc_ref[...].astype(out_ref.dtype)


def build_adjacency(slot_rows, coef_rows, nodes, columns):
    rows = 128
    subs = rows // SUB
    return pl.pallas_call(
        adjacency_kernel,
        grid=(nodes // rows,),
        in_specs=[
            pl.BlockSpec((subs, slot_rows.shape[1]), lambda b: (b, 0)),
            pl.BlockSpec((subs, coef_rows.shape[1]), lambda b: (b, 0)),
        ],
        out_specs=pl.BlockSpec((rows, columns), lambda b: (b, 0)),
        out_shape=jax.ShapeDtypeStruct((nodes, columns), jnp.bfloat16),
        scratch_shapes=[pltpu.VMEM((rows, columns), jnp.float32)],
    )(slot_rows, coef_rows)


def node_kernel(adj_ref, table_ref, embed_ref, w_self_ref, w_nbr_ref, bias_ref, send_ref, out_ref, outbound_ref, held_ref):
    b = pl.program_id(0)
    rows = out_ref.shape[0]
    total = jnp.dot(adj_ref[...], table_ref[...], preferred_element_type=jnp.float32)
    pre = (
        jnp.dot(embed_ref[...], w_self_ref[...], preferred_element_type=jnp.float32)
        + bias_ref[...]
        + jnp.dot(total.astype(jnp.bfloat16), w_nbr_ref[...], preferred_element_type=jnp.float32)
    )
    hidden = jnp.maximum(pre, 0.0).astype(out_ref.dtype)
    out_ref[...] = hidden
    held_ref[pl.ds(pl.multiple_of(b * rows, rows), rows), :] = hidden

    @pl.when(b == pl.num_programs(0) - 1)
    def _():
        nodes = held_ref.shape[0]
        chooser = jnp.where(
            send_ref[...] == lax.broadcasted_iota(jnp.int32, (send_ref.shape[0], nodes), 1), 1.0, 0.0
        ).astype(jnp.bfloat16)
        outbound_ref[...] = jnp.dot(chooser, held_ref[...], preferred_element_type=jnp.float32).astype(
            outbound_ref.dtype
        )


def node_layer(adjacency, table, embed_bf, w_self, w_nbr, bias, send_flat):
    nodes, width = embed_bf.shape
    hidden = w_self.shape[1]
    columns = adjacency.shape[1]
    rows = 512
    slots = send_flat.shape[0]
    return pl.pallas_call(
        node_kernel,
        grid=(nodes // rows,),
        in_specs=[
            pl.BlockSpec((rows, columns), lambda b: (b, 0)),
            pl.BlockSpec(table.shape, lambda b: (0, 0)),
            pl.BlockSpec((rows, width), lambda b: (b, 0)),
            pl.BlockSpec(w_self.shape, lambda b: (0, 0)),
            pl.BlockSpec(w_nbr.shape, lambda b: (0, 0)),
            pl.BlockSpec((1, hidden), lambda b: (0, 0)),
            pl.BlockSpec((slots, 1), lambda b: (0, 0)),
        ],
        out_specs=[
            pl.BlockSpec((rows, hidden), lambda b: (b, 0)),
            pl.BlockSpec((slots, hidden), lambda b: (0, 0)),
        ],
        out_shape=[
            jax.ShapeDtypeStruct((nodes, hidden), jnp.bfloat16),
            jax.ShapeDtypeStruct((slots, hidden), jnp.bfloat16),
        ],
        scratch_shapes=[pltpu.VMEM((nodes, hidden), jnp.bfloat16)],
        compiler_params=pltpu.CompilerParams(vmem_limit_bytes=48 * 1024 * 1024),
    )(adjacency, table, embed_bf, w_self, w_nbr, bias.reshape(1, hidden), send_flat.reshape(slots, 1))


def select_matrix(indices, count, dtype):
    return (indices[:, None] == jnp.arange(count, dtype=jnp.int32)[None, :]).astype(dtype)


def scatter_sum(indices, values, count):
    hit = indices[:, None] == jnp.arange(count, dtype=jnp.int32)[None, :]
    return jnp.sum(jnp.where(hit, values[:, None], jnp.float32(0.0)), axis=0)


def body(
    embed,
    knn_slot,
    knn_weight,
    tile_list,
    send_rows,
    members,
    sub_len,
    w_self,
    w_nbr,
    bias_v,
    w_conf,
    w_diff,
    w_ctx,
    bias_e,
    w_edge,
):
    nodes = embed.shape[0]
    width = embed.shape[1]
    neighbour_count = knn_slot.shape[1]
    shard_count = lax.axis_size("shard")
    list_len = tile_list.shape[2]
    peer_span = list_len * TILE
    column_total = shard_count * peer_span
    embed_bf = embed.astype(jnp.bfloat16)
    weight_sum = jnp.sum(knn_weight, axis=1, keepdims=True)
    coeff_bf = (knn_weight / weight_sum).astype(jnp.bfloat16)
    sub_rows = nodes // SUB
    adjacency = build_adjacency(
        knn_slot.reshape(sub_rows, SUB * neighbour_count),
        coeff_bf.astype(jnp.float32).reshape(sub_rows, SUB * neighbour_count),
        nodes,
        column_total,
    )
    tile_count = nodes // TILE
    embed_tiles = embed.reshape(tile_count, TILE, width)
    outgoing = embed_tiles.at[tile_list[0].reshape(shard_count * list_len)].get(mode="promise_in_bounds")
    outgoing = outgoing.astype(jnp.bfloat16)
    outgoing = outgoing.reshape(shard_count, peer_span, width)
    provided = lax.all_to_all(outgoing, "shard", split_axis=0, concat_axis=0, tiled=True)
    provided = provided.reshape(column_total, width)
    send_flat = send_rows[0].reshape(send_rows.shape[1] * send_rows.shape[2])
    node_hidden, outbound = node_layer(adjacency, provided, embed_bf, w_self, w_nbr, bias_v, send_flat)
    confidence = jnp.dot(node_hidden, w_conf, preferred_element_type=jnp.float32)
    device_total = send_rows.shape[1]
    capacity = send_rows.shape[2]
    hidden_width = node_hidden.shape[1]
    slot_total = device_total * capacity
    outbound = outbound.reshape(device_total, capacity, hidden_width)
    received = lax.all_to_all(outbound, ("grp", "shard"), split_axis=0, concat_axis=0, tiled=True)
    received_rows = received.reshape(slot_total, hidden_width)
    sub_count = members.shape[0]
    member_width = members.shape[1]
    member_flat = members.reshape(sub_count * member_width)
    member_chooser = select_matrix(member_flat, slot_total, jnp.bfloat16)
    member_rows = jnp.dot(member_chooser, received_rows, preferred_element_type=jnp.float32)
    member_rows = member_rows.reshape(sub_count, member_width, hidden_width)
    relative = member_rows - member_rows[:, :1, :]
    alive = jnp.arange(member_width, dtype=jnp.int32)[None, :] < sub_len[:, None]
    masked = jnp.where(alive[:, :, None], relative, 0.0)
    context = (jnp.sum(masked, axis=1) / sub_len[:, None].astype(jnp.float32)).astype(jnp.bfloat16)
    relative_bf = relative.astype(jnp.bfloat16)
    inner = jnp.einsum("smh,hk->smk", relative_bf, w_diff, preferred_element_type=jnp.float32)
    inner = inner + jnp.dot(context, w_ctx, preferred_element_type=jnp.float32)[:, None, :] + bias_e
    edge_hidden = jax.nn.relu(inner).astype(jnp.bfloat16)
    logits = jnp.einsum("smk,k->sm", edge_hidden, w_edge, preferred_element_type=jnp.float32)
    edge_scores = jnp.where(alive, jax.nn.sigmoid(logits), 0.0)
    slot_scores = scatter_sum(member_flat, edge_scores.reshape(sub_count * member_width), slot_total)
    slot_scores = slot_scores.reshape(device_total, capacity)
    returned = lax.all_to_all(
        slot_scores, ("grp", "shard"), split_axis=0, concat_axis=0, tiled=True
    )
    node_votes = scatter_sum(send_flat, returned.reshape(slot_total), nodes)
    return (node_hidden, confidence, edge_scores, node_votes)


def solution(mesh):
    return jax.shard_map(
        body,
        mesh=mesh,
        in_specs=(
            P(("grp", "shard"), None),
            P(("grp", "shard"), None),
            P(("grp", "shard"), None),
            P(("grp", "shard"), None, None),
            P(("grp", "shard"), None, None),
            P(("grp", "shard"), None),
            P(("grp", "shard")),
            P(),
            P(),
            P(),
            P(),
            P(),
            P(),
            P(),
            P(),
        ),
        out_specs=(
            P(("grp", "shard"), None),
            P(("grp", "shard")),
            P(("grp", "shard"), None),
            P(("grp", "shard")),
        ),
        check_vma=False,
    )
```

```python
import math

import jax
import jax.numpy as jnp
from jax import lax
from jax.experimental import pallas as pl
from jax.experimental.pallas import tpu as pltpu
from jax.sharding import PartitionSpec as P

TILE = 128


SUB = 8


def adjacency_kernel(slot_ref, coef_ref, out_ref, acc_ref):
    span = 256
    peers = out_ref.shape[1] // span
    sub_count = out_ref.shape[0] // SUB
    width = slot_ref.shape[1]
    row_hit = lax.broadcasted_iota(jnp.int32, (span, width), 0)
    lane_node = lax.broadcasted_iota(jnp.int32, (peers * SUB, width), 1) // (width // SUB)
    pair_row = lax.broadcasted_iota(jnp.int32, (peers * SUB, width), 0)
    pair_peer = pair_row // SUB
    pair_node = pair_row % SUB

    def one_sub(s, carry):
        slots = slot_ref[pl.ds(s, 1), :]
        coefs = coef_ref[pl.ds(s, 1), :]
        onehot = jnp.where(row_hit == slots % span, 1.0, 0.0).astype(jnp.bfloat16)
        picked = (pair_peer == slots // span) & (pair_node == lane_node)
        weights = jnp.where(picked, coefs, 0.0).astype(jnp.bfloat16)
        block = lax.dot_general(
            weights, onehot, (((1,), (1,)), ((), ())), preferred_element_type=jnp.float32
        )
        block = block.astype(jnp.bfloat16).astype(jnp.float32)
        rows = pl.ds(pl.multiple_of(s * SUB, SUB), SUB)
        for p in range(peers):
            acc_ref[rows, p * span:(p + 1) * span] = block[p * SUB:(p + 1) * SUB, :]
        return carry

    lax.fori_loop(0, sub_count, one_sub, 0)
    out_ref[...] = acc_ref[...].astype(out_ref.dtype)


def build_adjacency(slot_rows, coef_rows, nodes, columns):
    rows = 128
    subs = rows // SUB
    return pl.pallas_call(
        adjacency_kernel,
        grid=(nodes // rows,),
        in_specs=[
            pl.BlockSpec((subs, slot_rows.shape[1]), lambda b: (b, 0)),
            pl.BlockSpec((subs, coef_rows.shape[1]), lambda b: (b, 0)),
        ],
        out_specs=pl.BlockSpec((rows, columns), lambda b: (b, 0)),
        out_shape=jax.ShapeDtypeStruct((nodes, columns), jnp.bfloat16),
        scratch_shapes=[pltpu.VMEM((rows, columns), jnp.float32)],
    )(slot_rows, coef_rows)


def node_kernel(adj_ref, table_ref, self_ref, w_nbr_ref, out_ref):
    total = jnp.dot(adj_ref[...], table_ref[...], preferred_element_type=jnp.float32)
    pre = self_ref[...] + jnp.dot(total.astype(jnp.bfloat16), w_nbr_ref[...], preferred_element_type=jnp.float32)
    out_ref[...] = jnp.maximum(pre, 0.0).astype(out_ref.dtype)


def node_layer(adjacency, table, self_term, w_nbr):
    count, columns = adjacency.shape
    hidden = w_nbr.shape[1]
    rows = 256
    return pl.pallas_call(
        node_kernel,
        grid=(count // rows,),
        in_specs=[
            pl.BlockSpec((rows, columns), lambda b: (b, 0)),
            pl.BlockSpec(table.shape, lambda b: (0, 0)),
            pl.BlockSpec((rows, hidden), lambda b: (b, 0)),
            pl.BlockSpec(w_nbr.shape, lambda b: (0, 0)),
        ],
        out_specs=pl.BlockSpec((rows, hidden), lambda b: (b, 0)),
        out_shape=jax.ShapeDtypeStruct((count, hidden), jnp.bfloat16),
        compiler_params=pltpu.CompilerParams(vmem_limit_bytes=48 * 1024 * 1024),
    )(adjacency, table, self_term, w_nbr)


def select_matrix(indices, count, dtype):
    return (indices[:, None] == jnp.arange(count, dtype=jnp.int32)[None, :]).astype(dtype)


def scatter_sum(indices, values, count):
    hit = indices[:, None] == jnp.arange(count, dtype=jnp.int32)[None, :]
    return jnp.sum(jnp.where(hit, values[:, None], jnp.float32(0.0)), axis=0)


def body(
    embed,
    knn_slot,
    knn_weight,
    tile_list,
    send_rows,
    members,
    sub_len,
    w_self,
    w_nbr,
    bias_v,
    w_conf,
    w_diff,
    w_ctx,
    bias_e,
    w_edge,
):
    nodes = embed.shape[0]
    width = embed.shape[1]
    neighbour_count = knn_slot.shape[1]
    shard_count = lax.axis_size("shard")
    list_len = tile_list.shape[2]
    peer_span = list_len * TILE
    column_total = shard_count * peer_span
    embed_bf = embed.astype(jnp.bfloat16)
    weight_sum = jnp.sum(knn_weight, axis=1, keepdims=True)
    coeff_bf = (knn_weight / weight_sum).astype(jnp.bfloat16)
    sub_rows = nodes // SUB
    adjacency = build_adjacency(
        knn_slot.reshape(sub_rows, SUB * neighbour_count),
        coeff_bf.astype(jnp.float32).reshape(sub_rows, SUB * neighbour_count),
        nodes,
        column_total,
    )
    tile_count = nodes // TILE
    embed_tiles = embed.reshape(tile_count, TILE, width)
    outgoing = embed_tiles.at[tile_list[0].reshape(shard_count * list_len)].get(mode="promise_in_bounds")
    outgoing = outgoing.astype(jnp.bfloat16)
    outgoing = outgoing.reshape(shard_count, peer_span, width)
    provided = lax.all_to_all(outgoing, "shard", split_axis=0, concat_axis=0, tiled=True)
    provided = provided.reshape(column_total, width)
    send_flat = send_rows[0].reshape(send_rows.shape[1] * send_rows.shape[2])
    self_term = jnp.dot(embed_bf, w_self, preferred_element_type=jnp.float32) + bias_v
    send_chooser = select_matrix(send_flat, nodes, jnp.bfloat16)
    send_adjacency = jnp.dot(send_chooser, adjacency, preferred_element_type=jnp.float32).astype(jnp.bfloat16)
    send_embed = jnp.dot(send_chooser, embed_bf, preferred_element_type=jnp.float32).astype(jnp.bfloat16)
    send_self = jnp.dot(send_embed, w_self, preferred_element_type=jnp.float32) + bias_v
    outbound = node_layer(send_adjacency, provided, send_self, w_nbr)
    node_hidden = node_layer(adjacency, provided, self_term, w_nbr)
    confidence = jnp.dot(node_hidden, w_conf, preferred_element_type=jnp.float32)
    device_total = send_rows.shape[1]
    capacity = send_rows.shape[2]
    hidden_width = node_hidden.shape[1]
    slot_total = device_total * capacity
    outbound = outbound.reshape(device_total, capacity, hidden_width)
    received = lax.all_to_all(outbound, ("grp", "shard"), split_axis=0, concat_axis=0, tiled=True)
    received_rows = received.reshape(slot_total, hidden_width)
    sub_count = members.shape[0]
    member_width = members.shape[1]
    member_flat = members.reshape(sub_count * member_width)
    member_chooser = select_matrix(member_flat, slot_total, jnp.bfloat16)
    member_rows = jnp.dot(member_chooser, received_rows, preferred_element_type=jnp.float32)
    member_rows = member_rows.reshape(sub_count, member_width, hidden_width)
    relative = member_rows - member_rows[:, :1, :]
    alive = jnp.arange(member_width, dtype=jnp.int32)[None, :] < sub_len[:, None]
    masked = jnp.where(alive[:, :, None], relative, 0.0)
    context = (jnp.sum(masked, axis=1) / sub_len[:, None].astype(jnp.float32)).astype(jnp.bfloat16)
    relative_bf = relative.astype(jnp.bfloat16)
    inner = jnp.einsum("smh,hk->smk", relative_bf, w_diff, preferred_element_type=jnp.float32)
    inner = inner + jnp.dot(context, w_ctx, preferred_element_type=jnp.float32)[:, None, :] + bias_e
    edge_hidden = jax.nn.relu(inner).astype(jnp.bfloat16)
    logits = jnp.einsum("smk,k->sm", edge_hidden, w_edge, preferred_element_type=jnp.float32)
    edge_scores = jnp.where(alive, jax.nn.sigmoid(logits), 0.0)
    slot_scores = scatter_sum(member_flat, edge_scores.reshape(sub_count * member_width), slot_total)
    slot_scores = slot_scores.reshape(device_total, capacity)
    returned = lax.all_to_all(
        slot_scores, ("grp", "shard"), split_axis=0, concat_axis=0, tiled=True
    )
    node_votes = scatter_sum(send_flat, returned.reshape(slot_total), nodes)
    return (node_hidden, confidence, edge_scores, node_votes)


def solution(mesh):
    return jax.shard_map(
        body,
        mesh=mesh,
        in_specs=(
            P(("grp", "shard"), None),
            P(("grp", "shard"), None),
            P(("grp", "shard"), None),
            P(("grp", "shard"), None, None),
            P(("grp", "shard"), None, None),
            P(("grp", "shard"), None),
            P(("grp", "shard")),
            P(),
            P(),
            P(),
            P(),
            P(),
            P(),
            P(),
            P(),
        ),
        out_specs=(
            P(("grp", "shard"), None),
            P(("grp", "shard")),
            P(("grp", "shard"), None),
            P(("grp", "shard")),
        ),
        check_vma=False,
    )
```

```python
import math

import jax
import jax.numpy as jnp
from jax import lax
from jax.experimental import pallas as pl
from jax.experimental.pallas import tpu as pltpu
from jax.sharding import PartitionSpec as P

TILE = 128


SUB = 8


def adjacency_kernel(slot_ref, coef_ref, out_ref, acc_ref):
    span = 256
    peers = out_ref.shape[1] // span
    sub_count = out_ref.shape[0] // SUB
    width = slot_ref.shape[1]
    row_hit = lax.broadcasted_iota(jnp.int32, (span, width), 0)
    lane_node = lax.broadcasted_iota(jnp.int32, (peers * SUB, width), 1) // (width // SUB)
    pair_row = lax.broadcasted_iota(jnp.int32, (peers * SUB, width), 0)
    pair_peer = pair_row // SUB
    pair_node = pair_row % SUB

    def one_sub(s, carry):
        slots = slot_ref[pl.ds(s, 1), :]
        coefs = coef_ref[pl.ds(s, 1), :]
        onehot = jnp.where(row_hit == slots % span, 1.0, 0.0).astype(jnp.bfloat16)
        picked = (pair_peer == slots // span) & (pair_node == lane_node)
        weights = jnp.where(picked, coefs, 0.0).astype(jnp.bfloat16)
        block = lax.dot_general(
            weights, onehot, (((1,), (1,)), ((), ())), preferred_element_type=jnp.float32
        )
        block = block.astype(jnp.bfloat16).astype(jnp.float32)
        rows = pl.ds(pl.multiple_of(s * SUB, SUB), SUB)
        for p in range(peers):
            acc_ref[rows, p * span:(p + 1) * span] = block[p * SUB:(p + 1) * SUB, :]
        return carry

    lax.fori_loop(0, sub_count, one_sub, 0)
    out_ref[...] = acc_ref[...].astype(out_ref.dtype)


def build_adjacency(slot_rows, coef_rows, nodes, columns):
    rows = 128
    subs = rows // SUB
    return pl.pallas_call(
        adjacency_kernel,
        grid=(nodes // rows,),
        in_specs=[
            pl.BlockSpec((subs, slot_rows.shape[1]), lambda b: (b, 0)),
            pl.BlockSpec((subs, coef_rows.shape[1]), lambda b: (b, 0)),
        ],
        out_specs=pl.BlockSpec((rows, columns), lambda b: (b, 0)),
        out_shape=jax.ShapeDtypeStruct((nodes, columns), jnp.bfloat16),
        scratch_shapes=[pltpu.VMEM((rows, columns), jnp.float32)],
    )(slot_rows, coef_rows)


def node_kernel(adj_ref, table_ref, embed_ref, w_self_ref, w_nbr_ref, bias_ref, send_ref, out_ref, outbound_ref, held_ref, acc_ref):
    b = pl.program_id(0)
    k = pl.program_id(1)
    rows = out_ref.shape[0]

    @pl.when(k == 0)
    def _():
        acc_ref[...] = jnp.zeros_like(acc_ref)

    acc_ref[...] += jnp.dot(adj_ref[...], table_ref[...], preferred_element_type=jnp.float32)

    @pl.when(k == pl.num_programs(1) - 1)
    def _():
        pre = (
            jnp.dot(embed_ref[...], w_self_ref[...], preferred_element_type=jnp.float32)
            + bias_ref[...]
            + jnp.dot(acc_ref[...].astype(jnp.bfloat16), w_nbr_ref[...], preferred_element_type=jnp.float32)
        )
        hidden = jnp.maximum(pre, 0.0).astype(out_ref.dtype)
        out_ref[...] = hidden
        held_ref[pl.ds(pl.multiple_of(b * rows, rows), rows), :] = hidden

    @pl.when((b == pl.num_programs(0) - 1) & (k == pl.num_programs(1) - 1))
    def _():
        nodes = held_ref.shape[0]
        chooser = jnp.where(
            send_ref[...] == lax.broadcasted_iota(jnp.int32, (send_ref.shape[0], nodes), 1), 1.0, 0.0
        ).astype(jnp.bfloat16)
        outbound_ref[...] = jnp.dot(chooser, held_ref[...], preferred_element_type=jnp.float32).astype(
            outbound_ref.dtype
        )


def node_layer(adjacency, table, embed_bf, w_self, w_nbr, bias, send_flat):
    nodes, width = embed_bf.shape
    hidden = w_self.shape[1]
    columns = adjacency.shape[1]
    rows = 256
    depth = 1024
    slots = send_flat.shape[0]
    return pl.pallas_call(
        node_kernel,
        grid=(nodes // rows, columns // depth),
        in_specs=[
            pl.BlockSpec((rows, depth), lambda b, k: (b, k)),
            pl.BlockSpec((depth, table.shape[1]), lambda b, k: (k, 0)),
            pl.BlockSpec((rows, width), lambda b, k: (b, 0)),
            pl.BlockSpec(w_self.shape, lambda b, k: (0, 0)),
            pl.BlockSpec(w_nbr.shape, lambda b, k: (0, 0)),
            pl.BlockSpec((1, hidden), lambda b, k: (0, 0)),
            pl.BlockSpec((slots, 1), lambda b, k: (0, 0)),
        ],
        out_specs=[
            pl.BlockSpec((rows, hidden), lambda b, k: (b, 0)),
            pl.BlockSpec((slots, hidden), lambda b, k: (0, 0)),
        ],
        out_shape=[
            jax.ShapeDtypeStruct((nodes, hidden), jnp.bfloat16),
            jax.ShapeDtypeStruct((slots, hidden), jnp.bfloat16),
        ],
        scratch_shapes=[
            pltpu.VMEM((nodes, hidden), jnp.bfloat16),
            pltpu.VMEM((rows, table.shape[1]), jnp.float32),
        ],
        compiler_params=pltpu.CompilerParams(vmem_limit_bytes=48 * 1024 * 1024),
    )(adjacency, table, embed_bf, w_self, w_nbr, bias.reshape(1, hidden), send_flat.reshape(slots, 1))


def select_matrix(indices, count, dtype):
    return (indices[:, None] == jnp.arange(count, dtype=jnp.int32)[None, :]).astype(dtype)


def scatter_sum(indices, values, count):
    hit = indices[:, None] == jnp.arange(count, dtype=jnp.int32)[None, :]
    return jnp.sum(jnp.where(hit, values[:, None], jnp.float32(0.0)), axis=0)


def body(
    embed,
    knn_slot,
    knn_weight,
    tile_list,
    send_rows,
    members,
    sub_len,
    w_self,
    w_nbr,
    bias_v,
    w_conf,
    w_diff,
    w_ctx,
    bias_e,
    w_edge,
):
    nodes = embed.shape[0]
    width = embed.shape[1]
    neighbour_count = knn_slot.shape[1]
    shard_count = lax.axis_size("shard")
    list_len = tile_list.shape[2]
    peer_span = list_len * TILE
    column_total = shard_count * peer_span
    embed_bf = embed.astype(jnp.bfloat16)
    weight_sum = jnp.sum(knn_weight, axis=1, keepdims=True)
    coeff_bf = (knn_weight / weight_sum).astype(jnp.bfloat16)
    sub_rows = nodes // SUB
    adjacency = build_adjacency(
        knn_slot.reshape(sub_rows, SUB * neighbour_count),
        coeff_bf.astype(jnp.float32).reshape(sub_rows, SUB * neighbour_count),
        nodes,
        column_total,
    )
    tile_count = nodes // TILE
    embed_tiles = embed.reshape(tile_count, TILE, width)
    outgoing = embed_tiles.at[tile_list[0].reshape(shard_count * list_len)].get(mode="promise_in_bounds")
    outgoing = outgoing.astype(jnp.bfloat16)
    outgoing = outgoing.reshape(shard_count, peer_span, width)
    provided = lax.all_to_all(outgoing, "shard", split_axis=0, concat_axis=0, tiled=True)
    provided = provided.reshape(column_total, width)
    send_flat = send_rows[0].reshape(send_rows.shape[1] * send_rows.shape[2])
    node_hidden, outbound = node_layer(adjacency, provided, embed_bf, w_self, w_nbr, bias_v, send_flat)
    confidence = jnp.dot(node_hidden, w_conf, preferred_element_type=jnp.float32)
    device_total = send_rows.shape[1]
    capacity = send_rows.shape[2]
    hidden_width = node_hidden.shape[1]
    slot_total = device_total * capacity
    outbound = outbound.reshape(device_total, capacity, hidden_width)
    received = lax.all_to_all(outbound, ("grp", "shard"), split_axis=0, concat_axis=0, tiled=True)
    received_rows = received.reshape(slot_total, hidden_width)
    sub_count = members.shape[0]
    member_width = members.shape[1]
    member_flat = members.reshape(sub_count * member_width)
    member_chooser = select_matrix(member_flat, slot_total, jnp.bfloat16)
    member_rows = jnp.dot(member_chooser, received_rows, preferred_element_type=jnp.float32)
    member_rows = member_rows.reshape(sub_count, member_width, hidden_width)
    relative = member_rows - member_rows[:, :1, :]
    alive = jnp.arange(member_width, dtype=jnp.int32)[None, :] < sub_len[:, None]
    masked = jnp.where(alive[:, :, None], relative, 0.0)
    context = (jnp.sum(masked, axis=1) / sub_len[:, None].astype(jnp.float32)).astype(jnp.bfloat16)
    relative_bf = relative.astype(jnp.bfloat16)
    inner = jnp.einsum("smh,hk->smk", relative_bf, w_diff, preferred_element_type=jnp.float32)
    inner = inner + jnp.dot(context, w_ctx, preferred_element_type=jnp.float32)[:, None, :] + bias_e
    edge_hidden = jax.nn.relu(inner).astype(jnp.bfloat16)
    logits = jnp.einsum("smk,k->sm", edge_hidden, w_edge, preferred_element_type=jnp.float32)
    edge_scores = jnp.where(alive, jax.nn.sigmoid(logits), 0.0)
    slot_scores = scatter_sum(member_flat, edge_scores.reshape(sub_count * member_width), slot_total)
    slot_scores = slot_scores.reshape(device_total, capacity)
    returned = lax.all_to_all(
        slot_scores, ("grp", "shard"), split_axis=0, concat_axis=0, tiled=True
    )
    node_votes = scatter_sum(send_flat, returned.reshape(slot_total), nodes)
    return (node_hidden, confidence, edge_scores, node_votes)


def solution(mesh):
    return jax.shard_map(
        body,
        mesh=mesh,
        in_specs=(
            P(("grp", "shard"), None),
            P(("grp", "shard"), None),
            P(("grp", "shard"), None),
            P(("grp", "shard"), None, None),
            P(("grp", "shard"), None, None),
            P(("grp", "shard"), None),
            P(("grp", "shard")),
            P(),
            P(),
            P(),
            P(),
            P(),
            P(),
            P(),
            P(),
        ),
        out_specs=(
            P(("grp", "shard"), None),
            P(("grp", "shard")),
            P(("grp", "shard"), None),
            P(("grp", "shard")),
        ),
        check_vma=False,
    )
```

```python
import math

import jax
import jax.numpy as jnp
from jax import lax
from jax.experimental import pallas as pl
from jax.experimental.pallas import tpu as pltpu
from jax.sharding import PartitionSpec as P

TILE = 128


SUB = 8


def adjacency_kernel(slot_ref, coef_ref, out_ref, acc_ref):
    span = 256
    peers = out_ref.shape[1] // span
    sub_count = out_ref.shape[0] // SUB
    width = slot_ref.shape[1]
    row_hit = lax.broadcasted_iota(jnp.int32, (span, width), 0)
    lane_node = lax.broadcasted_iota(jnp.int32, (peers * SUB, width), 1) // (width // SUB)
    pair_row = lax.broadcasted_iota(jnp.int32, (peers * SUB, width), 0)
    pair_peer = pair_row // SUB
    pair_node = pair_row % SUB

    def one_sub(s, carry):
        slots = slot_ref[pl.ds(s, 1), :]
        coefs = coef_ref[pl.ds(s, 1), :]
        onehot = jnp.where(row_hit == slots % span, 1.0, 0.0).astype(jnp.bfloat16)
        picked = (pair_peer == slots // span) & (pair_node == lane_node)
        weights = jnp.where(picked, coefs, 0.0).astype(jnp.bfloat16)
        block = lax.dot_general(
            weights, onehot, (((1,), (1,)), ((), ())), preferred_element_type=jnp.float32
        )
        block = block.astype(jnp.bfloat16).astype(jnp.float32)
        rows = pl.ds(pl.multiple_of(s * SUB, SUB), SUB)
        for p in range(peers):
            acc_ref[rows, p * span:(p + 1) * span] = block[p * SUB:(p + 1) * SUB, :]
        return carry

    lax.fori_loop(0, sub_count, one_sub, 0)
    out_ref[...] = acc_ref[...].astype(out_ref.dtype)


def build_adjacency(slot_rows, coef_rows, nodes, columns):
    rows = 128
    subs = rows // SUB
    return pl.pallas_call(
        adjacency_kernel,
        grid=(nodes // rows,),
        in_specs=[
            pl.BlockSpec((subs, slot_rows.shape[1]), lambda b: (b, 0)),
            pl.BlockSpec((subs, coef_rows.shape[1]), lambda b: (b, 0)),
        ],
        out_specs=pl.BlockSpec((rows, columns), lambda b: (b, 0)),
        out_shape=jax.ShapeDtypeStruct((nodes, columns), jnp.bfloat16),
        scratch_shapes=[pltpu.VMEM((rows, columns), jnp.float32)],
    )(slot_rows, coef_rows)


def node_kernel(adj_ref, table_ref, embed_ref, w_self_ref, w_nbr_ref, bias_ref, send_ref, out_ref, outbound_ref, held_ref):
    b = pl.program_id(0)
    rows = out_ref.shape[0]
    total = jnp.dot(adj_ref[...], table_ref[...], preferred_element_type=jnp.float32)
    pre = (
        jnp.dot(embed_ref[...], w_self_ref[...], preferred_element_type=jnp.float32)
        + bias_ref[...]
        + jnp.dot(total.astype(jnp.bfloat16), w_nbr_ref[...], preferred_element_type=jnp.float32)
    )
    hidden = jnp.maximum(pre, 0.0).astype(out_ref.dtype)
    out_ref[...] = hidden
    held_ref[pl.ds(pl.multiple_of(b * rows, rows), rows), :] = hidden

    @pl.when(b == pl.num_programs(0) - 1)
    def _():
        outbound_ref[...] = jnp.dot(send_ref[...], held_ref[...], preferred_element_type=jnp.float32).astype(
            outbound_ref.dtype
        )


def node_layer(adjacency, table, embed_bf, w_self, w_nbr, bias, send_flat):
    nodes, width = embed_bf.shape
    hidden = w_self.shape[1]
    columns = adjacency.shape[1]
    rows = 256
    slots = send_flat.shape[0]
    return pl.pallas_call(
        node_kernel,
        grid=(nodes // rows,),
        in_specs=[
            pl.BlockSpec((rows, columns), lambda b: (b, 0)),
            pl.BlockSpec(table.shape, lambda b: (0, 0)),
            pl.BlockSpec((rows, width), lambda b: (b, 0)),
            pl.BlockSpec(w_self.shape, lambda b: (0, 0)),
            pl.BlockSpec(w_nbr.shape, lambda b: (0, 0)),
            pl.BlockSpec((1, hidden), lambda b: (0, 0)),
            pl.BlockSpec((slots, nodes), lambda b: (0, 0)),
        ],
        out_specs=[
            pl.BlockSpec((rows, hidden), lambda b: (b, 0)),
            pl.BlockSpec((slots, hidden), lambda b: (0, 0)),
        ],
        out_shape=[
            jax.ShapeDtypeStruct((nodes, hidden), jnp.bfloat16),
            jax.ShapeDtypeStruct((slots, hidden), jnp.bfloat16),
        ],
        scratch_shapes=[pltpu.VMEM((nodes, hidden), jnp.bfloat16)],
        compiler_params=pltpu.CompilerParams(vmem_limit_bytes=48 * 1024 * 1024),
    )(adjacency, table, embed_bf, w_self, w_nbr, bias.reshape(1, hidden), select_matrix(send_flat, nodes, jnp.bfloat16))


def select_matrix(indices, count, dtype):
    return (indices[:, None] == jnp.arange(count, dtype=jnp.int32)[None, :]).astype(dtype)


def scatter_sum(indices, values, count):
    hit = indices[:, None] == jnp.arange(count, dtype=jnp.int32)[None, :]
    return jnp.sum(jnp.where(hit, values[:, None], jnp.float32(0.0)), axis=0)


def body(
    embed,
    knn_slot,
    knn_weight,
    tile_list,
    send_rows,
    members,
    sub_len,
    w_self,
    w_nbr,
    bias_v,
    w_conf,
    w_diff,
    w_ctx,
    bias_e,
    w_edge,
):
    nodes = embed.shape[0]
    width = embed.shape[1]
    neighbour_count = knn_slot.shape[1]
    shard_count = lax.axis_size("shard")
    list_len = tile_list.shape[2]
    peer_span = list_len * TILE
    column_total = shard_count * peer_span
    embed_bf = embed.astype(jnp.bfloat16)
    weight_sum = jnp.sum(knn_weight, axis=1, keepdims=True)
    coeff_bf = (knn_weight / weight_sum).astype(jnp.bfloat16)
    sub_rows = nodes // SUB
    adjacency = build_adjacency(
        knn_slot.reshape(sub_rows, SUB * neighbour_count),
        coeff_bf.astype(jnp.float32).reshape(sub_rows, SUB * neighbour_count),
        nodes,
        column_total,
    )
    tile_count = nodes // TILE
    embed_tiles = embed.reshape(tile_count, TILE, width)
    outgoing = embed_tiles.at[tile_list[0].reshape(shard_count * list_len)].get(mode="promise_in_bounds")
    outgoing = outgoing.astype(jnp.bfloat16)
    outgoing = outgoing.reshape(shard_count, peer_span, width)
    provided = lax.all_to_all(outgoing, "shard", split_axis=0, concat_axis=0, tiled=True)
    provided = provided.reshape(column_total, width)
    send_flat = send_rows[0].reshape(send_rows.shape[1] * send_rows.shape[2])
    node_hidden, outbound = node_layer(adjacency, provided, embed_bf, w_self, w_nbr, bias_v, send_flat)
    confidence = jnp.dot(node_hidden, w_conf, preferred_element_type=jnp.float32)
    device_total = send_rows.shape[1]
    capacity = send_rows.shape[2]
    hidden_width = node_hidden.shape[1]
    slot_total = device_total * capacity
    outbound = outbound.reshape(device_total, capacity, hidden_width)
    received = lax.all_to_all(outbound, ("grp", "shard"), split_axis=0, concat_axis=0, tiled=True)
    received_rows = received.reshape(slot_total, hidden_width)
    sub_count = members.shape[0]
    member_width = members.shape[1]
    member_flat = members.reshape(sub_count * member_width)
    member_chooser = lax.optimization_barrier(select_matrix(member_flat, slot_total, jnp.bfloat16))
    member_rows = jnp.dot(member_chooser, received_rows, preferred_element_type=jnp.float32)
    member_rows = member_rows.reshape(sub_count, member_width, hidden_width)
    relative = member_rows - member_rows[:, :1, :]
    alive = jnp.arange(member_width, dtype=jnp.int32)[None, :] < sub_len[:, None]
    masked = jnp.where(alive[:, :, None], relative, 0.0)
    context = (jnp.sum(masked, axis=1) / sub_len[:, None].astype(jnp.float32)).astype(jnp.bfloat16)
    relative_bf = relative.astype(jnp.bfloat16)
    inner = jnp.einsum("smh,hk->smk", relative_bf, w_diff, preferred_element_type=jnp.float32)
    inner = inner + jnp.dot(context, w_ctx, preferred_element_type=jnp.float32)[:, None, :] + bias_e
    edge_hidden = jax.nn.relu(inner).astype(jnp.bfloat16)
    logits = jnp.einsum("smk,k->sm", edge_hidden, w_edge, preferred_element_type=jnp.float32)
    edge_scores = jnp.where(alive, jax.nn.sigmoid(logits), 0.0)
    slot_scores = scatter_sum(member_flat, edge_scores.reshape(sub_count * member_width), slot_total)
    slot_scores = slot_scores.reshape(device_total, capacity)
    returned = lax.all_to_all(
        slot_scores, ("grp", "shard"), split_axis=0, concat_axis=0, tiled=True
    )
    node_votes = scatter_sum(send_flat, returned.reshape(slot_total), nodes)
    return (node_hidden, confidence, edge_scores, node_votes)


def solution(mesh):
    return jax.shard_map(
        body,
        mesh=mesh,
        in_specs=(
            P(("grp", "shard"), None),
            P(("grp", "shard"), None),
            P(("grp", "shard"), None),
            P(("grp", "shard"), None, None),
            P(("grp", "shard"), None, None),
            P(("grp", "shard"), None),
            P(("grp", "shard")),
            P(),
            P(),
            P(),
            P(),
            P(),
            P(),
            P(),
            P(),
        ),
        out_specs=(
            P(("grp", "shard"), None),
            P(("grp", "shard")),
            P(("grp", "shard"), None),
            P(("grp", "shard")),
        ),
        check_vma=False,
    )
```

```python
import math

import jax
import jax.numpy as jnp
from jax import lax
from jax.experimental import pallas as pl
from jax.experimental.pallas import tpu as pltpu
from jax.sharding import PartitionSpec as P

TILE = 128


SUB = 8


def adjacency_kernel(slot_ref, coef_ref, out_ref, acc_ref):
    span = 256
    peers = out_ref.shape[1] // span
    sub_count = out_ref.shape[0] // SUB
    width = slot_ref.shape[1]
    row_hit = lax.broadcasted_iota(jnp.int32, (span, width), 0)
    lane_node = lax.broadcasted_iota(jnp.int32, (peers * SUB, width), 1) // (width // SUB)
    pair_row = lax.broadcasted_iota(jnp.int32, (peers * SUB, width), 0)
    pair_peer = pair_row // SUB
    pair_node = pair_row % SUB

    def one_sub(s, carry):
        slots = slot_ref[pl.ds(s, 1), :]
        coefs = coef_ref[pl.ds(s, 1), :]
        onehot = jnp.where(row_hit == slots % span, 1.0, 0.0).astype(jnp.bfloat16)
        picked = (pair_peer == slots // span) & (pair_node == lane_node)
        weights = jnp.where(picked, coefs, 0.0).astype(jnp.bfloat16)
        block = lax.dot_general(
            weights, onehot, (((1,), (1,)), ((), ())), preferred_element_type=jnp.float32
        )
        block = block.astype(jnp.bfloat16).astype(jnp.float32)
        rows = pl.ds(pl.multiple_of(s * SUB, SUB), SUB)
        for p in range(peers):
            acc_ref[rows, p * span:(p + 1) * span] = block[p * SUB:(p + 1) * SUB, :]
        return carry

    lax.fori_loop(0, sub_count, one_sub, 0)
    out_ref[...] = acc_ref[...].astype(out_ref.dtype)


def build_adjacency(slot_rows, coef_rows, nodes, columns):
    rows = 128
    subs = rows // SUB
    return pl.pallas_call(
        adjacency_kernel,
        grid=(nodes // rows,),
        in_specs=[
            pl.BlockSpec((subs, slot_rows.shape[1]), lambda b: (b, 0)),
            pl.BlockSpec((subs, coef_rows.shape[1]), lambda b: (b, 0)),
        ],
        out_specs=pl.BlockSpec((rows, columns), lambda b: (b, 0)),
        out_shape=jax.ShapeDtypeStruct((nodes, columns), jnp.bfloat16),
        scratch_shapes=[pltpu.VMEM((rows, columns), jnp.float32)],
    )(slot_rows, coef_rows)


def node_kernel(adj_ref, table_hbm, embed_ref, w_self_ref, w_nbr_ref, bias_ref, send_ref, out_ref, outbound_ref, held_ref, table_ref, sems):
    b = pl.program_id(0)
    rows = out_ref.shape[0]
    chunks = table_ref.shape[0]
    depth = table_ref.shape[1]
    copies = [pltpu.make_async_copy(table_hbm.at[c], table_ref.at[c], sems.at[c]) for c in range(chunks)]

    @pl.when(b == 0)
    def _():
        for copy in copies:
            copy.start()

    total = jnp.zeros((rows, table_ref.shape[2]), jnp.float32)
    for c in range(chunks):
        @pl.when(b == 0)
        def _():
            copies[c].wait()

        total = total + jnp.dot(
            adj_ref[:, c * depth:(c + 1) * depth], table_ref[c], preferred_element_type=jnp.float32
        )
    pre = (
        jnp.dot(embed_ref[...], w_self_ref[...], preferred_element_type=jnp.float32)
        + bias_ref[...]
        + jnp.dot(total.astype(jnp.bfloat16), w_nbr_ref[...], preferred_element_type=jnp.float32)
    )
    hidden = jnp.maximum(pre, 0.0).astype(out_ref.dtype)
    out_ref[...] = hidden
    held_ref[pl.ds(pl.multiple_of(b * rows, rows), rows), :] = hidden

    @pl.when(b == pl.num_programs(0) - 1)
    def _():
        nodes = held_ref.shape[0]
        chooser = jnp.where(
            send_ref[...] == lax.broadcasted_iota(jnp.int32, (send_ref.shape[0], nodes), 1), 1.0, 0.0
        ).astype(jnp.bfloat16)
        outbound_ref[...] = jnp.dot(chooser, held_ref[...], preferred_element_type=jnp.float32).astype(
            outbound_ref.dtype
        )


def node_layer(adjacency, table, embed_bf, w_self, w_nbr, bias, send_flat):
    nodes, width = embed_bf.shape
    hidden = w_self.shape[1]
    columns = adjacency.shape[1]
    rows = 256
    slots = send_flat.shape[0]
    return pl.pallas_call(
        node_kernel,
        grid=(nodes // rows,),
        in_specs=[
            pl.BlockSpec((rows, columns), lambda b: (b, 0)),
            pl.BlockSpec(memory_space=pl.ANY),
            pl.BlockSpec((rows, width), lambda b: (b, 0)),
            pl.BlockSpec(w_self.shape, lambda b: (0, 0)),
            pl.BlockSpec(w_nbr.shape, lambda b: (0, 0)),
            pl.BlockSpec((1, hidden), lambda b: (0, 0)),
            pl.BlockSpec((slots, 1), lambda b: (0, 0)),
        ],
        out_specs=[
            pl.BlockSpec((rows, hidden), lambda b: (b, 0)),
            pl.BlockSpec((slots, hidden), lambda b: (0, 0)),
        ],
        out_shape=[
            jax.ShapeDtypeStruct((nodes, hidden), jnp.bfloat16),
            jax.ShapeDtypeStruct((slots, hidden), jnp.bfloat16),
        ],
        scratch_shapes=[
            pltpu.VMEM((nodes, hidden), jnp.bfloat16),
            pltpu.VMEM((4, table.shape[0] // 4, table.shape[1]), jnp.bfloat16),
            pltpu.SemaphoreType.DMA((4,)),
        ],
        compiler_params=pltpu.CompilerParams(vmem_limit_bytes=48 * 1024 * 1024),
    )(adjacency, table.reshape(4, table.shape[0] // 4, table.shape[1]), embed_bf, w_self, w_nbr, bias.reshape(1, hidden), send_flat.reshape(slots, 1))


def select_matrix(indices, count, dtype):
    return (indices[:, None] == jnp.arange(count, dtype=jnp.int32)[None, :]).astype(dtype)


def scatter_sum(indices, values, count):
    hit = indices[:, None] == jnp.arange(count, dtype=jnp.int32)[None, :]
    return jnp.sum(jnp.where(hit, values[:, None], jnp.float32(0.0)), axis=0)


def body(
    embed,
    knn_slot,
    knn_weight,
    tile_list,
    send_rows,
    members,
    sub_len,
    w_self,
    w_nbr,
    bias_v,
    w_conf,
    w_diff,
    w_ctx,
    bias_e,
    w_edge,
):
    nodes = embed.shape[0]
    width = embed.shape[1]
    neighbour_count = knn_slot.shape[1]
    shard_count = lax.axis_size("shard")
    list_len = tile_list.shape[2]
    peer_span = list_len * TILE
    column_total = shard_count * peer_span
    embed_bf = embed.astype(jnp.bfloat16)
    weight_sum = jnp.sum(knn_weight, axis=1, keepdims=True)
    coeff_bf = (knn_weight / weight_sum).astype(jnp.bfloat16)
    sub_rows = nodes // SUB
    adjacency = build_adjacency(
        knn_slot.reshape(sub_rows, SUB * neighbour_count),
        coeff_bf.astype(jnp.float32).reshape(sub_rows, SUB * neighbour_count),
        nodes,
        column_total,
    )
    tile_count = nodes // TILE
    embed_tiles = embed.reshape(tile_count, TILE, width)
    outgoing = embed_tiles.at[tile_list[0].reshape(shard_count * list_len)].get(mode="promise_in_bounds")
    outgoing = outgoing.astype(jnp.bfloat16)
    outgoing = outgoing.reshape(shard_count, peer_span, width)
    provided = lax.all_to_all(outgoing, "shard", split_axis=0, concat_axis=0, tiled=True)
    provided = provided.reshape(column_total, width)
    send_flat = send_rows[0].reshape(send_rows.shape[1] * send_rows.shape[2])
    node_hidden, outbound = node_layer(adjacency, provided, embed_bf, w_self, w_nbr, bias_v, send_flat)
    confidence = jnp.dot(node_hidden, w_conf, preferred_element_type=jnp.float32)
    device_total = send_rows.shape[1]
    capacity = send_rows.shape[2]
    hidden_width = node_hidden.shape[1]
    slot_total = device_total * capacity
    outbound = outbound.reshape(device_total, capacity, hidden_width)
    received = lax.all_to_all(outbound, ("grp", "shard"), split_axis=0, concat_axis=0, tiled=True)
    received_rows = received.reshape(slot_total, hidden_width)
    sub_count = members.shape[0]
    member_width = members.shape[1]
    member_flat = members.reshape(sub_count * member_width)
    member_chooser = select_matrix(member_flat, slot_total, jnp.bfloat16)
    member_rows = jnp.dot(member_chooser, received_rows, preferred_element_type=jnp.float32)
    member_rows = member_rows.reshape(sub_count, member_width, hidden_width)
    relative = member_rows - member_rows[:, :1, :]
    alive = jnp.arange(member_width, dtype=jnp.int32)[None, :] < sub_len[:, None]
    masked = jnp.where(alive[:, :, None], relative, 0.0)
    context = (jnp.sum(masked, axis=1) / sub_len[:, None].astype(jnp.float32)).astype(jnp.bfloat16)
    relative_bf = relative.astype(jnp.bfloat16)
    inner = jnp.einsum("smh,hk->smk", relative_bf, w_diff, preferred_element_type=jnp.float32)
    inner = inner + jnp.dot(context, w_ctx, preferred_element_type=jnp.float32)[:, None, :] + bias_e
    edge_hidden = jax.nn.relu(inner).astype(jnp.bfloat16)
    logits = jnp.einsum("smk,k->sm", edge_hidden, w_edge, preferred_element_type=jnp.float32)
    edge_scores = jnp.where(alive, jax.nn.sigmoid(logits), 0.0)
    slot_scores = scatter_sum(member_flat, edge_scores.reshape(sub_count * member_width), slot_total)
    slot_scores = slot_scores.reshape(device_total, capacity)
    returned = lax.all_to_all(
        slot_scores, ("grp", "shard"), split_axis=0, concat_axis=0, tiled=True
    )
    node_votes = scatter_sum(send_flat, returned.reshape(slot_total), nodes)
    return (node_hidden, confidence, edge_scores, node_votes)


def solution(mesh):
    return jax.shard_map(
        body,
        mesh=mesh,
        in_specs=(
            P(("grp", "shard"), None),
            P(("grp", "shard"), None),
            P(("grp", "shard"), None),
            P(("grp", "shard"), None, None),
            P(("grp", "shard"), None, None),
            P(("grp", "shard"), None),
            P(("grp", "shard")),
            P(),
            P(),
            P(),
            P(),
            P(),
            P(),
            P(),
            P(),
        ),
        out_specs=(
            P(("grp", "shard"), None),
            P(("grp", "shard")),
            P(("grp", "shard"), None),
            P(("grp", "shard")),
        ),
        check_vma=False,
    )
```

```python
import math

import jax
import jax.numpy as jnp
from jax import lax
from jax.experimental import pallas as pl
from jax.experimental.pallas import tpu as pltpu
from jax.sharding import PartitionSpec as P

TILE = 128


SUB = 8


def adjacency_kernel(slot_ref, coef_ref, out_ref, acc_ref):
    span = 256
    peers = out_ref.shape[1] // span
    sub_count = out_ref.shape[0] // SUB
    width = slot_ref.shape[1]
    row_hit = lax.broadcasted_iota(jnp.int32, (span, width), 0)
    lane_node = lax.broadcasted_iota(jnp.int32, (peers * SUB, width), 1) // (width // SUB)
    pair_row = lax.broadcasted_iota(jnp.int32, (peers * SUB, width), 0)
    pair_peer = pair_row // SUB
    pair_node = pair_row % SUB

    def one_sub(s, carry):
        slots = slot_ref[pl.ds(s, 1), :]
        coefs = coef_ref[pl.ds(s, 1), :]
        onehot = jnp.where(row_hit == slots % span, 1.0, 0.0).astype(jnp.bfloat16)
        picked = (pair_peer == slots // span) & (pair_node == lane_node)
        weights = jnp.where(picked, coefs, 0.0).astype(jnp.bfloat16)
        block = lax.dot_general(
            weights, onehot, (((1,), (1,)), ((), ())), preferred_element_type=jnp.float32
        )
        block = block.astype(jnp.bfloat16).astype(jnp.float32)
        rows = pl.ds(pl.multiple_of(s * SUB, SUB), SUB)
        for p in range(peers):
            acc_ref[rows, p * span:(p + 1) * span] = block[p * SUB:(p + 1) * SUB, :]
        return carry

    lax.fori_loop(0, sub_count, one_sub, 0)
    out_ref[...] = acc_ref[...].astype(out_ref.dtype)


def build_adjacency(slot_rows, coef_rows, nodes, columns):
    rows = 128
    subs = rows // SUB
    return pl.pallas_call(
        adjacency_kernel,
        grid=(nodes // rows,),
        in_specs=[
            pl.BlockSpec((subs, slot_rows.shape[1]), lambda b: (b, 0)),
            pl.BlockSpec((subs, coef_rows.shape[1]), lambda b: (b, 0)),
        ],
        out_specs=pl.BlockSpec((rows, columns), lambda b: (b, 0)),
        out_shape=jax.ShapeDtypeStruct((nodes, columns), jnp.bfloat16),
        scratch_shapes=[pltpu.VMEM((rows, columns), jnp.float32)],
    )(slot_rows, coef_rows)


def node_kernel(adj_ref, table_ref, embed_ref, w_self_ref, w_nbr_ref, bias_ref, send_ref, out_ref, outbound_ref, held_ref, chooser_ref):
    b = pl.program_id(0)

    @pl.when(b == 0)
    def _():
        chooser_ref[...] = jnp.where(
            send_ref[...] == lax.broadcasted_iota(jnp.int32, chooser_ref.shape, 1), 1.0, 0.0
        ).astype(jnp.bfloat16)

    rows = out_ref.shape[0]
    total = jnp.dot(adj_ref[...], table_ref[...], preferred_element_type=jnp.float32)
    pre = (
        jnp.dot(embed_ref[...], w_self_ref[...], preferred_element_type=jnp.float32)
        + bias_ref[...]
        + jnp.dot(total.astype(jnp.bfloat16), w_nbr_ref[...], preferred_element_type=jnp.float32)
    )
    hidden = jnp.maximum(pre, 0.0).astype(out_ref.dtype)
    out_ref[...] = hidden
    held_ref[pl.ds(pl.multiple_of(b * rows, rows), rows), :] = hidden

    @pl.when(b == pl.num_programs(0) - 1)
    def _():
        outbound_ref[...] = jnp.dot(chooser_ref[...], held_ref[...], preferred_element_type=jnp.float32).astype(
            outbound_ref.dtype
        )


def node_layer(adjacency, table, embed_bf, w_self, w_nbr, bias, send_flat):
    nodes, width = embed_bf.shape
    hidden = w_self.shape[1]
    columns = adjacency.shape[1]
    rows = 256
    slots = send_flat.shape[0]
    return pl.pallas_call(
        node_kernel,
        grid=(nodes // rows,),
        in_specs=[
            pl.BlockSpec((rows, columns), lambda b: (b, 0)),
            pl.BlockSpec(table.shape, lambda b: (0, 0)),
            pl.BlockSpec((rows, width), lambda b: (b, 0)),
            pl.BlockSpec(w_self.shape, lambda b: (0, 0)),
            pl.BlockSpec(w_nbr.shape, lambda b: (0, 0)),
            pl.BlockSpec((1, hidden), lambda b: (0, 0)),
            pl.BlockSpec((slots, 1), lambda b: (0, 0)),
        ],
        out_specs=[
            pl.BlockSpec((rows, hidden), lambda b: (b, 0)),
            pl.BlockSpec((slots, hidden), lambda b: (0, 0)),
        ],
        out_shape=[
            jax.ShapeDtypeStruct((nodes, hidden), jnp.bfloat16),
            jax.ShapeDtypeStruct((slots, hidden), jnp.bfloat16),
        ],
        scratch_shapes=[pltpu.VMEM((nodes, hidden), jnp.bfloat16), pltpu.VMEM((slots, nodes), jnp.bfloat16)],
        compiler_params=pltpu.CompilerParams(vmem_limit_bytes=48 * 1024 * 1024),
    )(adjacency, table, embed_bf, w_self, w_nbr, bias.reshape(1, hidden), send_flat.reshape(slots, 1))


def select_matrix(indices, count, dtype):
    return (indices[:, None] == jnp.arange(count, dtype=jnp.int32)[None, :]).astype(dtype)


def scatter_sum(indices, values, count):
    hit = indices[:, None] == jnp.arange(count, dtype=jnp.int32)[None, :]
    return jnp.sum(jnp.where(hit, values[:, None], jnp.float32(0.0)), axis=0)


def body(
    embed,
    knn_slot,
    knn_weight,
    tile_list,
    send_rows,
    members,
    sub_len,
    w_self,
    w_nbr,
    bias_v,
    w_conf,
    w_diff,
    w_ctx,
    bias_e,
    w_edge,
):
    nodes = embed.shape[0]
    width = embed.shape[1]
    neighbour_count = knn_slot.shape[1]
    shard_count = lax.axis_size("shard")
    list_len = tile_list.shape[2]
    peer_span = list_len * TILE
    column_total = shard_count * peer_span
    embed_bf = embed.astype(jnp.bfloat16)
    weight_sum = jnp.sum(knn_weight, axis=1, keepdims=True)
    coeff_bf = (knn_weight / weight_sum).astype(jnp.bfloat16)
    sub_rows = nodes // SUB
    adjacency = build_adjacency(
        knn_slot.reshape(sub_rows, SUB * neighbour_count),
        coeff_bf.astype(jnp.float32).reshape(sub_rows, SUB * neighbour_count),
        nodes,
        column_total,
    )
    tile_count = nodes // TILE
    embed_tiles = embed.reshape(tile_count, TILE, width)
    outgoing = embed_tiles.at[tile_list[0].reshape(shard_count * list_len)].get(mode="promise_in_bounds")
    outgoing = outgoing.astype(jnp.bfloat16)
    outgoing = outgoing.reshape(shard_count, peer_span, width)
    provided = lax.all_to_all(outgoing, "shard", split_axis=0, concat_axis=0, tiled=True)
    provided = provided.reshape(column_total, width)
    send_flat = send_rows[0].reshape(send_rows.shape[1] * send_rows.shape[2])
    node_hidden, outbound = node_layer(adjacency, provided, embed_bf, w_self, w_nbr, bias_v, send_flat)
    confidence = jnp.dot(node_hidden, w_conf, preferred_element_type=jnp.float32)
    device_total = send_rows.shape[1]
    capacity = send_rows.shape[2]
    hidden_width = node_hidden.shape[1]
    slot_total = device_total * capacity
    outbound = outbound.reshape(device_total, capacity, hidden_width)
    received = lax.all_to_all(outbound, ("grp", "shard"), split_axis=0, concat_axis=0, tiled=True)
    received_rows = received.reshape(slot_total, hidden_width)
    sub_count = members.shape[0]
    member_width = members.shape[1]
    member_flat = members.reshape(sub_count * member_width)
    member_chooser = select_matrix(member_flat, slot_total, jnp.bfloat16)
    member_rows = jnp.dot(member_chooser, received_rows, preferred_element_type=jnp.float32)
    member_rows = member_rows.reshape(sub_count, member_width, hidden_width)
    relative = member_rows - member_rows[:, :1, :]
    alive = jnp.arange(member_width, dtype=jnp.int32)[None, :] < sub_len[:, None]
    masked = jnp.where(alive[:, :, None], relative, 0.0)
    context = (jnp.sum(masked, axis=1) / sub_len[:, None].astype(jnp.float32)).astype(jnp.bfloat16)
    relative_bf = relative.astype(jnp.bfloat16)
    inner = jnp.einsum("smh,hk->smk", relative_bf, w_diff, preferred_element_type=jnp.float32)
    inner = inner + jnp.dot(context, w_ctx, preferred_element_type=jnp.float32)[:, None, :] + bias_e
    edge_hidden = jax.nn.relu(inner).astype(jnp.bfloat16)
    logits = jnp.einsum("smk,k->sm", edge_hidden, w_edge, preferred_element_type=jnp.float32)
    edge_scores = jnp.where(alive, jax.nn.sigmoid(logits), 0.0)
    slot_scores = scatter_sum(member_flat, edge_scores.reshape(sub_count * member_width), slot_total)
    slot_scores = slot_scores.reshape(device_total, capacity)
    returned = lax.all_to_all(
        slot_scores, ("grp", "shard"), split_axis=0, concat_axis=0, tiled=True
    )
    node_votes = scatter_sum(send_flat, returned.reshape(slot_total), nodes)
    return (node_hidden, confidence, edge_scores, node_votes)


def solution(mesh):
    return jax.shard_map(
        body,
        mesh=mesh,
        in_specs=(
            P(("grp", "shard"), None),
            P(("grp", "shard"), None),
            P(("grp", "shard"), None),
            P(("grp", "shard"), None, None),
            P(("grp", "shard"), None, None),
            P(("grp", "shard"), None),
            P(("grp", "shard")),
            P(),
            P(),
            P(),
            P(),
            P(),
            P(),
            P(),
            P(),
        ),
        out_specs=(
            P(("grp", "shard"), None),
            P(("grp", "shard")),
            P(("grp", "shard"), None),
            P(("grp", "shard")),
        ),
        check_vma=False,
    )
```

```python
import math

import jax
import jax.numpy as jnp
from jax import lax
from jax.experimental import pallas as pl
from jax.experimental.pallas import tpu as pltpu
from jax.sharding import PartitionSpec as P

TILE = 128


SUB = 8


def adjacency_kernel(slot_ref, coef_ref, out_ref, acc_ref):
    span = 256
    peers = out_ref.shape[1] // span
    sub_count = out_ref.shape[0] // SUB
    width = slot_ref.shape[1]
    row_hit = lax.broadcasted_iota(jnp.int32, (span, width), 0)
    lane_node = lax.broadcasted_iota(jnp.int32, (peers * SUB, width), 1) // (width // SUB)
    pair_row = lax.broadcasted_iota(jnp.int32, (peers * SUB, width), 0)
    pair_peer = pair_row // SUB
    pair_node = pair_row % SUB

    def one_sub(s, carry):
        slots = slot_ref[pl.ds(s, 1), :]
        coefs = coef_ref[pl.ds(s, 1), :]
        onehot = jnp.where(row_hit == slots % span, 1.0, 0.0).astype(jnp.bfloat16)
        picked = (pair_peer == slots // span) & (pair_node == lane_node)
        weights = jnp.where(picked, coefs, 0.0).astype(jnp.bfloat16)
        block = lax.dot_general(
            weights, onehot, (((1,), (1,)), ((), ())), preferred_element_type=jnp.float32
        )
        block = block.astype(jnp.bfloat16).astype(jnp.float32)
        rows = pl.ds(pl.multiple_of(s * SUB, SUB), SUB)
        for p in range(peers):
            acc_ref[rows, p * span:(p + 1) * span] = block[p * SUB:(p + 1) * SUB, :]
        return carry

    lax.fori_loop(0, sub_count, one_sub, 0)
    out_ref[...] = acc_ref[...].astype(out_ref.dtype)


def build_adjacency(slot_rows, coef_rows, nodes, columns):
    rows = 128
    subs = rows // SUB
    return pl.pallas_call(
        adjacency_kernel,
        grid=(nodes // rows,),
        in_specs=[
            pl.BlockSpec((subs, slot_rows.shape[1]), lambda b: (b, 0)),
            pl.BlockSpec((subs, coef_rows.shape[1]), lambda b: (b, 0)),
        ],
        out_specs=pl.BlockSpec((rows, columns), lambda b: (b, 0)),
        out_shape=jax.ShapeDtypeStruct((nodes, columns), jnp.bfloat16),
        scratch_shapes=[pltpu.VMEM((rows, columns), jnp.float32)],
    )(slot_rows, coef_rows)


def node_kernel(adj_ref, table_ref, embed_ref, w_self_ref, w_nbr_ref, bias_ref, send_ref, out_ref, outbound_ref, held_ref):
    b = pl.program_id(0)
    rows = out_ref.shape[0]
    total = jnp.dot(adj_ref[...], table_ref[...], preferred_element_type=jnp.float32)
    pre = (
        jnp.dot(embed_ref[...], w_self_ref[...], preferred_element_type=jnp.float32)
        + bias_ref[...]
        + jnp.dot(total.astype(jnp.bfloat16), w_nbr_ref[...], preferred_element_type=jnp.float32)
    )
    hidden = jnp.maximum(pre, 0.0).astype(out_ref.dtype)
    out_ref[...] = hidden
    held_ref[pl.ds(pl.multiple_of(b * rows, rows), rows), :] = hidden

    @pl.when(b == pl.num_programs(0) - 1)
    def _():
        nodes = held_ref.shape[0]
        chooser = jnp.where(
            send_ref[...] == lax.broadcasted_iota(jnp.int32, (send_ref.shape[0], nodes), 1), 1.0, 0.0
        ).astype(jnp.bfloat16)
        outbound_ref[...] = jnp.dot(chooser, held_ref[...], preferred_element_type=jnp.float32).astype(
            outbound_ref.dtype
        )


def node_layer(adjacency, table, embed_bf, w_self, w_nbr, bias, send_flat):
    nodes, width = embed_bf.shape
    hidden = w_self.shape[1]
    columns = adjacency.shape[1]
    rows = 256
    slots = send_flat.shape[0]
    return pl.pallas_call(
        node_kernel,
        grid=(nodes // rows,),
        in_specs=[
            pl.BlockSpec((rows, columns), lambda b: (b, 0)),
            pl.BlockSpec(table.shape, lambda b: (0, 0)),
            pl.BlockSpec((rows, width), lambda b: (b, 0)),
            pl.BlockSpec(w_self.shape, lambda b: (0, 0)),
            pl.BlockSpec(w_nbr.shape, lambda b: (0, 0)),
            pl.BlockSpec((1, hidden), lambda b: (0, 0)),
            pl.BlockSpec((slots, 1), lambda b: (0, 0)),
        ],
        out_specs=[
            pl.BlockSpec((rows, hidden), lambda b: (b, 0)),
            pl.BlockSpec((slots, hidden), lambda b: (0, 0)),
        ],
        out_shape=[
            jax.ShapeDtypeStruct((nodes, hidden), jnp.bfloat16),
            jax.ShapeDtypeStruct((slots, hidden), jnp.bfloat16),
        ],
        scratch_shapes=[pltpu.VMEM((nodes, hidden), jnp.bfloat16)],
        compiler_params=pltpu.CompilerParams(vmem_limit_bytes=48 * 1024 * 1024),
    )(adjacency, table, embed_bf, w_self, w_nbr, bias.reshape(1, hidden), send_flat.reshape(slots, 1))


def select_matrix(indices, count, dtype):
    return (indices[:, None] == jnp.arange(count, dtype=jnp.int32)[None, :]).astype(dtype)


def scatter_sum(indices, values, count):
    hit = indices[:, None] == jnp.arange(count, dtype=jnp.int32)[None, :]
    return jnp.sum(jnp.where(hit, values[:, None], jnp.float32(0.0)), axis=0)


def body(
    embed,
    knn_slot,
    knn_weight,
    tile_list,
    send_rows,
    members,
    sub_len,
    w_self,
    w_nbr,
    bias_v,
    w_conf,
    w_diff,
    w_ctx,
    bias_e,
    w_edge,
):
    nodes = embed.shape[0]
    width = embed.shape[1]
    neighbour_count = knn_slot.shape[1]
    shard_count = lax.axis_size("shard")
    list_len = tile_list.shape[2]
    peer_span = list_len * TILE
    column_total = shard_count * peer_span
    embed_bf = embed.astype(jnp.bfloat16)
    weight_sum = jnp.sum(knn_weight, axis=1, keepdims=True)
    coeff_bf = (knn_weight / weight_sum).astype(jnp.bfloat16)
    sub_rows = nodes // SUB
    adjacency = build_adjacency(
        knn_slot.reshape(sub_rows, SUB * neighbour_count),
        coeff_bf.astype(jnp.float32).reshape(sub_rows, SUB * neighbour_count),
        nodes,
        column_total,
    )
    tile_count = nodes // TILE
    embed_tiles = embed.reshape(tile_count, TILE, width)
    outgoing = embed_tiles.at[tile_list[0].reshape(shard_count * list_len)].get(mode="promise_in_bounds")
    outgoing = outgoing.astype(jnp.bfloat16)
    outgoing = outgoing.reshape(shard_count, peer_span, width)
    provided = lax.all_to_all(outgoing, "shard", split_axis=0, concat_axis=0, tiled=True)
    provided = provided.reshape(column_total, width)
    send_flat = send_rows[0].reshape(send_rows.shape[1] * send_rows.shape[2])
    node_hidden, outbound = node_layer(adjacency, provided, embed_bf, w_self, w_nbr, bias_v, send_flat)
    confidence = jnp.dot(node_hidden, w_conf, preferred_element_type=jnp.float32)
    device_total = send_rows.shape[1]
    capacity = send_rows.shape[2]
    hidden_width = node_hidden.shape[1]
    slot_total = device_total * capacity
    outbound = outbound.reshape(device_total, capacity, hidden_width)
    received = lax.all_to_all(outbound, ("grp", "shard"), split_axis=0, concat_axis=0, tiled=True)
    received_rows = received.reshape(slot_total, hidden_width)
    sub_count = members.shape[0]
    member_width = members.shape[1]
    member_flat = members.reshape(sub_count * member_width)
    member_chooser = select_matrix(member_flat, slot_total, jnp.bfloat16)
    member_rows = jnp.dot(member_chooser, received_rows, preferred_element_type=jnp.float32).astype(jnp.bfloat16)
    member_rows = lax.reduce_precision(member_rows, exponent_bits=8, mantissa_bits=7).astype(jnp.float32)
    member_rows = member_rows.reshape(sub_count, member_width, hidden_width)
    relative = member_rows - member_rows[:, :1, :]
    alive = jnp.arange(member_width, dtype=jnp.int32)[None, :] < sub_len[:, None]
    masked = jnp.where(alive[:, :, None], relative, 0.0)
    context = (jnp.sum(masked, axis=1) / sub_len[:, None].astype(jnp.float32)).astype(jnp.bfloat16)
    relative_bf = relative.astype(jnp.bfloat16)
    inner = jnp.einsum("smh,hk->smk", relative_bf, w_diff, preferred_element_type=jnp.float32)
    inner = inner + jnp.dot(context, w_ctx, preferred_element_type=jnp.float32)[:, None, :] + bias_e
    edge_hidden = jax.nn.relu(inner).astype(jnp.bfloat16)
    logits = jnp.einsum("smk,k->sm", edge_hidden, w_edge, preferred_element_type=jnp.float32)
    edge_scores = jnp.where(alive, jax.nn.sigmoid(logits), 0.0)
    slot_scores = scatter_sum(member_flat, edge_scores.reshape(sub_count * member_width), slot_total)
    slot_scores = slot_scores.reshape(device_total, capacity)
    returned = lax.all_to_all(
        slot_scores, ("grp", "shard"), split_axis=0, concat_axis=0, tiled=True
    )
    node_votes = scatter_sum(send_flat, returned.reshape(slot_total), nodes)
    return (node_hidden, confidence, edge_scores, node_votes)


def solution(mesh):
    return jax.shard_map(
        body,
        mesh=mesh,
        in_specs=(
            P(("grp", "shard"), None),
            P(("grp", "shard"), None),
            P(("grp", "shard"), None),
            P(("grp", "shard"), None, None),
            P(("grp", "shard"), None, None),
            P(("grp", "shard"), None),
            P(("grp", "shard")),
            P(),
            P(),
            P(),
            P(),
            P(),
            P(),
            P(),
            P(),
        ),
        out_specs=(
            P(("grp", "shard"), None),
            P(("grp", "shard")),
            P(("grp", "shard"), None),
            P(("grp", "shard")),
        ),
        check_vma=False,
    )
```
